256 devices in a mesh: tile: 64 (over z, x, core), rot: 4 (over y).
Axes of the slice: x: 4, y: 4, z: 8, core: 2. Of those that a mesh axis runs over, the one named last changes fastest.
Arguments:
- tomogram: bfloat16 [2048, 5120], P('tile'), may hold values from -12 to 12
- templates: bfloat16 [16, 110592], P('rot', 'tile'), may hold values from -6 to 6
- valid: int32 [2048, 80], P('tile'), may hold values from 0 to 1, as said below
- quats: float32 [4, 4096], replicated, may hold values from -1 to 1, as said below
- rot_index: int32 [16], P('rot'), may hold values from 0 to 4095
Outputs:
- best: float32 [2048, 5120], P('tile', 'rot')
- evidence: float32 [2048, 5120], P('tile', 'rot')
- moments: float32 [4, 2048, 5120], P(None, 'tile', 'rot')
The draws below stay inside these ranges and needn't reach their ends.
Inputs may be any that keep to these rules, and one draw needn't show every extreme that they name: `valid`: 1 marks a column (x, y) of voxels inside the lamella. `quats`: each column is a unit quaternion with a non-negative first component.
All inputs are finite; a program needn't handle non-finite values.
Results may differ from the reference program's by a relative error of at most 0.0003.
Values may be sent and summed in bfloat16 or wider, within the bound.
A program may use at most 128 MiB of HBM per device.

```python
import math
import jax
import jax.numpy as jnp
from jax import lax

TEMPL = 48
HALF = 24
NY = 80
Z = 64
NQ = 4096
ROTS = 16
NX = 2048


def template_bank(key):
    shape_bank = (ROTS, TEMPL ** 3)
    base = jnp.clip(jax.random.normal(jax.random.fold_in(key, 11), shape_bank, jnp.float32), -4.5, 4.5)
    return base


def draw_templates(key, part):
    return template_bank(key).astype(jnp.bfloat16)


def draw_tomogram(key, part):
    column_scale = jnp.exp(jax.random.uniform(jax.random.fold_in(key, 21), (NX, NY, 1), jnp.float32, math.log(0.3), math.log(3.0)))
    volume = jnp.clip(jax.random.normal(jax.random.fold_in(key, 23), (NX, NY, Z), jnp.float32), -4.0, 4.0) * column_scale
    return volume.reshape(NX, NY * Z).astype(jnp.bfloat16)


def draw_valid(key, part):
    threshold = NX + 2 * jnp.arange(NX, dtype=jnp.int32)[:, None]
    numbers = jax.random.randint(jax.random.fold_in(key, 31), (NX, NY), 0, 4 * NX)
    return (numbers < threshold).astype(jnp.int32)


def draw_quats(key, part):
    raw_quats = jax.random.normal(jax.random.fold_in(key, 41), (4, NQ), jnp.float32)
    unit_quats = raw_quats / jnp.sqrt(jnp.sum(raw_quats * raw_quats, axis=0, keepdims=True))
    return unit_quats.at[0].set(jnp.abs(unit_quats[0]))


def touch_ends(array, own_key, smallest, largest):
    place = [jax.random.randint(jax.random.fold_in(own_key, axis), (), 0, length) for axis, length in enumerate(array.shape)]
    longest = array.shape.index(max(array.shape))
    neighbour = place[:longest] + [(place[longest] + 1) % array.shape[longest]] + place[longest + 1:]
    return array.at[tuple(place)].set(smallest).at[tuple(neighbour)].set(largest)


def setup_inputs(seed: int = 0) -> dict:
    splits = jax.random.split(jax.random.key(seed), 6)
    return {
        "tomogram": draw_tomogram(jax.random.fold_in(splits[5], 71), 0),
        "templates": draw_templates(jax.random.fold_in(splits[5], 71), 0),
        "valid": draw_valid(jax.random.fold_in(splits[5], 71), 0),
        "quats": draw_quats(jax.random.fold_in(splits[5], 71), 0),
        "rot_index": touch_ends(jax.random.randint(splits[4], (ROTS,), 0, NQ), jax.random.fold_in(splits[4], 1), 0, NQ - 1).astype(jnp.int32),
    }


EPSILON = 1e-06

def unit_templates(templates):
    bank_float = templates.astype(jnp.float32)
    centred = bank_float - lax.optimization_barrier(jnp.mean(bank_float, axis=1, keepdims=True))
    spread = jnp.sqrt(lax.optimization_barrier(jnp.mean(centred * centred, axis=1, keepdims=True)) + EPSILON)
    return centred / (spread * jnp.float32(TEMPL) ** 1.5)

def correlate(slab_vol, kernel):
    padded_shape = (NX + TEMPL, NY + TEMPL, Z + TEMPL)
    padded = jnp.pad(slab_vol, HALF)
    kernel_pad = jnp.zeros(padded_shape, slab_vol.dtype).at[:TEMPL, :TEMPL, :TEMPL].set(kernel)
    spectrum = jnp.fft.rfftn(padded) * jnp.conj(jnp.fft.rfftn(kernel_pad))
    circular = jnp.fft.irfftn(spectrum, s=padded_shape)
    return circular[:NX, :NY, :Z].astype(slab_vol.dtype)

def reference(tomogram, templates, valid, quats, rot_index):
    slab_vol = tomogram.astype(jnp.float32).reshape(NX, NY, Z)
    kernels = unit_templates(templates).reshape(ROTS, TEMPL, TEMPL, TEMPL)
    inside = valid.astype(jnp.float32)[:, :, None]
    voxel_count = jnp.sum(inside) * Z

    def statistics(kernel):
        correlation = correlate(slab_vol, kernel)
        average = jnp.sum(inside * correlation) / voxel_count
        deviation = correlation - average
        spread = jnp.sqrt(jnp.sum(inside * deviation * deviation) / voxel_count + EPSILON)
        return (average, spread)
    averages, spreads = lax.map(statistics, kernels)
    orient = quats[:, rot_index].T

    def accumulate(state_in, rot_item):
        highest, exp_total, moment = state_in
        kernel, average, spread, quaternion = rot_item
        scores = (correlate(slab_vol, kernel) - average) / spread
        new_high = jnp.maximum(highest, scores)
        rescale = jnp.exp(highest - new_high)
        weight = jnp.exp(scores - new_high)
        exp_total = exp_total * rescale + weight
        moment = moment * rescale[None] + weight[None] * quaternion[:, None, None, None]
        return ((new_high, exp_total, moment), None)
    start_state = (jnp.full((NX, NY, Z), -jnp.inf, jnp.float32), jnp.zeros((NX, NY, Z), jnp.float32), jnp.zeros((4, NX, NY, Z), jnp.float32))
    (highest, exp_total, moment), _ = lax.scan(accumulate, start_state, (kernels, averages, spreads, orient))
    best = (inside * highest).reshape(NX, NY * Z)
    evidence = (inside * (highest + jnp.log(exp_total))).reshape(NX, NY * Z)
    moments = (inside[None] * moment / exp_total[None]).reshape(4, NX, NY * Z)
    return (best, evidence, moments)
```

```python
import functools
import math

import jax
import jax.numpy as jnp
import ml_dtypes
import numpy as np
from jax import lax
from jax.experimental import pallas as pl
from jax.experimental.pallas import tpu as pltpu
from jax.sharding import PartitionSpec as P

TEMPL = 48
HALF = 24
EPSILON = 1e-06
LANES = 128
ZF = 64
F32 = jnp.float32
BF16 = jnp.bfloat16


def halves(table):
    high = table.astype(np.float32).astype(ml_dtypes.bfloat16)
    low = (table - high.astype(np.float64)).astype(np.float32).astype(ml_dtypes.bfloat16)
    return high, low


def row_tables(table):
    high, low = halves(table)
    return np.concatenate([high, low], axis=0)


def col_tables(table):
    high, low = halves(table)
    return np.concatenate([high, low], axis=1)


def phases(rows, cols, length):
    index = np.outer(np.asarray(rows), np.asarray(cols)) % length
    return index * (2.0 * np.pi / length)


def padded_rows(table, rows):
    return np.pad(table, ((0, rows - table.shape[0]), (0, 0)))


def padded_cols(table, cols):
    return np.pad(table, ((0, 0), (0, cols - table.shape[1])))


def up8(n):
    return -(-n // 8) * 8


class Plan:
    def __init__(self, xs, ys, zs):
        self.xs, self.ys, self.zs = xs, ys, zs
        self.lx, self.ly, self.lz = xs + TEMPL, ys + HALF, zs + HALF
        self.kx, self.ky, self.kz = self.lx // 2 + 1, self.ly // 2 + 1, self.lz // 2 + 1
        self.kxp, self.kyp = up8(self.kx), up8(self.ky)
        self.kxi = up8(2 * self.kx)

    def folded(self, count, pad, points, length):
        angle = phases(np.arange(count), points, length)
        return np.concatenate(
            [padded_rows(np.cos(angle), pad), padded_rows(np.sin(angle), pad)], axis=0
        )

    def slab_z(self):
        angle = phases(np.arange(self.zs), np.arange(self.kz), self.lz)
        cos = padded_cols(np.cos(angle), ZF)
        sin = padded_cols(-np.sin(angle), ZF)
        one = np.concatenate([cos, cos, sin, sin], axis=1)
        none = np.zeros_like(one)
        high, low = halves(np.block([[one, none], [none, one]]))
        return np.concatenate([high, low], axis=0)

    def tmpl_z(self):
        angle = phases(np.arange(TEMPL) - HALF, np.arange(self.kz), self.lz)
        cos = np.zeros((ZF, ZF))
        sin = np.zeros((ZF, ZF))
        cos[:TEMPL, : self.kz] = np.cos(angle)
        sin[:TEMPL, : self.kz] = np.sin(angle)
        none = np.zeros_like(cos)
        return np.block([[cos, none, sin, none], [none, cos, none, sin]])

    def inverse_rows(self, points, count, length, k_pad, tail):
        angle = phases(points, np.arange(count), length)
        weight = np.full((1, count), 1.0 / length)
        weight[0, 0] *= 0.5
        weight[0, count - 1] *= 0.5
        cos = padded_cols(np.cos(angle) * weight, k_pad)
        sin = padded_cols(np.sin(angle) * weight, k_pad)
        return padded_cols(np.concatenate([cos, sin], axis=1), tail)

    def inverse_z(self):
        angle = phases(np.arange(self.kz), np.arange(self.zs), self.lz)
        weight = np.full((self.kz, 1), 2.0 / self.lz)
        weight[0] *= 0.5
        weight[self.kz - 1] *= 0.5
        cos = padded_rows(np.cos(angle) * weight, ZF)
        sin = padded_rows(-np.sin(angle) * weight, ZF)
        none = np.zeros_like(cos)
        return np.block([[cos, none], [none, cos], [sin, none], [none, sin]])


def split(value):
    high = value.astype(BF16)
    return high, (value - high.astype(F32)).astype(BF16)


def mm(left, right):
    return jnp.dot(left, right, preferred_element_type=F32)


def rows_product(table, value):
    count = table.shape[0] // 2
    high, low = split(value)
    both = mm(table, high)
    return both[:count] + both[count:] + mm(table[:count], low)


def plus_minus(folded, count, sign):
    cos_re, cos_im = folded[:count, :LANES], folded[:count, LANES:]
    sin_re, sin_im = folded[count:, :LANES], folded[count:, LANES:]
    first = (cos_re - sin_im, cos_im + sin_re)
    second = (cos_re + sin_im, cos_im - sin_re)
    return (first, second) if sign > 0 else (second, first)


def slab_kernel(plan, flags, own, low, high, table_z, table_x, table_y, spectrum, mid):
    kxp, kx = plan.kxp, plan.kx
    rows = 2 * kxp

    def first(j, carry):
        lanes = pl.ds(pl.multiple_of(j * LANES, LANES), LANES)

        def z_stage(ref):
            block = ref[:, lanes]
            return mm(jnp.concatenate([block, block], axis=1), table_z[...])

        low_z = jnp.where(flags[0] > 0, z_stage(low), 0.0)
        high_z = jnp.where(flags[1] > 0, z_stage(high), 0.0)
        strip = jnp.concatenate([low_z, z_stage(own), high_z], axis=0)
        for part in range(2):
            folded = rows_product(table_x[...], strip[:, part * 256 : part * 256 + 256])
            for s, (re, im) in enumerate(plus_minus(folded, kxp, -1)):
                at = pl.ds(pl.multiple_of((2 * j + part) * rows + s * kxp, 8), kxp)
                mid[0, at, :] = re
                mid[1, at, :] = im
        return carry

    lax.fori_loop(0, plan.ys // 2, first, 0)

    def second(k, carry):
        for s in range(2):
            at = pl.ds(k + s * kxp, plan.ys, stride=rows)
            value = jnp.concatenate([mid[0, at, :], mid[1, at, :]], axis=1)
            folded = rows_product(table_y[...], value)
            for u, (re, im) in enumerate(plus_minus(folded, plan.kyp, -1)):
                spectrum[k, s, u, :, :LANES] = re
                spectrum[k, s, u, :, LANES:] = im
        return carry

    lax.fori_loop(0, kx, second, 0)


def slab_spectrum(plan, flags, own, low, high):
    shape = (plan.kx, 2, 2, plan.kyp, 2 * LANES)
    table_z = plan.slab_z()
    table_x = row_tables(plan.folded(plan.kx, plan.kxp, np.arange(plan.lx), plan.lx))
    table_y = row_tables(plan.folded(plan.ky, plan.kyp, np.arange(plan.ys), plan.ly))
    smem = pl.BlockSpec(memory_space=pltpu.SMEM)
    vmem = pl.BlockSpec(memory_space=pltpu.VMEM)
    return pl.pallas_call(
        functools.partial(slab_kernel, plan),
        out_shape=jax.ShapeDtypeStruct(shape, F32),
        in_specs=[smem] + [vmem] * 6,
        out_specs=vmem,
        scratch_shapes=[pltpu.VMEM((2, plan.ys * 2 * plan.kxp, LANES), F32)],
        compiler_params=pltpu.CompilerParams(vmem_limit_bytes=56 << 20),
        name="slab_spectrum",
    )(flags, own, low, high, table_z, table_x, table_y)


def pair_kernel(
    plan, groups, where, bank, mask, spectrum_hbm, table_z, table_x, table_y, table_yi,
    table_xi, table_zi, zsum, ones, *rest
):
    outs, stats, (zed, mid, back, spectrum, sem) = rest[:groups], rest[groups], rest[groups + 1 :]
    kxp, kx, kyp, ys, xs = plan.kxp, plan.kx, plan.kyp, plan.ys, plan.xs
    rows = 2 * kxp
    fetch = pltpu.make_async_copy(spectrum_hbm, spectrum, sem)
    fetch.start()
    chunk = 384
    total = TEMPL * TEMPL
    count = float(TEMPL**3)
    lane = lax.broadcasted_iota(jnp.int32, (1, LANES), 1)
    used = lax.rem(lane, ZF) < TEMPL

    def add_up(i, carry):
        at = pl.ds(pl.multiple_of(i * chunk, chunk), chunk)
        return carry + jnp.sum(bank[at, :].astype(F32).reshape(chunk // 8, 8, LANES), axis=0)

    sums = lax.fori_loop(0, total // chunk, add_up, jnp.zeros((8, LANES), F32))
    mean = jnp.sum(exact(sums, ones[...]), axis=0, keepdims=True) / count

    def add_squares(i, carry):
        at = pl.ds(pl.multiple_of(i * chunk, chunk), chunk)
        off = jnp.where(used, bank[at, :].astype(F32) - mean, 0.0)
        return carry + jnp.sum((off * off).reshape(chunk // 8, 8, LANES), axis=0)

    squares = lax.fori_loop(0, total // chunk, add_squares, jnp.zeros((8, LANES), F32))
    variance = jnp.sum(exact(squares, ones[...]), axis=0, keepdims=True) / count
    factor = 1.0 / (jnp.sqrt(variance + EPSILON) * float(TEMPL) ** 1.5)
    shift = jnp.concatenate([mean, mean], axis=1) * zsum[...]
    scale = jnp.concatenate([factor, factor], axis=1)

    def z_stage(i, carry):
        at = pl.ds(pl.multiple_of(i * chunk, chunk), chunk)
        block = bank[at, :]
        value = mm(jnp.concatenate([block, block], axis=1), table_z[...])
        value = (value - shift) * scale
        zed[0, at, :] = value[:, :LANES]
        zed[1, at, :] = value[:, LANES:]
        return carry

    lax.fori_loop(0, total // chunk, z_stage, 0)

    def x_stage(i, carry):
        at = pl.ds(i, TEMPL, stride=TEMPL)
        value = jnp.concatenate([zed[0, at, :], zed[1, at, :]], axis=1)
        folded = rows_product(table_x[...], value)
        for s, (re, im) in enumerate(plus_minus(folded, kxp, 1)):
            to = pl.ds(pl.multiple_of(i * rows + s * kxp, 8), kxp)
            mid[0, to, :] = re
            mid[1, to, :] = im
        return carry

    lax.fori_loop(0, TEMPL, x_stage, 0)
    for pad in range(2 * kx, plan.kxi):
        back[:, pad * ys : pad * ys + ys, :] = jnp.zeros((2, ys, LANES), F32)
    fetch.wait()

    def y_stage(k, carry):
        found = []
        for s in range(2):
            at = pl.ds(k + s * kxp, TEMPL, stride=rows)
            value = jnp.concatenate([mid[0, at, :], mid[1, at, :]], axis=1)
            folded = rows_product(table_y[...], value)
            sides = []
            for u, (re, im) in enumerate(plus_minus(folded, kyp, 1)):
                slab_re = spectrum[k, s, u, :, :LANES]
                slab_im = spectrum[k, s, u, :, LANES:]
                sides.append((re * slab_re - im * slab_im, re * slab_im + im * slab_re))
            (re_p, im_p), (re_m, im_m) = sides
            even = jnp.concatenate([re_p + re_m, im_p + im_m], axis=1)
            odd = jnp.concatenate([im_m - im_p, re_p - re_m], axis=1)
            found.append(rows_product(table_yi[...], jnp.concatenate([even, odd], axis=0)))
        even = found[0] + found[1]
        odd = found[0] - found[1]
        to = pl.ds(pl.multiple_of(k * ys, 8), ys)
        back[0, to, :] = even[:, :LANES]
        back[1, to, :] = even[:, LANES:]
        to = pl.ds(pl.multiple_of((k + kx) * ys, 8), ys)
        back[0, to, :] = -odd[:, LANES:]
        back[1, to, :] = odd[:, :LANES]
        return carry

    lax.fori_loop(0, kx, y_stage, 0)
    share = ys // groups
    step = 4
    for j in range(groups):
        base = lax.rem(where[0] + j, groups) * share

        def last(i, carry):
            lines = []
            for part in range(step):
                at = pl.ds(base + i * step + part, plan.kxi, stride=ys)
                value = jnp.concatenate([back[0, at, :], back[1, at, :]], axis=1)
                lines.append(rows_product(table_xi[...], value))
            high, low = split(jnp.concatenate(lines, axis=0))
            both = mm(high, table_zi[...])
            value = both[:, :LANES] + both[:, LANES:] + mm(low, table_zi[:, :LANES])
            outs[j][pl.ds(pl.multiple_of(i * step * xs, 8), step * xs), :] = value
            return carry

        lax.fori_loop(0, share // step, last, 0)
    columns = jnp.sum(mask[...].astype(F32)) * (1.0 / 8.0)
    lane_sum = jnp.zeros((8, LANES), F32)
    for j in range(groups):
        lane_sum += exact(mask[j], outs[j][...])
    lane_mean = lane_sum[:1] / jnp.maximum(columns, 1.0)
    lane_square = jnp.zeros((8, LANES), F32)
    for j in range(groups):
        off = outs[j][...] - lane_mean
        lane_square += exact(mask[j], off * off)
    part_mean = exact(jnp.broadcast_to(lane_mean, (8, LANES)), ones[...]) / float(plan.zs)
    off = lane_mean - part_mean
    part_square = exact(lane_square + columns * off * off, ones[...])
    stats[...] = jnp.concatenate([part_mean[:4], part_square[:4]], axis=0)


def exact(left, right):
    return jnp.dot(left, right, precision=lax.Precision.HIGHEST, preferred_element_type=F32)


def pair_correlation(plan, groups, where, bank, mask, spectrum):
    z_table = plan.tmpl_z()
    ones = np.kron(np.eye(2), np.ones((ZF, ZF))).astype(np.float32)
    tables = [
        row_stack(z_table),
        row_tables(plan.folded(plan.kx, plan.kxp, np.arange(TEMPL), plan.lx)),
        row_tables(plan.folded(plan.ky, plan.kyp, np.arange(TEMPL) - HALF, plan.ly)),
        row_tables(plan.inverse_rows(np.arange(plan.ys), plan.ky, plan.ly, plan.kyp, 2 * plan.kyp)),
        row_tables(plan.inverse_rows(np.arange(plan.xs), plan.kx, plan.lx, plan.kx, plan.kxi)),
        col_tables(plan.inverse_z()),
        z_table.sum(axis=0, keepdims=True).astype(np.float32),
        ones,
    ]
    smem = pl.BlockSpec(memory_space=pltpu.SMEM)
    vmem = pl.BlockSpec(memory_space=pltpu.VMEM)
    share = plan.ys // groups * plan.xs
    return pl.pallas_call(
        functools.partial(pair_kernel, plan, groups),
        out_shape=[jax.ShapeDtypeStruct((share, LANES), F32)] * groups
        + [jax.ShapeDtypeStruct((8, LANES), F32)],
        in_specs=[smem, vmem, vmem, pl.BlockSpec(memory_space=pl.ANY)] + [vmem] * 8,
        out_specs=[vmem] * (groups + 1),
        scratch_shapes=[
            pltpu.VMEM((2, TEMPL * TEMPL, LANES), F32),
            pltpu.VMEM((2, TEMPL * 2 * plan.kxp, LANES), F32),
            pltpu.VMEM((2, plan.kxi * plan.ys, LANES), F32),
            pltpu.VMEM((plan.kx, 2, 2, plan.kyp, 2 * LANES), F32),
            pltpu.SemaphoreType.DMA,
        ],
        compiler_params=pltpu.CompilerParams(vmem_limit_bytes=60 << 20),
        name="pair_correlation",
    )(where, bank, mask, spectrum, *tables)


def row_stack(table):
    return np.concatenate(halves(table), axis=0)


MESH = pl.DeviceIdType.MESH
CORES = 2
RING_X = 4


def place():
    tile = lax.axis_index("tile")
    core = lax.rem(tile, CORES)
    x = lax.rem(tile // CORES, RING_X)
    z = tile // (CORES * RING_X)
    return z, x, core


def tile_of(z, x, core):
    return (z * RING_X + x) * CORES + core


def greet(peers):
    barrier = pltpu.get_barrier_semaphore()
    for peer in peers:
        pl.semaphore_signal(barrier, inc=1, device_id=peer, device_id_type=MESH)
    pl.semaphore_wait(barrier, len(peers))


def stage(source, target, sends, receives, first, peers):
    copies = []
    for index, peer in enumerate(peers):
        copy = pltpu.make_async_remote_copy(
            src_ref=source,
            dst_ref=target,
            send_sem=sends.at[first + index],
            recv_sem=receives.at[first + index],
            device_id=peer,
            device_id_type=MESH,
        )
        copy.start()
        copies.append(copy)
    for copy in copies:
        copy.wait()


def gather_kernel(ring_z, block, out, sends, receives, own_sem):
    z, x, core = place()
    z_peers = [{"tile": tile_of(lax.rem(z + d, ring_z), x, core)} for d in range(1, ring_z)]
    x_peers = [{"tile": tile_of(z, lax.rem(x + d, RING_X), core)} for d in range(1, RING_X)]
    other = [{"tile": tile_of(z, x, 1 - core)}]
    own = pltpu.make_async_copy(block, out.at[core, x, z], own_sem)
    own.start()
    greet(z_peers + x_peers + other)
    own.wait()
    mine = out.at[core, x, z]
    stage(mine, mine, sends, receives, 0, z_peers)
    mine = out.at[core, x]
    stage(mine, mine, sends, receives, len(z_peers), x_peers)
    mine = out.at[core]
    stage(mine, mine, sends, receives, len(z_peers) + len(x_peers), other)


def gathered(block, tiles):
    ring_z = tiles // (CORES * RING_X)
    peers = ring_z + RING_X - 1
    return pl.pallas_call(
        functools.partial(gather_kernel, ring_z),
        out_shape=jax.ShapeDtypeStruct((CORES, RING_X, ring_z) + block.shape, block.dtype),
        in_specs=[pl.BlockSpec(memory_space=pltpu.VMEM)],
        out_specs=pl.BlockSpec(memory_space=pltpu.VMEM),
        scratch_shapes=[
            pltpu.SemaphoreType.DMA((peers,)),
            pltpu.SemaphoreType.DMA((peers,)),
            pltpu.SemaphoreType.DMA,
        ],
        compiler_params=pltpu.CompilerParams(
            collective_id=0, has_side_effects=True, vmem_limit_bytes=32 << 20
        ),
        name="gather_templates",
    )(block)


def stats_kernel(ring_z, groups, first, second, extra, out, sends, receives):
    z, x, core = place()
    rot = lax.axis_index("rot")
    z_peers = [{"tile": tile_of(lax.rem(z + d, ring_z), x, core)} for d in range(1, ring_z)]
    flat = x * CORES + core
    plane = []
    for d in range(1, RING_X * CORES):
        there = lax.rem(flat + d, RING_X * CORES)
        plane.append({"tile": tile_of(z, there // CORES, lax.rem(there, CORES))})
    others = [{"rot": lax.rem(rot + d, groups)} for d in range(1, groups)]
    field = lax.rem(lax.broadcasted_iota(jnp.int32, (1, LANES), 1), ZF)
    row = extra[...]
    for index, value in enumerate((first[0:1], first[4:5], second[0:1], second[4:5])):
        row = jnp.where(field == index, value, row)
    out[rot, flat, z] = row
    greet(z_peers + plane + others)
    mine = out.at[rot, flat, z]
    stage(mine, mine, sends, receives, 0, z_peers)
    mine = out.at[rot, flat]
    stage(mine, mine, sends, receives, len(z_peers), plane)
    mine = out.at[rot]
    stage(mine, mine, sends, receives, len(z_peers) + len(plane), others)


def exchanged(first, second, extra, tiles, groups):
    ring_z = tiles // (CORES * RING_X)
    peers = ring_z + RING_X * CORES + groups - 3
    vmem = pl.BlockSpec(memory_space=pltpu.VMEM)
    return pl.pallas_call(
        functools.partial(stats_kernel, ring_z, groups),
        out_shape=jax.ShapeDtypeStruct((groups, RING_X * CORES, ring_z, 1, LANES), F32),
        in_specs=[vmem] * 3,
        out_specs=vmem,
        scratch_shapes=[pltpu.SemaphoreType.DMA((peers,)), pltpu.SemaphoreType.DMA((peers,))],
        compiler_params=pltpu.CompilerParams(
            collective_id=1, has_side_effects=True, vmem_limit_bytes=32 << 20
        ),
        name="exchange_statistics",
    )(first, second, extra)


FIELD_COUNT = 4
FIELD_QUAT = 5


def final_kernel(groups, xs, zs, where, valid, stats, *rest):
    parts = [rest[2 * j : 2 * j + 2] for j in range(groups)]
    best, evidence, moments = rest[2 * groups : 2 * groups + 3]
    lane = lax.broadcasted_iota(jnp.int32, (1, LANES), 1)
    low_half = lane < ZF

    def spread_field(rows, index):
        return jnp.where(low_half, rows[:, index : index + 1], rows[:, ZF + index : ZF + index + 1])

    terms = []
    for j in range(groups):
        group = lax.rem(where[0] + groups - j, groups)
        rows = stats[group]
        rows = rows.reshape(-1, LANES)
        columns = spread_field(rows, FIELD_COUNT)
        total = jnp.sum(columns, axis=0, keepdims=True)
        for p in range(2):
            mean = spread_field(rows, 2 * p)
            square = spread_field(rows, 2 * p + 1)
            average = jnp.sum(columns * mean, axis=0, keepdims=True) / total
            off = mean - average
            square = jnp.sum(square + (zs * columns) * off * off, axis=0, keepdims=True)
            inverse = 1.0 / jnp.sqrt(square / (total * zs) + EPSILON)
            quat = [spread_field(rows[:1], FIELD_QUAT + 4 * p + c) for c in range(4)]
            terms.append((parts[j][p], average, inverse, quat))

    def column(y):
        at = pl.ds(pl.multiple_of(y * xs, 8), xs)
        scores = [(ref[at, :] - average) * inverse for ref, average, inverse, _ in terms]
        high = functools.reduce(jnp.maximum, scores)
        high = jnp.maximum(high, pltpu.roll(high, ZF, 1))
        weights = [jnp.exp(score - high) for score in scores]
        sums = [functools.reduce(jnp.add, weights)]
        for c in range(4):
            sums.append(functools.reduce(jnp.add, [w * t[3][c] for w, t in zip(weights, terms)]))
        return [high] + [value + pltpu.roll(value, ZF, 1) for value in sums]

    for j in range(valid.shape[1] // 2):
        both = [jnp.where(low_half, a, b) for a, b in zip(column(2 * j), column(2 * j + 1))]
        inside = jnp.where(low_half, valid[:, 2 * j : 2 * j + 1], valid[:, 2 * j + 1 : 2 * j + 2])
        inside = inside.astype(F32)
        high, total = both[0], both[1]
        lanes = slice(j * LANES, j * LANES + LANES)
        best[:, lanes] = inside * high
        evidence[:, lanes] = inside * (high + jnp.log(total))
        ratio = inside / total
        for c in range(4):
            moments[c, :, lanes] = both[2 + c] * ratio


def finished(where, valid, stats, parts, zs):
    groups = len(parts)
    xs, share = valid.shape
    smem = pl.BlockSpec(memory_space=pltpu.SMEM)
    vmem = pl.BlockSpec(memory_space=pltpu.VMEM)
    flat = jax.ShapeDtypeStruct((xs, share * zs), F32)
    return pl.pallas_call(
        functools.partial(final_kernel, groups, xs, zs),
        out_shape=[flat, flat, jax.ShapeDtypeStruct((4, xs, share * zs), F32)],
        in_specs=[smem] + [vmem] * (2 + 2 * groups),
        out_specs=[vmem] * 3,
        compiler_params=pltpu.CompilerParams(vmem_limit_bytes=48 << 20),
        name="finish",
    )(where, valid, stats, *[ref for part in parts for ref in part])


def local(tomogram, templates, valid, quats, rot_index):
    xs, voxels = tomogram.shape
    ys = valid.shape[1]
    zs = voxels // ys
    plan = Plan(xs, ys, zs)
    tiles, groups = lax.axis_size("tile"), lax.axis_size("rot")
    tile, rot = lax.axis_index("tile"), lax.axis_index("rot")
    share = ys // groups
    where = rot.astype(jnp.int32).reshape(1)
    forward = [(i, i + 1) for i in range(tiles - 1)]
    backward = [(i + 1, i) for i in range(tiles - 1)]
    low = lax.ppermute(tomogram[xs - HALF :], "tile", forward)
    high = lax.ppermute(tomogram[:HALF], "tile", backward)
    flags = jnp.stack([tile > 0, tile < tiles - 1]).astype(jnp.int32)
    bank = gathered(templates, tiles)
    per = templates.shape[1] // TEMPL
    bank = bank.reshape(CORES, RING_X, -1, 2, 2, per, TEMPL).transpose(3, 2, 1, 0, 5, 4, 6)
    bank = jnp.pad(bank, [(0, 0)] * 6 + [(0, ZF - TEMPL)]).reshape(2, TEMPL * TEMPL, LANES)
    spectrum = slab_spectrum(plan, flags, tomogram, low, high)
    turned = jnp.roll(valid.T.reshape(groups, share * xs), -rot, axis=0)
    mask = jnp.broadcast_to(turned.astype(F32)[:, None, :], (groups, 8, share * xs))
    columns = jnp.sum(valid).astype(F32)
    one_hot = rot_index[:, None] == jnp.arange(quats.shape[1], dtype=jnp.int32)[None, :]
    orient = jnp.sum(jnp.where(one_hot[:, None, :], quats[None], 0.0), axis=2)
    fields = orient.reshape(2, 2, 4).transpose(1, 0, 2).reshape(2, 8)
    extra = jnp.concatenate(
        [jnp.zeros((2, 4), F32), jnp.full((2, 1), columns), fields, jnp.zeros((2, ZF - 13), F32)],
        axis=1,
    ).reshape(1, LANES)
    received, stats = [], []
    for p in range(2):
        *chunks, stat = pair_correlation(plan, groups, where, bank[p], mask, spectrum)
        stats.append(stat)
        received.append(
            [chunks[0]]
            + [
                lax.ppermute(chunks[j], "rot", [(i, (i + j) % groups) for i in range(groups)])
                for j in range(1, groups)
            ]
        )
    rows = exchanged(stats[0], stats[1], extra, tiles, groups).reshape(groups, tiles, 1, LANES)
    own_valid = lax.dynamic_slice_in_dim(valid, rot * share, share, 1)
    parts = [[received[0][j], received[1][j]] for j in range(groups)]
    return tuple(finished(where, own_valid, rows, parts, zs))


def solution(mesh):
    placed = (P("tile", None), P("rot", "tile"), P("tile", None), P(), P("rot"))
    return jax.shard_map(
        local,
        mesh=mesh,
        in_specs=placed,
        out_specs=(P("tile", "rot"), P("tile", "rot"), P(None, "tile", "rot")),
        check_vma=False,
    )
```

```python
import functools
import math

import jax
import jax.numpy as jnp
import ml_dtypes
import numpy as np
from jax import lax
from jax.experimental import pallas as pl
from jax.experimental.pallas import tpu as pltpu
from jax.sharding import PartitionSpec as P

TEMPL = 48
HALF = 24
EPSILON = 1e-06
LANES = 128
ZF = 64
CORES = 2
RING_X = 4
BLOCK = 48
MESH = pl.DeviceIdType.MESH
FIELD_COUNT = 4
FIELD_QUAT = 5
F32 = jnp.float32
BF16 = jnp.bfloat16


def halves(table):
    high = table.astype(np.float32).astype(ml_dtypes.bfloat16)
    low = (table - high.astype(np.float64)).astype(np.float32).astype(ml_dtypes.bfloat16)
    return high, low


def row_tables(table):
    high, low = halves(table)
    return np.concatenate([high, low], axis=0)


def col_tables(table):
    high, low = halves(table)
    return np.concatenate([high, low], axis=1)


def phases(rows, cols, length):
    index = np.outer(np.asarray(rows), np.asarray(cols)) % length
    return index * (2.0 * np.pi / length)


def padded_rows(table, rows):
    return np.pad(table, ((0, rows - table.shape[0]), (0, 0)))


def padded_cols(table, cols):
    return np.pad(table, ((0, 0), (0, cols - table.shape[1])))


def up8(n):
    return -(-n // 8) * 8


class Plan:
    def __init__(self, xs, ys, zs):
        self.xs, self.ys, self.zs = xs, ys, zs
        self.lx, self.ly, self.lz = xs + TEMPL, ys + HALF, zs + HALF
        self.kx, self.ky, self.kz = self.lx // 2 + 1, self.ly // 2 + 1, self.lz // 2 + 1
        self.kxp, self.kyp = up8(self.kx), up8(self.ky)
        self.kxc = -(-self.kx // 4) * 4
        self.kxi = 2 * self.kxc

    def folded(self, count, pad, points, length):
        angle = phases(np.arange(count), points, length)
        return np.concatenate(
            [padded_rows(np.cos(angle), pad), padded_rows(np.sin(angle), pad)], axis=0
        )

    def slab_z(self):
        angle = phases(np.arange(self.zs), np.arange(self.kz), self.lz)
        cos = padded_cols(np.cos(angle), ZF)
        sin = padded_cols(-np.sin(angle), ZF)
        one = np.concatenate([cos, cos, sin, sin], axis=1)
        none = np.zeros_like(one)
        high, low = halves(np.block([[one, none], [none, one]]))
        return np.concatenate([high, low], axis=0)

    def tmpl_z(self):
        angle = phases(np.arange(TEMPL) - HALF, np.arange(self.kz), self.lz)
        cos = np.zeros((ZF, ZF))
        sin = np.zeros((ZF, ZF))
        cos[:TEMPL, : self.kz] = np.cos(angle)
        sin[:TEMPL, : self.kz] = np.sin(angle)
        none = np.zeros_like(cos)
        return np.block([[cos, none, sin, none], [none, cos, none, sin]])

    def inverse_rows(self, points, count, length, k_pad, tail):
        angle = phases(points, np.arange(count), length)
        weight = np.full((1, count), 1.0 / length)
        weight[0, 0] *= 0.5
        weight[0, count - 1] *= 0.5
        cos = padded_cols(np.cos(angle) * weight, k_pad)
        sin = padded_cols(np.sin(angle) * weight, k_pad)
        return padded_cols(np.concatenate([cos, sin], axis=1), tail)

    def inverse_z(self):
        angle = phases(np.arange(self.kz), np.arange(self.zs), self.lz)
        weight = np.full((self.kz, 1), 2.0 / self.lz)
        weight[0] *= 0.5
        weight[self.kz - 1] *= 0.5
        cos = padded_rows(np.cos(angle) * weight, ZF)
        sin = padded_rows(-np.sin(angle) * weight, ZF)
        none = np.zeros_like(cos)
        return np.block([[cos, none], [none, cos], [sin, none], [none, sin]])


def unrolled(body, count):
    def many(i, carry):
        return lax.fori_loop(0, count, lambda part, c: body(i * count + part, c), carry, unroll=True)

    return many


def split(value):
    high = value.astype(BF16)
    return high, (value - high.astype(F32)).astype(BF16)


def mm(left, right):
    return jnp.dot(left, right, preferred_element_type=F32)


def rows_product(table, value):
    count = table.shape[0] // 2
    high, low = split(value)
    both = mm(table, high)
    return both[:count] + both[count:] + mm(table[:count], low)


def stacked_table(table):
    high, low = halves(table)
    return np.concatenate([high, high, low], axis=1)


def stacked_product(table, value):
    high, low = split(value)
    return mm(table, jnp.concatenate([high, low, high], axis=0))


def paired_table(table):
    high, low = halves(table)
    return np.block([[high, high], [low, np.zeros_like(low)]])


def paired_product(table, value):
    high, low = split(value)
    count = table.shape[0] // 2
    both = mm(table, jnp.concatenate([high, low], axis=0))
    return both[:count] + both[count:]


def plus_minus(folded, count, sign):
    cos_re, cos_im = folded[:count, :LANES], folded[:count, LANES:]
    sin_re, sin_im = folded[count:, :LANES], folded[count:, LANES:]
    first = (cos_re - sin_im, cos_im + sin_re)
    second = (cos_re + sin_im, cos_im - sin_re)
    return (first, second) if sign > 0 else (second, first)


def exact(left, right):
    return jnp.dot(left, right, precision=lax.Precision.HIGHEST, preferred_element_type=F32)


def tall_sum(value):
    return jnp.sum(value.reshape(-1, 8, value.shape[-1]), axis=0)


def tile_of(z, x, core):
    return (z * RING_X + x) * CORES + core


def greet(peers):
    barrier = pltpu.get_barrier_semaphore()
    for peer in peers:
        pl.semaphore_signal(barrier, inc=1, device_id=peer, device_id_type=MESH)
    pl.semaphore_wait(barrier, len(peers))


def remote(source, target, sends, receives, index, peer):
    return pltpu.make_async_remote_copy(
        src_ref=source,
        dst_ref=target,
        send_sem=sends.at[index],
        recv_sem=receives.at[index],
        device_id=peer,
        device_id_type=MESH,
    )


def begin(source, target, sends, receives, first, peers):
    copies = [
        remote(source, target, sends, receives, first + index, peer)
        for index, peer in enumerate(peers)
    ]
    for copy in copies:
        copy.start()
    return copies


def finish(copies):
    for copy in copies:
        copy.wait()


def match_kernel(
    plan, tiles, groups, own, block, valid, extra, slab_z, slab_x, slab_y, table_z, table_x,
    table_y, table_yi, table_xi, table_zi, zsum, ones, parts, stats, low, high, bank, spectrum,
    slab_mid, zed, mid, back, marks, ready, row, sends, receives, part_sends, part_receives,
):
    ring_z = tiles // (CORES * RING_X)
    plane_size = RING_X * CORES
    kxp, kyp, ys, xs = plan.kxp, plan.kyp, plan.ys, plan.xs
    rows = 2 * kxp
    tile, rot = lax.axis_index("tile"), lax.axis_index("rot")
    core = lax.rem(tile, CORES)
    x = lax.rem(tile // CORES, RING_X)
    z = tile // (CORES * RING_X)
    flat = x * CORES + core
    z_peers = [{"tile": tile_of(lax.rem(z + d, ring_z), x, core)} for d in range(1, ring_z)]
    x_peers = [{"tile": tile_of(z, lax.rem(x + d, RING_X), core)} for d in range(1, RING_X)]
    other = [{"tile": tile_of(z, x, 1 - core)}]
    plane = []
    for d in range(1, plane_size):
        there = lax.rem(flat + d, plane_size)
        plane.append({"tile": tile_of(z, there // CORES, lax.rem(there, CORES))})
    rot_peers = [{"rot": lax.rem(rot + d, groups)} for d in range(1, groups)]
    after = {"tile": lax.rem(tile + 1, tiles)}
    before = {"tile": lax.rem(tile + tiles - 1, tiles)}

    bank[core, x, z] = block[...]
    greet([after, before] + z_peers + plane + rot_peers)
    halo = [
        remote(own, low, sends, receives, 0, after),
        remote(own, high, sends, receives, 1, before),
    ]
    for copy in halo:
        copy.start()
    mine = bank.at[core, x, z]
    copies = begin(mine, mine, sends, receives, 2, z_peers)

    flags = valid[...].astype(F32)
    columns = jnp.sum(flags)
    for y in range(ys):
        marks[y * xs : y * xs + xs, :] = jnp.broadcast_to(flags[:, y : y + 1], (xs, LANES))
    row[...] = extra[...]
    finish(halo)

    def slab_first(j, carry):
        lanes = pl.ds(pl.multiple_of(j * LANES, LANES), LANES)
        strips = [
            jnp.where(tile > 0, low[:, lanes].astype(F32)[xs - HALF :], 0.0),
            own[:, lanes].astype(F32),
            jnp.where(tile < tiles - 1, high[:, lanes].astype(F32)[:HALF], 0.0),
        ]
        strip = jnp.concatenate(strips, axis=0).astype(BF16)
        strip = mm(jnp.concatenate([strip, strip], axis=1), slab_z[...])
        for part in range(2):
            folded = stacked_product(slab_x[...], strip[:, part * 256 : part * 256 + 256])
            for s, (re, im) in enumerate(plus_minus(folded, kxp, -1)):
                at = pl.ds(pl.multiple_of((2 * j + part) * rows + s * kxp, 8), kxp)
                slab_mid[0, at, :] = re
                slab_mid[1, at, :] = im
        return carry

    trips = ys // 2 // 4
    lax.fori_loop(0, trips // 2, unrolled(slab_first, 4), 0)
    finish(copies)
    mine = bank.at[core, x]
    copies = begin(mine, mine, sends, receives, 1 + ring_z, x_peers)
    lax.fori_loop(trips // 2, trips, unrolled(slab_first, 4), 0)
    finish(copies)
    mine = bank.at[core]
    copies = begin(mine, mine, sends, receives, ring_z + RING_X, other)

    def slab_second(k, carry):
        for s in range(2):
            at = pl.ds(k + s * kxp, ys, stride=rows)
            value = jnp.concatenate([slab_mid[0, at, :], slab_mid[1, at, :]], axis=1)
            folded = stacked_product(slab_y[...], value)
            for u, (re, im) in enumerate(plus_minus(folded, kyp, -1)):
                spectrum[k, s, u, :, :LANES] = re
                spectrum[k, s, u, :, LANES:] = im
        return carry

    lax.fori_loop(0, plan.kxc // 11, unrolled(slab_second, 11), 0)
    finish(copies)

    per = TEMPL * TEMPL // tiles
    total = float(TEMPL**3)
    lane = lax.broadcasted_iota(jnp.int32, (BLOCK, LANES), 1)
    line = lax.broadcasted_iota(jnp.int32, (BLOCK, LANES), 0)
    used = jnp.logical_and(lax.rem(lane, ZF) < TEMPL, line < per)[None]
    field = lax.rem(lax.broadcasted_iota(jnp.int32, (1, LANES), 1), ZF)
    share = ys // groups
    step = share
    tall = ring_z * BLOCK

    def pair(p, outer):
        def add_up(i, carry):
            value = bank[i // RING_X, lax.rem(i, RING_X), :, p].astype(F32)
            return carry + tall_sum(value.reshape(tall, LANES))

        sums = lax.fori_loop(0, plane_size, add_up, jnp.zeros((8, LANES), F32))
        mean = jnp.sum(exact(sums, ones[...]), axis=0, keepdims=True) / total

        def add_squares(i, carry):
            value = bank[i // RING_X, lax.rem(i, RING_X), :, p].astype(F32)
            off = jnp.where(used, value - mean[None], 0.0)
            return carry + tall_sum((off * off).reshape(tall, LANES))

        squares = lax.fori_loop(0, plane_size, add_squares, jnp.zeros((8, LANES), F32))
        variance = jnp.sum(exact(squares, ones[...]), axis=0, keepdims=True) / total
        factor = 1.0 / (jnp.sqrt(variance + EPSILON) * float(TEMPL) ** 1.5)
        shift = jnp.concatenate([mean, mean], axis=1) * zsum[...]
        scale = jnp.concatenate([factor, factor], axis=1)

        def z_stage(i, carry):
            lines = bank[i // RING_X, lax.rem(i, RING_X), :, p].reshape(tall, LANES)
            value = mm(jnp.concatenate([lines, lines], axis=1), table_z[...])
            value = (value - shift) * scale
            at = pl.ds(pl.multiple_of(i * tall, tall), tall)
            zed[0, at, :] = value[:, :LANES]
            zed[1, at, :] = value[:, LANES:]
            return carry

        lax.fori_loop(0, plane_size, z_stage, 0)

        def x_stage(b, carry):
            lines = []
            for s in range(TEMPL // ring_z):
                index = s * TEMPL + b
                owner = index // per
                there = lax.rem(owner, CORES) * RING_X + owner // CORES
                at = pl.ds(there * tall + lax.rem(index, per), ring_z, stride=BLOCK)
                lines.append(jnp.concatenate([zed[0, at, :], zed[1, at, :]], axis=1))
            folded = stacked_product(table_x[...], jnp.concatenate(lines, axis=0))
            for s, (re, im) in enumerate(plus_minus(folded, kxp, 1)):
                to = pl.ds(pl.multiple_of(b * rows + s * kxp, 8), kxp)
                mid[0, to, :] = re
                mid[1, to, :] = im
            return carry

        lax.fori_loop(0, TEMPL // 12, unrolled(x_stage, 12), 0)

        def y_stage(k, carry):
            found = []
            for s in range(2):
                at = pl.ds(k + s * kxp, TEMPL, stride=rows)
                value = jnp.concatenate([mid[0, at, :], mid[1, at, :]], axis=1)
                folded = stacked_product(table_y[...], value)
                sides = []
                for u, (re, im) in enumerate(plus_minus(folded, kyp, 1)):
                    slab_re = spectrum[k, s, u, :, :LANES]
                    slab_im = spectrum[k, s, u, :, LANES:]
                    sides.append((re * slab_re - im * slab_im, re * slab_im + im * slab_re))
                (re_p, im_p), (re_m, im_m) = sides
                even = jnp.concatenate([re_p + re_m, im_p + im_m], axis=1)
                odd = jnp.concatenate([im_m - im_p, re_p - re_m], axis=1)
                found.append(paired_product(table_yi[...], jnp.concatenate([even, odd], axis=0)))
            even = found[0] + found[1]
            odd = found[0] - found[1]
            to = pl.ds(pl.multiple_of(k * ys, 8), ys)
            back[0, to, :] = even[:, :LANES]
            back[1, to, :] = even[:, LANES:]
            to = pl.ds(pl.multiple_of((k + plan.kxc) * ys, 8), ys)
            back[0, to, :] = -odd[:, LANES:]
            back[1, to, :] = odd[:, :LANES]
            return carry

        lax.fori_loop(0, plan.kxc // 11, unrolled(y_stage, 11), 0)

        def last(i, lane_sum):
            j = lax.rem(i + 1, groups)
            base = lax.rem(rot + j, groups) * share
            lines = []
            for y in range(step):
                at = pl.ds(base + y, plan.kxi, stride=ys)
                value = jnp.concatenate([back[0, at, :], back[1, at, :]], axis=1)
                lines.append(rows_product(table_xi[...], value))
            upper, lower = split(jnp.concatenate(lines, axis=0))
            both = mm(upper, table_zi[...])
            value = both[:, :LANES] + both[:, LANES:] + mm(lower, table_zi[:, :LANES])
            ready[p, j] = value

            @pl.when(j > 0)
            def _():
                send_part(p, j).start()

            mark = marks[pl.ds(pl.multiple_of(base * xs, 8), share * xs), :]
            return lane_sum + tall_sum(value * mark)

        def send_part(p, j):
            return pltpu.make_async_remote_copy(
                src_ref=ready.at[p, j],
                dst_ref=parts.at[p, j],
                send_sem=part_sends.at[p, j],
                recv_sem=part_receives.at[p, j],
                device_id={"rot": lax.rem(rot + j, groups)},
                device_id_type=MESH,
            )

        lane_sum = lax.fori_loop(0, groups, last, jnp.zeros((8, LANES), F32))
        parts[p, 0] = ready[p, 0]
        lane_mean = jnp.sum(lane_sum, axis=0, keepdims=True) / jnp.maximum(columns, 1.0)

        def add_off(j, carry):
            base = lax.rem(rot + j, groups) * (share * xs)
            mark = marks[pl.ds(pl.multiple_of(base, 8), share * xs), :]
            off = ready[p, j] - lane_mean
            return carry + tall_sum(off * off * mark)

        lane_square = lax.fori_loop(0, groups, add_off, jnp.zeros((8, LANES), F32))
        wide = jnp.broadcast_to(lane_mean, (8, LANES))
        part_mean = exact(wide, ones[...])[:1] / float(plan.zs)
        off = lane_mean - part_mean
        lane_square = jnp.sum(lane_square, axis=0, keepdims=True) + columns * off * off
        part_square = exact(jnp.broadcast_to(lane_square, (8, LANES)), ones[...])[:1]
        now = jnp.where(field == 2 * p, part_mean, row[...])
        row[...] = jnp.where(field == 2 * p + 1, part_square, now)
        return outer

    lax.fori_loop(0, 2, pair, 0)
    stats[rot, flat, z] = row[...]
    first = 1 + ring_z + RING_X
    mine = stats.at[rot, flat, z]
    finish(begin(mine, mine, sends, receives, first, z_peers))
    mine = stats.at[rot, flat]
    finish(begin(mine, mine, sends, receives, first + ring_z - 1, plane))
    mine = stats.at[rot]
    finish(begin(mine, mine, sends, receives, first + ring_z + plane_size - 2, rot_peers))
    for p in range(2):
        for j in range(1, groups):
            remote(
                ready.at[p, j], parts.at[p, j], part_sends.at[p], part_receives.at[p], j, rot_peers[j - 1]
            ).wait()


def matched(plan, tiles, groups, own, block, valid, extra):
    ring_z = tiles // (CORES * RING_X)
    order = (
        np.arange(TEMPL // ring_z)[:, None] + (TEMPL // ring_z) * np.arange(ring_z)[None]
    ).reshape(-1)
    z_table = plan.tmpl_z()
    tables = [
        plan.slab_z(),
        stacked_table(plan.folded(plan.kx, plan.kxp, np.arange(plan.lx), plan.lx)),
        stacked_table(plan.folded(plan.ky, plan.kyp, np.arange(plan.ys), plan.ly)),
        row_stack(z_table),
        stacked_table(plan.folded(plan.kx, plan.kxp, order, plan.lx)),
        stacked_table(plan.folded(plan.ky, plan.kyp, np.arange(TEMPL) - HALF, plan.ly)),
        paired_table(plan.inverse_rows(np.arange(plan.ys), plan.ky, plan.ly, plan.kyp, 2 * plan.kyp)),
        row_tables(plan.inverse_rows(np.arange(plan.xs), plan.kx, plan.lx, plan.kxc, plan.kxi)),
        col_tables(plan.inverse_z()),
        z_table.sum(axis=0, keepdims=True).astype(np.float32),
        np.kron(np.eye(2), np.ones((ZF, ZF))).astype(np.float32),
    ]
    share = plan.ys // groups * plan.xs
    copies = ring_z + RING_X + 1 + ring_z + RING_X * CORES + groups - 3
    vmem = pl.BlockSpec(memory_space=pltpu.VMEM)
    return pl.pallas_call(
        functools.partial(match_kernel, plan, tiles, groups),
        out_shape=[
            jax.ShapeDtypeStruct((2, groups, share, LANES), F32),
            jax.ShapeDtypeStruct((groups, RING_X * CORES, ring_z, 1, LANES), F32),
        ],
        in_specs=[vmem] * (4 + len(tables)),
        out_specs=[vmem] * 2,
        scratch_shapes=[
            pltpu.VMEM(own.shape, BF16),
            pltpu.VMEM(own.shape, BF16),
            pltpu.VMEM((CORES, RING_X, ring_z) + block.shape, BF16),
            pltpu.VMEM((plan.kxc, 2, 2, plan.kyp, 2 * LANES), F32),
            pltpu.VMEM((2, plan.ys * 2 * plan.kxp, LANES), F32),
            pltpu.VMEM((2, tiles * BLOCK, LANES), F32),
            pltpu.VMEM((2, TEMPL * 2 * plan.kxp, LANES), F32),
            pltpu.VMEM((2, plan.kxi * plan.ys, LANES), F32),
            pltpu.VMEM((plan.ys * plan.xs, LANES), F32),
            pltpu.VMEM((2, groups, share, LANES), F32),
            pltpu.VMEM((1, LANES), F32),
            pltpu.SemaphoreType.DMA((copies,)),
            pltpu.SemaphoreType.DMA((copies,)),
            pltpu.SemaphoreType.DMA((2, groups)),
            pltpu.SemaphoreType.DMA((2, groups)),
        ],
        compiler_params=pltpu.CompilerParams(
            collective_id=0, has_side_effects=True, vmem_limit_bytes=60 << 20
        ),
        name="match",
    )(own, block, valid, extra, *tables)


def row_stack(table):
    return np.concatenate(halves(table), axis=0)


def final_kernel(groups, xs, zs, where, valid, stats, parts, best, evidence, moments):
    lane = lax.broadcasted_iota(jnp.int32, (1, LANES), 1)
    low_half = lane < ZF

    def spread_field(rows, index):
        return jnp.where(low_half, rows[:, index : index + 1], rows[:, ZF + index : ZF + index + 1])

    terms = []
    for j in range(groups):
        group = lax.rem(where[0] + groups - j, groups)
        rows = stats[group]
        rows = rows.reshape(-1, LANES)
        columns = spread_field(rows, FIELD_COUNT)
        total = jnp.sum(columns, axis=0, keepdims=True)
        for p in range(2):
            mean = spread_field(rows, 2 * p)
            square = spread_field(rows, 2 * p + 1)
            average = jnp.sum(columns * mean, axis=0, keepdims=True) / total
            off = mean - average
            square = jnp.sum(square + (zs * columns) * off * off, axis=0, keepdims=True)
            inverse = 1.0 / jnp.sqrt(square / (total * zs) + EPSILON)
            quat = [spread_field(rows[:1], FIELD_QUAT + 4 * p + c) for c in range(4)]
            terms.append((parts.at[p, j], average, inverse, quat))

    def column(y):
        at = pl.ds(pl.multiple_of(y * xs, 8), xs)
        scores = [(ref[at, :] - average) * inverse for ref, average, inverse, _ in terms]
        high = functools.reduce(jnp.maximum, scores)
        high = jnp.maximum(high, pltpu.roll(high, ZF, 1))
        weights = [jnp.exp(score - high) for score in scores]
        sums = [functools.reduce(jnp.add, weights)]
        for c in range(4):
            sums.append(functools.reduce(jnp.add, [w * t[3][c] for w, t in zip(weights, terms)]))
        return [high] + [value + pltpu.roll(value, ZF, 1) for value in sums]

    for j in range(valid.shape[1] // 2):
        both = [jnp.where(low_half, a, b) for a, b in zip(column(2 * j), column(2 * j + 1))]
        inside = jnp.where(low_half, valid[:, 2 * j : 2 * j + 1], valid[:, 2 * j + 1 : 2 * j + 2])
        inside = inside.astype(F32)
        high, total = both[0], both[1]
        lanes = slice(j * LANES, j * LANES + LANES)
        best[:, lanes] = inside * high
        evidence[:, lanes] = inside * (high + jnp.log(total))
        ratio = inside / total
        for c in range(4):
            moments[c, :, lanes] = both[2 + c] * ratio


def finished(where, valid, stats, parts, zs):
    groups = parts.shape[1]
    xs, share = valid.shape
    smem = pl.BlockSpec(memory_space=pltpu.SMEM)
    vmem = pl.BlockSpec(memory_space=pltpu.VMEM)
    flat = jax.ShapeDtypeStruct((xs, share * zs), F32)
    return pl.pallas_call(
        functools.partial(final_kernel, groups, xs, zs),
        out_shape=[flat, flat, jax.ShapeDtypeStruct((4, xs, share * zs), F32)],
        in_specs=[smem] + [vmem] * 3,
        out_specs=[vmem] * 3,
        compiler_params=pltpu.CompilerParams(vmem_limit_bytes=48 << 20),
        name="finish_scores",
    )(where, valid, stats, parts)


def local(tomogram, templates, valid, quats, rot_index):
    xs, voxels = tomogram.shape
    ys = valid.shape[1]
    zs = voxels // ys
    plan = Plan(xs, ys, zs)
    tiles, groups = lax.axis_size("tile"), lax.axis_size("rot")
    rot = lax.axis_index("rot")
    share = ys // groups
    per = templates.shape[1] // TEMPL
    block = templates.reshape(2, 2, per, TEMPL).transpose(0, 2, 1, 3)
    block = jnp.pad(block, ((0, 0), (0, BLOCK - per), (0, 0), (0, ZF - TEMPL)))
    block = block.reshape(2, BLOCK, LANES)
    columns = jnp.sum(valid).astype(F32)
    one_hot = rot_index[:, None] == jnp.arange(quats.shape[1], dtype=jnp.int32)[None, :]
    orient = jnp.sum(jnp.where(one_hot[:, None, :], quats[None], 0.0), axis=2)
    fields = orient.reshape(2, 2, 4).transpose(1, 0, 2).reshape(2, 8)
    extra = jnp.concatenate(
        [jnp.zeros((2, 4), F32), jnp.full((2, 1), columns), fields, jnp.zeros((2, ZF - 13), F32)],
        axis=1,
    ).reshape(1, LANES)
    parts, rows = matched(plan, tiles, groups, tomogram, block, valid, extra)
    own_valid = lax.dynamic_slice_in_dim(valid, rot * share, share, 1)
    where = rot.astype(jnp.int32).reshape(1)
    rows = rows.reshape(groups, tiles, 1, LANES)
    return tuple(finished(where, own_valid, rows, parts, zs))


def solution(mesh):
    placed = (P("tile", None), P("rot", "tile"), P("tile", None), P(), P("rot"))
    return jax.shard_map(
        local,
        mesh=mesh,
        in_specs=placed,
        out_specs=(P("tile", "rot"), P("tile", "rot"), P(None, "tile", "rot")),
        check_vma=False,
    )
```

```python
import functools
import math

import jax
import jax.numpy as jnp
import ml_dtypes
import numpy as np
from jax import lax
from jax.experimental import pallas as pl
from jax.experimental.pallas import tpu as pltpu
from jax.sharding import PartitionSpec as P

TEMPL = 48
HALF = 24
EPSILON = 1e-06
LANES = 128
ZF = 64
CORES = 2
RING_X = 4
BLOCK = 80
HALO_PARTS = 4
MESH = pl.DeviceIdType.MESH
FIELD_COUNT = 4
FIELD_QUAT = 5
F32 = jnp.float32
BF16 = jnp.bfloat16


def halves(table):
    high = table.astype(np.float32).astype(ml_dtypes.bfloat16)
    low = (table - high.astype(np.float64)).astype(np.float32).astype(ml_dtypes.bfloat16)
    return high, low


def row_tables(table):
    high, low = halves(table)
    return np.concatenate([high, low], axis=0)


def col_tables(table):
    high, low = halves(table)
    return np.concatenate([high, low], axis=1)


def phases(rows, cols, length):
    index = np.outer(np.asarray(rows), np.asarray(cols)) % length
    return index * (2.0 * np.pi / length)


def padded_rows(table, rows):
    return np.pad(table, ((0, rows - table.shape[0]), (0, 0)))


def padded_cols(table, cols):
    return np.pad(table, ((0, 0), (0, cols - table.shape[1])))


def up8(n):
    return -(-n // 8) * 8


class Plan:
    def __init__(self, xs, ys, zs):
        self.xs, self.ys, self.zs = xs, ys, zs
        self.lx, self.ly, self.lz = xs + TEMPL, ys + HALF, zs + HALF
        self.kx, self.ky, self.kz = self.lx // 2 + 1, self.ly // 2 + 1, self.lz // 2 + 1
        self.kxp, self.kyp = up8(self.kx), up8(self.ky)
        self.kxc = -(-self.kx // 4) * 4
        self.kxi = 2 * self.kxc

    def folded(self, count, pad, points, length):
        angle = phases(np.arange(count), points, length)
        return np.concatenate(
            [padded_rows(np.cos(angle), pad), padded_rows(np.sin(angle), pad)], axis=0
        )

    def slab_z(self):
        angle = phases(np.arange(self.zs), np.arange(self.kz), self.lz)
        cos = padded_cols(np.cos(angle), ZF)
        sin = padded_cols(-np.sin(angle), ZF)
        one = np.concatenate([cos, sin], axis=1)
        return np.kron(np.eye(2), one)

    def tmpl_z(self):
        angle = phases(np.arange(TEMPL) - HALF, np.arange(self.kz), self.lz)
        cos = np.zeros((ZF, ZF))
        sin = np.zeros((ZF, ZF))
        cos[:TEMPL, : self.kz] = np.cos(angle)
        sin[:TEMPL, : self.kz] = np.sin(angle)
        none = np.zeros_like(cos)
        return np.block([[cos, none, sin, none], [none, cos, none, sin]])

    def inverse_rows(self, points, count, length, k_pad, tail):
        angle = phases(points, np.arange(count), length)
        weight = np.full((1, count), 1.0 / length)
        weight[0, 0] *= 0.5
        weight[0, count - 1] *= 0.5
        cos = padded_cols(np.cos(angle) * weight, k_pad)
        sin = padded_cols(np.sin(angle) * weight, k_pad)
        return padded_cols(np.concatenate([cos, sin], axis=1), tail)

    def inverse_z(self):
        angle = phases(np.arange(self.kz), np.arange(self.zs), self.lz)
        weight = np.full((self.kz, 1), 2.0 / self.lz)
        weight[0] *= 0.5
        weight[self.kz - 1] *= 0.5
        cos = padded_rows(np.cos(angle) * weight, ZF)
        sin = padded_rows(-np.sin(angle) * weight, ZF)
        none = np.zeros_like(cos)
        return np.block([[cos, none], [none, cos], [sin, none], [none, sin]])


def unrolled(body, count):
    def many(i, carry):
        return lax.fori_loop(0, count, lambda part, c: body(i * count + part, c), carry, unroll=True)

    return many


def split(value):
    high = value.astype(BF16)
    return high, (value - high.astype(F32)).astype(BF16)


def mm(left, right):
    return jnp.dot(left, right, preferred_element_type=F32)


def rows_product(table, value):
    count = table.shape[0] // 2
    high, low = split(value)
    both = mm(table, high)
    return both[:count] + both[count:] + mm(table[:count], low)


def stacked_table(table):
    high, low = halves(table)
    return np.concatenate([high, high, low], axis=1)


def stacked_product(table, value):
    high, low = split(value)
    return mm(table, jnp.concatenate([high, low, high], axis=0))


def paired_table(table):
    high, low = halves(table)
    return np.block([[high, high], [low, np.zeros_like(low)]])


def paired_product(table, value):
    high, low = split(value)
    count = table.shape[0] // 2
    both = mm(table, jnp.concatenate([high, low], axis=0))
    return both[:count] + both[count:]


def plus_minus(folded, count, sign):
    cos_re, cos_im = folded[:count, :LANES], folded[:count, LANES:]
    sin_re, sin_im = folded[count:, :LANES], folded[count:, LANES:]
    first = (cos_re - sin_im, cos_im + sin_re)
    second = (cos_re + sin_im, cos_im - sin_re)
    return (first, second) if sign > 0 else (second, first)


def exact(left, right):
    return jnp.dot(left, right, precision=lax.Precision.HIGHEST, preferred_element_type=F32)


def tall_sum(value):
    return jnp.sum(value.reshape(-1, 8, value.shape[-1]), axis=0)


def tile_of(z, x, core):
    return (z * RING_X + x) * CORES + core


def greet(peers):
    barrier = pltpu.get_barrier_semaphore()
    for peer in peers:
        pl.semaphore_signal(barrier, inc=1, device_id=peer, device_id_type=MESH)
    pl.semaphore_wait(barrier, len(peers))


def remote(source, target, sends, receives, index, peer):
    return pltpu.make_async_remote_copy(
        src_ref=source,
        dst_ref=target,
        send_sem=sends.at[index],
        recv_sem=receives.at[index],
        device_id=peer,
        device_id_type=MESH,
    )


def begin(source, target, sends, receives, first, peers):
    copies = [
        remote(source, target, sends, receives, first + index, peer)
        for index, peer in enumerate(peers)
    ]
    for copy in copies:
        copy.start()
    return copies


def finish(copies):
    for copy in copies:
        copy.wait()


def packed_sides(folded, count, low_half):
    cos, sin = folded[:count], folded[count:]
    swapped = pltpu.roll(sin, ZF, 1)
    turned = jnp.where(low_half, swapped, -swapped)
    return cos + turned, cos - turned


def match_kernel(
    plan, tiles, groups, own, block, valid, quats, rot_index, slab_z, slab_x, slab_y, table_z,
    table_x, table_y, table_yi, table_xi, table_zi, zsum, ones, best, evidence, moments, parts,
    stats, low, high, bank, spectrum, slab_mid, zed, mid, back, marks, ready, row, sends,
    receives, part_sends, part_receives,
):
    ring_z = tiles // (CORES * RING_X)
    plane_size = RING_X * CORES
    kxp, kyp, ys, xs = plan.kxp, plan.kyp, plan.ys, plan.xs
    rows = 2 * kxp
    tile, rot = lax.axis_index("tile"), lax.axis_index("rot")
    core = lax.rem(tile, CORES)
    x = lax.rem(tile // CORES, RING_X)
    z = tile // (CORES * RING_X)
    flat = x * CORES + core
    z_peers = [{"tile": tile_of(lax.rem(z + d, ring_z), x, core)} for d in range(1, ring_z)]
    x_peers = [{"tile": tile_of(z, lax.rem(x + d, RING_X), core)} for d in range(1, RING_X)]
    other = {"tile": tile_of(z, x, 1 - core)}
    plane = []
    for d in range(1, plane_size):
        there = lax.rem(flat + d, plane_size)
        plane.append({"tile": tile_of(z, there // CORES, lax.rem(there, CORES))})
    rot_peers = [{"rot": lax.rem(rot + d, groups)} for d in range(1, groups)]
    after = {"tile": lax.rem(tile + 1, tiles)}
    before = {"tile": lax.rem(tile + tiles - 1, tiles)}
    low_half = lax.broadcasted_iota(jnp.int32, (1, LANES), 1) < ZF
    width = ys * plan.zs // HALO_PARTS
    first_halo, first_z = 0, 2 * HALO_PARTS
    first_x = first_z + ring_z - 1
    first_pass = first_x + RING_X
    first_stats = first_pass + RING_X - 1

    greet([after, before] + z_peers + plane + rot_peers)

    def halo(q):
        lanes = pl.ds(pl.multiple_of(q * width, LANES), width)
        return [
            remote(own.at[:, lanes], low.at[:, lanes], sends, receives, first_halo + 2 * q, after),
            remote(own.at[:, lanes], high.at[:, lanes], sends, receives, first_halo + 2 * q + 1, before),
        ]

    for q in range(HALO_PARTS):
        for copy in halo(q):
            copy.start()
    bank[core, x, z] = block[...]
    mine = bank.at[core, x, z]
    copies = begin(mine, mine, sends, receives, first_z, z_peers)

    flags = valid[...].astype(F32)
    columns = jnp.sum(flags)
    for y in range(ys):
        marks[y * xs : y * xs + xs, :] = jnp.broadcast_to(flags[:, y : y + 1], (xs, LANES))
    field = lax.rem(lax.broadcasted_iota(jnp.int32, (1, LANES), 1), ZF)
    line = jnp.where(field == FIELD_COUNT, columns, 0.0)
    entry = lax.broadcasted_iota(jnp.int32, quats.shape, 1)
    for r in range(4):
        found = jnp.sum(jnp.where(entry == rot_index[r], quats[...], 0.0), axis=1, keepdims=True)
        half = low_half if r % 2 == 0 else jnp.logical_not(low_half)
        for c in range(4):
            here = jnp.logical_and(field == FIELD_QUAT + 4 * (r // 2) + c, half)
            line = jnp.where(here, found[c : c + 1], line)
    row[...] = line

    def slab_first(j, carry):
        lanes = pl.ds(pl.multiple_of(j * LANES, LANES), LANES)
        strips = [
            jnp.where(tile > 0, low[:, lanes].astype(F32)[xs - HALF :], 0.0),
            own[:, lanes].astype(F32),
            jnp.where(tile < tiles - 1, high[:, lanes].astype(F32)[:HALF], 0.0),
        ]
        strip = jnp.concatenate(strips, axis=0).astype(BF16)
        strip = mm(jnp.concatenate([strip, strip], axis=1), slab_z[...])
        folded = stacked_product(slab_x[...], strip)
        for part in range(2):
            sides = packed_sides(folded[:, part * LANES : part * LANES + LANES], kxp, low_half)
            for s in range(2):
                at = pl.ds(pl.multiple_of((2 * j + part) * rows + s * kxp, 8), kxp)
                slab_mid[at, :] = sides[s]
        return carry

    pieces = ys // 2 // HALO_PARTS

    def slab_part(q, carry):
        for copy in halo(q):
            copy.wait()

        def body(i, inner):
            return lax.fori_loop(
                0, 5, lambda t, c: slab_first(q * pieces + i * 5 + t, c), inner, unroll=True
            )

        return lax.fori_loop(0, pieces // 5, body, carry)

    lax.fori_loop(0, HALO_PARTS // 2, slab_part, 0)
    finish(copies)
    mine = bank.at[core, x]
    copies = begin(mine, mine, sends, receives, first_x, x_peers + [other])
    lax.fori_loop(HALO_PARTS // 2, HALO_PARTS, slab_part, 0)

    def slab_second(k, carry):
        lines = [slab_mid[pl.ds(k + s * kxp, ys, stride=rows), :] for s in range(2)]
        folded = stacked_product(slab_y[...], jnp.concatenate(lines, axis=1))
        for s in range(2):
            sides = packed_sides(folded[:, s * LANES : s * LANES + LANES], kyp, low_half)
            for u in range(2):
                swapped = pltpu.roll(sides[u], ZF, 1)
                spectrum[k, s, u, :, :LANES] = jnp.where(low_half, sides[u], swapped)
                spectrum[k, s, u, :, LANES:] = jnp.where(low_half, swapped, sides[u])
        return carry

    trips = plan.kxc // 11
    lax.fori_loop(0, trips // 2, unrolled(slab_second, 11), 0)
    forwards = []
    for d in range(1, RING_X):
        copies[d - 1].wait()
        mine = bank.at[core, lax.rem(x + RING_X - d, RING_X)]
        forward = remote(mine, mine, sends, receives, first_pass + d - 1, other)
        forward.start()
        forwards.append(forward)
    lax.fori_loop(trips // 2, trips, unrolled(slab_second, 11), 0)
    copies[-1].wait()
    finish(forwards)

    per = TEMPL * TEMPL // tiles
    total = float(TEMPL**3)
    lane = lax.broadcasted_iota(jnp.int32, (BLOCK, LANES), 1)
    place = lax.broadcasted_iota(jnp.int32, (BLOCK, LANES), 0)
    used = jnp.logical_and(lax.rem(lane, ZF) < TEMPL, place < 2 * per)[None]
    tall = ring_z * BLOCK

    def lane_groups(value):
        wide = jnp.broadcast_to(jnp.sum(value, axis=0, keepdims=True), (8, LANES))
        return exact(wide, ones[...])[:1]

    def both_pairs(value):
        first = lane_groups(jnp.where(place < per, value, 0.0))
        second = lane_groups(jnp.where(place < per, 0.0, value))
        return first, second

    def bank_rows(i):
        return bank[i // RING_X, lax.rem(i, RING_X)]

    def add_up(i, carry):
        return carry + jnp.sum(bank_rows(i).astype(F32), axis=0)

    empty = jnp.zeros((BLOCK, LANES), F32)
    means = both_pairs(lax.fori_loop(0, plane_size, add_up, empty))
    means = [mean / total for mean in means]
    mean_rows = jnp.where(place < per, means[0], means[1])[None]

    def add_squares(i, carry):
        off = jnp.where(used, bank_rows(i).astype(F32) - mean_rows, 0.0)
        return carry + jnp.sum(off * off, axis=0)

    squares = both_pairs(lax.fori_loop(0, plane_size, add_squares, empty))
    factors = [
        1.0 / (jnp.sqrt(square / total + EPSILON) * float(TEMPL) ** 1.5) for square in squares
    ]
    scale_rows = jnp.where(place < per, factors[0], factors[1])[None]

    def z_stage(i, carry):
        lines = bank_rows(i).reshape(tall, LANES)
        value = mm(jnp.concatenate([lines, lines], axis=1), table_z[...])
        at = pl.ds(pl.multiple_of(i * tall, tall), tall)
        for part in range(2):
            lanes = slice(part * LANES, part * LANES + LANES)
            side = value[:, lanes].reshape(ring_z, BLOCK, LANES)
            side = (side - mean_rows * zsum[:, lanes]) * scale_rows
            zed[part, at, :] = side.reshape(tall, LANES)
        return carry

    lax.fori_loop(0, plane_size, z_stage, 0)
    share = ys // groups
    step = share

    def pair(p, outer):
        def x_stage(b, carry):
            lines = []
            for s in range(TEMPL // ring_z):
                index = s * TEMPL + b
                owner = index // per
                there = lax.rem(owner, CORES) * RING_X + owner // CORES
                at = pl.ds(there * tall + p * per + lax.rem(index, per), ring_z, stride=BLOCK)
                lines.append(jnp.concatenate([zed[0, at, :], zed[1, at, :]], axis=1))
            folded = stacked_product(table_x[...], jnp.concatenate(lines, axis=0))
            for s, (re, im) in enumerate(plus_minus(folded, kxp, 1)):
                to = pl.ds(pl.multiple_of(b * rows + s * kxp, 8), kxp)
                mid[0, to, :] = re
                mid[1, to, :] = im
            return carry

        lax.fori_loop(0, TEMPL // 12, unrolled(x_stage, 12), 0)

        def y_stage(k, carry):
            found = []
            for s in range(2):
                at = pl.ds(k + s * kxp, TEMPL, stride=rows)
                value = jnp.concatenate([mid[0, at, :], mid[1, at, :]], axis=1)
                folded = stacked_product(table_y[...], value)
                sides = []
                for u, (re, im) in enumerate(plus_minus(folded, kyp, 1)):
                    slab_re = spectrum[k, s, u, :, :LANES]
                    slab_im = spectrum[k, s, u, :, LANES:]
                    sides.append((re * slab_re - im * slab_im, re * slab_im + im * slab_re))
                (re_p, im_p), (re_m, im_m) = sides
                even = jnp.concatenate([re_p + re_m, im_p + im_m], axis=1)
                odd = jnp.concatenate([im_m - im_p, re_p - re_m], axis=1)
                found.append(paired_product(table_yi[...], jnp.concatenate([even, odd], axis=0)))
            even = found[0] + found[1]
            odd = found[0] - found[1]
            to = pl.ds(pl.multiple_of(k * ys, 8), ys)
            back[0, to, :] = even[:, :LANES]
            back[1, to, :] = even[:, LANES:]
            to = pl.ds(pl.multiple_of((k + plan.kxc) * ys, 8), ys)
            back[0, to, :] = -odd[:, LANES:]
            back[1, to, :] = odd[:, :LANES]
            return carry

        lax.fori_loop(0, plan.kxc // 11, unrolled(y_stage, 11), 0)

        def last(i, lane_sum):
            j = lax.rem(2 + 3 * i + 3 * (i * (i - 1) // 2), groups)
            base = lax.rem(rot + j, groups) * share
            lines = []
            for y in range(step):
                at = pl.ds(base + y, plan.kxi, stride=ys)
                value = jnp.concatenate([back[0, at, :], back[1, at, :]], axis=1)
                lines.append(rows_product(table_xi[...], value))
            upper, lower = split(jnp.concatenate(lines, axis=0))
            both = mm(upper, table_zi[...])
            value = both[:, :LANES] + both[:, LANES:] + mm(lower, table_zi[:, :LANES])
            ready[p, j] = value

            @pl.when(j > 0)
            def _():
                send_part(p, j).start()

            mark = marks[pl.ds(pl.multiple_of(base * xs, 8), share * xs), :]
            return lane_sum + tall_sum(value * mark)

        def send_part(p, j):
            return pltpu.make_async_remote_copy(
                src_ref=ready.at[p, j],
                dst_ref=parts.at[p, j],
                send_sem=part_sends.at[p, j],
                recv_sem=part_receives.at[p, j],
                device_id={"rot": lax.rem(rot + j, groups)},
                device_id_type=MESH,
            )

        lane_sum = lax.fori_loop(0, groups, last, jnp.zeros((8, LANES), F32))
        parts[p, 0] = ready[p, 0]
        lane_mean = jnp.sum(lane_sum, axis=0, keepdims=True) / jnp.maximum(columns, 1.0)

        def add_off(j, carry):
            base = lax.rem(rot + j, groups) * (share * xs)
            mark = marks[pl.ds(pl.multiple_of(base, 8), share * xs), :]
            off = ready[p, j] - lane_mean
            return carry + tall_sum(off * off * mark)

        lane_square = lax.fori_loop(0, groups, add_off, jnp.zeros((8, LANES), F32))
        wide = jnp.broadcast_to(lane_mean, (8, LANES))
        part_mean = exact(wide, ones[...])[:1] / float(plan.zs)
        off = lane_mean - part_mean
        lane_square = jnp.sum(lane_square, axis=0, keepdims=True) + columns * off * off
        part_square = exact(jnp.broadcast_to(lane_square, (8, LANES)), ones[...])[:1]
        now = jnp.where(field == 2 * p, part_mean, row[...])
        row[...] = jnp.where(field == 2 * p + 1, part_square, now)
        return outer

    lax.fori_loop(0, 2, pair, 0)
    stats[rot, flat, z] = row[...]
    mine = stats.at[rot, flat, z]
    finish(begin(mine, mine, sends, receives, first_stats, z_peers))
    mine = stats.at[rot, flat]
    finish(begin(mine, mine, sends, receives, first_stats + ring_z - 1, plane))
    mine = stats.at[rot]
    finish(begin(mine, mine, sends, receives, first_stats + ring_z + plane_size - 2, rot_peers))
    incoming = [
        remote(ready.at[p, j], parts.at[p, j], part_sends.at[p], part_receives.at[p], j, rot_peers[j - 1])
        for p in range(2)
        for j in range(1, groups)
    ]

    def spread_field(lines, index):
        return jnp.where(
            low_half, lines[:, index : index + 1], lines[:, ZF + index : ZF + index + 1]
        )

    terms = []
    for j in range(groups):
        group = lax.rem(rot + groups - j, groups)
        lines = stats[group].reshape(-1, LANES)
        count = spread_field(lines, FIELD_COUNT)
        total = jnp.sum(count, axis=0, keepdims=True)
        for p in range(2):
            mean = spread_field(lines, 2 * p)
            square = spread_field(lines, 2 * p + 1)
            average = jnp.sum(count * mean, axis=0, keepdims=True) / total
            off = mean - average
            square = jnp.sum(square + (plan.zs * count) * off * off, axis=0, keepdims=True)
            inverse = 1.0 / jnp.sqrt(square / (total * plan.zs) + EPSILON)
            quat = [spread_field(lines[:1], FIELD_QUAT + 4 * p + c) for c in range(4)]
            terms.append((parts.at[p, j], average, inverse, quat))

    finish(incoming)

    def column(y):
        at = pl.ds(pl.multiple_of(y * xs, 8), xs)
        scores = [(ref[at, :] - average) * inverse for ref, average, inverse, _ in terms]
        high = functools.reduce(jnp.maximum, scores)
        high = jnp.maximum(high, pltpu.roll(high, ZF, 1))
        weights = [jnp.exp(score - high) for score in scores]
        sums = [functools.reduce(jnp.add, weights)]
        for c in range(4):
            sums.append(functools.reduce(jnp.add, [w * t[3][c] for w, t in zip(weights, terms)]))
        return [high] + [value + pltpu.roll(value, ZF, 1) for value in sums]

    def answer(j, carry):
        both = [jnp.where(low_half, a, b) for a, b in zip(column(2 * j), column(2 * j + 1))]
        base = pl.multiple_of(rot * (share * xs) + 2 * j * xs, 8)
        inside = jnp.where(
            low_half, marks[pl.ds(base, xs), :], marks[pl.ds(pl.multiple_of(base + xs, 8), xs), :]
        )
        high, total = both[0], both[1]
        lanes = pl.ds(pl.multiple_of(j * LANES, LANES), LANES)
        best[:, lanes] = inside * high
        evidence[:, lanes] = inside * (high + jnp.log(total))
        ratio = inside / total
        for c in range(4):
            moments[c, :, lanes] = both[2 + c] * ratio
        return carry

    lax.fori_loop(0, share // 2 // 5, unrolled(answer, 5), 0)


def matched(plan, tiles, groups, own, block, valid, quats, rot_index):
    ring_z = tiles // (CORES * RING_X)
    order = (
        np.arange(TEMPL // ring_z)[:, None] + (TEMPL // ring_z) * np.arange(ring_z)[None]
    ).reshape(-1)
    z_table = plan.tmpl_z()
    tables = [
        row_stack(plan.slab_z()),
        stacked_table(plan.folded(plan.kx, plan.kxp, np.arange(plan.lx), plan.lx)),
        stacked_table(plan.folded(plan.ky, plan.kyp, np.arange(plan.ys), plan.ly)),
        row_stack(z_table),
        stacked_table(plan.folded(plan.kx, plan.kxp, order, plan.lx)),
        stacked_table(plan.folded(plan.ky, plan.kyp, np.arange(TEMPL) - HALF, plan.ly)),
        paired_table(plan.inverse_rows(np.arange(plan.ys), plan.ky, plan.ly, plan.kyp, 2 * plan.kyp)),
        row_tables(plan.inverse_rows(np.arange(plan.xs), plan.kx, plan.lx, plan.kxc, plan.kxi)),
        col_tables(plan.inverse_z()),
        z_table.sum(axis=0, keepdims=True).astype(np.float32),
        np.kron(np.eye(2), np.ones((ZF, ZF))).astype(np.float32),
    ]
    share = plan.ys // groups * plan.xs
    copies = 2 * HALO_PARTS + 2 * ring_z + 2 * RING_X + RING_X * CORES + groups - 5
    vmem = pl.BlockSpec(memory_space=pltpu.VMEM)
    flat_out = jax.ShapeDtypeStruct((plan.xs, plan.ys // groups * plan.zs), F32)
    return pl.pallas_call(
        functools.partial(match_kernel, plan, tiles, groups),
        out_shape=[flat_out, flat_out, jax.ShapeDtypeStruct((4,) + flat_out.shape, F32)],
        in_specs=[vmem] * 4
        + [pl.BlockSpec(memory_space=pltpu.SMEM)]
        + [vmem] * len(tables),
        out_specs=[vmem] * 3,
        scratch_shapes=[
            pltpu.VMEM((2, groups, share, LANES), F32),
            pltpu.VMEM((groups, RING_X * CORES, ring_z, 1, LANES), F32),
            pltpu.VMEM(own.shape, BF16),
            pltpu.VMEM(own.shape, BF16),
            pltpu.VMEM((CORES, RING_X, ring_z) + block.shape, BF16),
            pltpu.VMEM((plan.kxc, 2, 2, plan.kyp, 2 * LANES), F32),
            pltpu.VMEM((plan.ys * 2 * plan.kxp, LANES), F32),
            pltpu.VMEM((2, tiles * BLOCK, LANES), F32),
            pltpu.VMEM((2, TEMPL * 2 * plan.kxp, LANES), F32),
            pltpu.VMEM((2, plan.kxi * plan.ys, LANES), F32),
            pltpu.VMEM((plan.ys * plan.xs, LANES), F32),
            pltpu.VMEM((2, groups, share, LANES), F32),
            pltpu.VMEM((1, LANES), F32),
            pltpu.SemaphoreType.DMA((copies,)),
            pltpu.SemaphoreType.DMA((copies,)),
            pltpu.SemaphoreType.DMA((2, groups)),
            pltpu.SemaphoreType.DMA((2, groups)),
        ],
        compiler_params=pltpu.CompilerParams(
            collective_id=0, has_side_effects=True, vmem_limit_bytes=60 << 20
        ),
        name="match",
    )(own, block, valid, quats, rot_index, *tables)


def row_stack(table):
    return np.concatenate(halves(table), axis=0)


def local(tomogram, templates, valid, quats, rot_index):
    xs, voxels = tomogram.shape
    ys = valid.shape[1]
    zs = voxels // ys
    plan = Plan(xs, ys, zs)
    tiles, groups = lax.axis_size("tile"), lax.axis_size("rot")
    per = templates.shape[1] // TEMPL
    block = templates.reshape(2, 2, per, TEMPL).transpose(0, 2, 1, 3)
    block = jnp.pad(block, ((0, 0), (0, 0), (0, 0), (0, ZF - TEMPL))).reshape(2 * per, LANES)
    block = jnp.pad(block, ((0, BLOCK - 2 * per), (0, 0)))
    return tuple(matched(plan, tiles, groups, tomogram, block, valid, quats, rot_index))


def solution(mesh):
    placed = (P("tile", None), P("rot", "tile"), P("tile", None), P(), P("rot"))
    return jax.shard_map(
        local,
        mesh=mesh,
        in_specs=placed,
        out_specs=(P("tile", "rot"), P("tile", "rot"), P(None, "tile", "rot")),
        check_vma=False,
    )
```

```python
import functools
import math

import jax
import jax.numpy as jnp
import ml_dtypes
import numpy as np
from jax import lax
from jax.experimental import pallas as pl
from jax.experimental.pallas import tpu as pltpu
from jax.sharding import PartitionSpec as P

TEMPL = 48
HALF = 24
EPSILON = 1e-06
LANES = 128
ZF = 64
CORES = 2
RING_X = 4
BLOCK = 80
HALO_PARTS = 4
MESH = pl.DeviceIdType.MESH
FIELD_COUNT = 4
FIELD_QUAT = 5
F32 = jnp.float32
BF16 = jnp.bfloat16


def halves(table):
    high = table.astype(np.float32).astype(ml_dtypes.bfloat16)
    low = (table - high.astype(np.float64)).astype(np.float32).astype(ml_dtypes.bfloat16)
    return high, low


def row_tables(table):
    high, low = halves(table)
    return np.concatenate([high, low], axis=0)


def col_tables(table):
    high, low = halves(table)
    return np.concatenate([high, low], axis=1)


def phases(rows, cols, length):
    index = np.outer(np.asarray(rows), np.asarray(cols)) % length
    return index * (2.0 * np.pi / length)


def padded_rows(table, rows):
    return np.pad(table, ((0, rows - table.shape[0]), (0, 0)))


def padded_cols(table, cols):
    return np.pad(table, ((0, 0), (0, cols - table.shape[1])))


def up8(n):
    return -(-n // 8) * 8


class Plan:
    def __init__(self, xs, ys, zs):
        self.xs, self.ys, self.zs = xs, ys, zs
        self.lx, self.ly, self.lz = xs + TEMPL, ys + HALF, zs + HALF
        self.kx, self.ky, self.kz = self.lx // 2 + 1, self.ly // 2 + 1, self.lz // 2 + 1
        self.kxp, self.kyp = up8(self.kx), up8(self.ky)
        self.kxc = -(-self.kx // 4) * 4
        self.kxi = 2 * self.kxc

    def folded(self, count, pad, points, length):
        angle = phases(np.arange(count), points, length)
        return np.concatenate(
            [padded_rows(np.cos(angle), pad), padded_rows(np.sin(angle), pad)], axis=0
        )

    def slab_z(self):
        angle = phases(np.arange(self.zs), np.arange(self.kz), self.lz)
        cos = padded_cols(np.cos(angle), ZF)
        sin = padded_cols(-np.sin(angle), ZF)
        one = np.concatenate([cos, sin], axis=1)
        return np.kron(np.eye(2), one)

    def tmpl_z(self):
        angle = phases(np.arange(TEMPL) - HALF, np.arange(self.kz), self.lz)
        cos = np.zeros((ZF, ZF))
        sin = np.zeros((ZF, ZF))
        cos[:TEMPL, : self.kz] = np.cos(angle)
        sin[:TEMPL, : self.kz] = np.sin(angle)
        none = np.zeros_like(cos)
        return np.block([[cos, none, sin, none], [none, cos, none, sin]])

    def inverse_rows(self, points, count, length, k_pad, tail):
        angle = phases(points, np.arange(count), length)
        weight = np.full((1, count), 1.0 / length)
        weight[0, 0] *= 0.5
        weight[0, count - 1] *= 0.5
        cos = padded_cols(np.cos(angle) * weight, k_pad)
        sin = padded_cols(np.sin(angle) * weight, k_pad)
        return padded_cols(np.concatenate([cos, sin], axis=1), tail)

    def inverse_z(self):
        angle = phases(np.arange(self.kz), np.arange(self.zs), self.lz)
        weight = np.full((self.kz, 1), 2.0 / self.lz)
        weight[0] *= 0.5
        weight[self.kz - 1] *= 0.5
        cos = padded_rows(np.cos(angle) * weight, ZF)
        sin = padded_rows(-np.sin(angle) * weight, ZF)
        none = np.zeros_like(cos)
        return np.block([[cos, none], [none, cos], [sin, none], [none, sin]])


def unrolled(body, count):
    def many(i, carry):
        return lax.fori_loop(0, count, lambda part, c: body(i * count + part, c), carry, unroll=True)

    return many


def split(value):
    high = value.astype(BF16)
    return high, (value - high.astype(F32)).astype(BF16)


def mm(left, right):
    return jnp.dot(left, right, preferred_element_type=F32)


def rows_product(table, value):
    count = table.shape[0] // 2
    high, low = split(value)
    both = mm(table, high)
    return both[:count] + both[count:] + mm(table[:count], low)


def stacked_table(table):
    high, low = halves(table)
    return np.concatenate([high, high, low], axis=1)


def stacked_product(table, value):
    high, low = split(value)
    return mm(table, jnp.concatenate([high, low, high], axis=0))


def paired_table(table):
    high, low = halves(table)
    return np.block([[high, high], [low, np.zeros_like(low)]])


def paired_product(table, value):
    high, low = split(value)
    count = table.shape[0] // 2
    both = mm(table, jnp.concatenate([high, low], axis=0))
    return both[:count] + both[count:]


def plus_minus(folded, count, sign):
    cos_re, cos_im = folded[:count, :LANES], folded[:count, LANES:]
    sin_re, sin_im = folded[count:, :LANES], folded[count:, LANES:]
    first = (cos_re - sin_im, cos_im + sin_re)
    second = (cos_re + sin_im, cos_im - sin_re)
    return (first, second) if sign > 0 else (second, first)


def exact(left, right):
    return jnp.dot(left, right, precision=lax.Precision.HIGHEST, preferred_element_type=F32)


def tall_sum(value):
    return jnp.sum(value.reshape(-1, 8, value.shape[-1]), axis=0)


def tile_of(z, x, core):
    return (z * RING_X + x) * CORES + core


def greet(peers):
    barrier = pltpu.get_barrier_semaphore()
    for peer in peers:
        pl.semaphore_signal(barrier, inc=1, device_id=peer, device_id_type=MESH)
    pl.semaphore_wait(barrier, len(peers))


def remote(source, target, sends, receives, index, peer):
    return pltpu.make_async_remote_copy(
        src_ref=source,
        dst_ref=target,
        send_sem=sends.at[index],
        recv_sem=receives.at[index],
        device_id=peer,
        device_id_type=MESH,
    )


def begin(source, target, sends, receives, first, peers):
    copies = [
        remote(source, target, sends, receives, first + index, peer)
        for index, peer in enumerate(peers)
    ]
    for copy in copies:
        copy.start()
    return copies


def finish(copies):
    for copy in copies:
        copy.wait()


def packed_sides(folded, count, low_half):
    cos, sin = folded[:count], folded[count:]
    swapped = pltpu.roll(sin, ZF, 1)
    turned = jnp.where(low_half, swapped, -swapped)
    return cos + turned, cos - turned


def match_kernel(
    plan, tiles, groups, spots, own, block, valid, quats, rot_index, packed, zsum, ones, best, evidence, moments, parts,
    stats, low, high, bank, spectrum, slab_mid, zed, mid, back, marks, ready, row, sends,
    receives, part_sends, part_receives,
):
    slab_z, slab_x, slab_y, table_z, table_x, table_y, table_yi, table_xi, table_zi = [
        packed.at[first : first + tall, :wide] for first, tall, wide in spots
    ]
    ring_z = tiles // (CORES * RING_X)
    plane_size = RING_X * CORES
    kxp, kyp, ys, xs = plan.kxp, plan.kyp, plan.ys, plan.xs
    rows = 2 * kxp
    tile, rot = lax.axis_index("tile"), lax.axis_index("rot")
    core = lax.rem(tile, CORES)
    x = lax.rem(tile // CORES, RING_X)
    z = tile // (CORES * RING_X)
    z_peers = [{"tile": tile_of(lax.rem(z + d, ring_z), x, core)} for d in range(1, ring_z)]
    x_peers = [{"tile": tile_of(z, lax.rem(x + d, RING_X), core)} for d in range(1, RING_X)]
    other = {"tile": tile_of(z, x, 1 - core)}
    line_size, sheet_size = ring_z * CORES, RING_X * groups
    line_peers, sheet_peers = [], []
    for d in range(1, line_size):
        there = lax.rem(z * CORES + core + d, line_size)
        line_peers.append({"tile": tile_of(there // CORES, x, lax.rem(there, CORES))})
    for d in range(1, sheet_size):
        there = lax.rem(x * groups + rot + d, sheet_size)
        sheet_peers.append(
            {"tile": tile_of(z, there // groups, core), "rot": lax.rem(there, groups)}
        )
    after = {"tile": lax.rem(tile + 1, tiles)}
    before = {"tile": lax.rem(tile + tiles - 1, tiles)}
    low_half = lax.broadcasted_iota(jnp.int32, (1, LANES), 1) < ZF
    width = ys * plan.zs // HALO_PARTS
    first_halo, first_z = 0, 2 * HALO_PARTS
    first_x = first_z + ring_z - 1
    first_pass = first_x + RING_X
    first_stats = first_pass + RING_X - 1

    greet([after, before] + line_peers + sheet_peers)

    def halo(q):
        lanes = pl.ds(pl.multiple_of(q * width, LANES), width)
        return [
            remote(own.at[:, lanes], low.at[:, lanes], sends, receives, first_halo + 2 * q, after),
            remote(own.at[:, lanes], high.at[:, lanes], sends, receives, first_halo + 2 * q + 1, before),
        ]

    for q in range(HALO_PARTS):
        for copy in halo(q):
            copy.start()
    bank[core, x, z] = block[...]
    mine = bank.at[core, x, z]
    copies = begin(mine, mine, sends, receives, first_z, z_peers)

    flags = valid[...].astype(F32)
    columns = jnp.sum(flags)
    for y in range(ys):
        marks[y * xs : y * xs + xs, :] = jnp.broadcast_to(flags[:, y : y + 1], (xs, LANES))
    field = lax.rem(lax.broadcasted_iota(jnp.int32, (1, LANES), 1), ZF)
    line = jnp.where(field == FIELD_COUNT, columns, 0.0)
    entry = lax.broadcasted_iota(jnp.int32, quats.shape, 1)
    for r in range(4):
        found = jnp.sum(jnp.where(entry == rot_index[r], quats[...], 0.0), axis=1, keepdims=True)
        half = low_half if r % 2 == 0 else jnp.logical_not(low_half)
        for c in range(4):
            here = jnp.logical_and(field == FIELD_QUAT + 4 * (r // 2) + c, half)
            line = jnp.where(here, found[c : c + 1], line)
    row[...] = line

    def slab_first(j, carry):
        lanes = pl.ds(pl.multiple_of(j * LANES, LANES), LANES)
        strips = [
            jnp.where(tile > 0, low[:, lanes].astype(F32)[xs - HALF :], 0.0),
            own[:, lanes].astype(F32),
            jnp.where(tile < tiles - 1, high[:, lanes].astype(F32)[:HALF], 0.0),
        ]
        strip = jnp.concatenate(strips, axis=0).astype(BF16)
        strip = mm(jnp.concatenate([strip, strip], axis=1), slab_z[...])
        folded = stacked_product(slab_x[...], strip)
        for part in range(2):
            sides = packed_sides(folded[:, part * LANES : part * LANES + LANES], kxp, low_half)
            for s in range(2):
                at = pl.ds(pl.multiple_of((2 * j + part) * rows + s * kxp, 8), kxp)
                slab_mid[at, :] = sides[s]
        return carry

    pieces = ys // 2 // HALO_PARTS

    def slab_part(q, carry):
        for copy in halo(q):
            copy.wait()

        def body(i, inner):
            return lax.fori_loop(
                0, 5, lambda t, c: slab_first(q * pieces + i * 5 + t, c), inner, unroll=True
            )

        return lax.fori_loop(0, pieces // 5, body, carry)

    lax.fori_loop(0, HALO_PARTS // 2, slab_part, 0)
    finish(copies)
    mine = bank.at[core, x]
    copies = begin(mine, mine, sends, receives, first_x, x_peers + [other])
    lax.fori_loop(HALO_PARTS // 2, HALO_PARTS, slab_part, 0)

    def slab_second(k, carry):
        lines = [slab_mid[pl.ds(k + s * kxp, ys, stride=rows), :] for s in range(2)]
        folded = stacked_product(slab_y[...], jnp.concatenate(lines, axis=1))
        for s in range(2):
            sides = packed_sides(folded[:, s * LANES : s * LANES + LANES], kyp, low_half)
            for u in range(2):
                swapped = pltpu.roll(sides[u], ZF, 1)
                spectrum[k, s, u, :, :LANES] = jnp.where(low_half, sides[u], swapped)
                spectrum[k, s, u, :, LANES:] = jnp.where(low_half, swapped, sides[u])
        return carry

    trips = plan.kxc // 11
    lax.fori_loop(0, trips // 2, unrolled(slab_second, 11), 0)
    forwards = []
    for d in range(1, RING_X):
        copies[d - 1].wait()
        mine = bank.at[core, lax.rem(x + RING_X - d, RING_X)]
        forward = remote(mine, mine, sends, receives, first_pass + d - 1, other)
        forward.start()
        forwards.append(forward)
    lax.fori_loop(trips // 2, trips, unrolled(slab_second, 11), 0)
    copies[-1].wait()
    finish(forwards)

    per = TEMPL * TEMPL // tiles
    total = float(TEMPL**3)
    lane = lax.broadcasted_iota(jnp.int32, (BLOCK, LANES), 1)
    place = lax.broadcasted_iota(jnp.int32, (BLOCK, LANES), 0)
    used = jnp.logical_and(lax.rem(lane, ZF) < TEMPL, place < 2 * per)[None]
    tall = ring_z * BLOCK

    def lane_groups(value):
        wide = jnp.broadcast_to(jnp.sum(value, axis=0, keepdims=True), (8, LANES))
        return exact(wide, ones[...])[:1]

    def both_pairs(value):
        first = lane_groups(jnp.where(place < per, value, 0.0))
        second = lane_groups(jnp.where(place < per, 0.0, value))
        return first, second

    def bank_rows(i):
        return bank[i // RING_X, lax.rem(i, RING_X)]

    def add_up(i, carry):
        return carry + jnp.sum(bank_rows(i).astype(F32), axis=0)

    empty = jnp.zeros((BLOCK, LANES), F32)
    means = both_pairs(lax.fori_loop(0, plane_size, add_up, empty))
    means = [mean / total for mean in means]
    mean_rows = jnp.where(place < per, means[0], means[1])[None]

    def add_squares(i, carry):
        off = jnp.where(used, bank_rows(i).astype(F32) - mean_rows, 0.0)
        return carry + jnp.sum(off * off, axis=0)

    squares = both_pairs(lax.fori_loop(0, plane_size, add_squares, empty))
    factors = [
        1.0 / (jnp.sqrt(square / total + EPSILON) * float(TEMPL) ** 1.5) for square in squares
    ]
    scale_rows = jnp.where(place < per, factors[0], factors[1])[None]

    def z_stage(i, carry):
        lines = bank_rows(i).reshape(tall, LANES)
        value = mm(jnp.concatenate([lines, lines], axis=1), table_z[...])
        at = pl.ds(pl.multiple_of(i * tall, tall), tall)
        for part in range(2):
            lanes = slice(part * LANES, part * LANES + LANES)
            side = value[:, lanes].reshape(ring_z, BLOCK, LANES)
            side = (side - mean_rows * zsum[:, lanes]) * scale_rows
            zed[part, at, :] = side.reshape(tall, LANES)
        return carry

    lax.fori_loop(0, plane_size, z_stage, 0)
    share = ys // groups
    step = share

    def pair(p, outer):
        def x_stage(b, carry):
            lines = []
            for s in range(TEMPL // ring_z):
                index = s * TEMPL + b
                owner = index // per
                there = lax.rem(owner, CORES) * RING_X + owner // CORES
                at = pl.ds(there * tall + p * per + lax.rem(index, per), ring_z, stride=BLOCK)
                lines.append(jnp.concatenate([zed[0, at, :], zed[1, at, :]], axis=1))
            folded = stacked_product(table_x[...], jnp.concatenate(lines, axis=0))
            for s, (re, im) in enumerate(plus_minus(folded, kxp, 1)):
                to = pl.ds(pl.multiple_of(b * rows + s * kxp, 8), kxp)
                mid[0, to, :] = re
                mid[1, to, :] = im
            return carry

        lax.fori_loop(0, TEMPL // 12, unrolled(x_stage, 12), 0)

        def y_stage(k, carry):
            found = []
            for s in range(2):
                at = pl.ds(k + s * kxp, TEMPL, stride=rows)
                value = jnp.concatenate([mid[0, at, :], mid[1, at, :]], axis=1)
                folded = stacked_product(table_y[...], value)
                sides = []
                for u, (re, im) in enumerate(plus_minus(folded, kyp, 1)):
                    slab_re = spectrum[k, s, u, :, :LANES]
                    slab_im = spectrum[k, s, u, :, LANES:]
                    sides.append((re * slab_re - im * slab_im, re * slab_im + im * slab_re))
                (re_p, im_p), (re_m, im_m) = sides
                even = jnp.concatenate([re_p + re_m, im_p + im_m], axis=1)
                odd = jnp.concatenate([im_m - im_p, re_p - re_m], axis=1)
                found.append(paired_product(table_yi[...], jnp.concatenate([even, odd], axis=0)))
            even = found[0] + found[1]
            odd = found[0] - found[1]
            to = pl.ds(pl.multiple_of(k * ys, 8), ys)
            back[0, to, :] = even[:, :LANES]
            back[1, to, :] = even[:, LANES:]
            to = pl.ds(pl.multiple_of((k + plan.kxc) * ys, 8), ys)
            back[0, to, :] = -odd[:, LANES:]
            back[1, to, :] = odd[:, :LANES]
            return carry

        lax.fori_loop(0, plan.kxc // 11, unrolled(y_stage, 11), 0)

        def last(i, lane_sum):
            j = lax.rem(2 + 3 * i + 3 * (i * (i - 1) // 2), groups)
            base = lax.rem(rot + j, groups) * share
            lines = []
            for y in range(step):
                at = pl.ds(base + y, plan.kxi, stride=ys)
                value = jnp.concatenate([back[0, at, :], back[1, at, :]], axis=1)
                lines.append(rows_product(table_xi[...], value))
            upper, lower = split(jnp.concatenate(lines, axis=0))
            both = mm(upper, table_zi[...])
            value = both[:, :LANES] + both[:, LANES:] + mm(lower, table_zi[:, :LANES])
            ready[p, j] = value

            @pl.when(j > 0)
            def _():
                send_part(p, j).start()

            mark = marks[pl.ds(pl.multiple_of(base * xs, 8), share * xs), :]
            return lane_sum + tall_sum(value * mark)

        def send_part(p, j):
            return pltpu.make_async_remote_copy(
                src_ref=ready.at[p, j],
                dst_ref=parts.at[p, j],
                send_sem=part_sends.at[p, j],
                recv_sem=part_receives.at[p, j],
                device_id={"rot": lax.rem(rot + j, groups)},
                device_id_type=MESH,
            )

        lane_sum = lax.fori_loop(0, groups, last, jnp.zeros((8, LANES), F32))
        lane_mean = jnp.sum(lane_sum, axis=0, keepdims=True) / jnp.maximum(columns, 1.0)

        def add_off(j, carry):
            base = lax.rem(rot + j, groups) * (share * xs)
            mark = marks[pl.ds(pl.multiple_of(base, 8), share * xs), :]
            off = ready[p, j] - lane_mean
            return carry + tall_sum(off * off * mark)

        lane_square = lax.fori_loop(0, groups, add_off, jnp.zeros((8, LANES), F32))
        wide = jnp.broadcast_to(lane_mean, (8, LANES))
        part_mean = exact(wide, ones[...])[:1] / float(plan.zs)
        off = lane_mean - part_mean
        lane_square = jnp.sum(lane_square, axis=0, keepdims=True) + columns * off * off
        part_square = exact(jnp.broadcast_to(lane_square, (8, LANES)), ones[...])[:1]
        now = jnp.where(field == 2 * p, part_mean, row[...])
        row[...] = jnp.where(field == 2 * p + 1, part_square, now)
        return outer

    lax.fori_loop(0, 2, pair, 0)
    place = z * CORES + core
    stats[rot, x, place] = row[...]
    mine = stats.at[rot, x, place]
    finish(begin(mine, mine, sends, receives, first_stats, line_peers))
    mine = stats.at[rot, x]
    finish(begin(mine, mine, sends, receives, first_stats + line_size - 1, sheet_peers))
    incoming = [
        remote(ready.at[p, j], parts.at[p, j], part_sends.at[p], part_receives.at[p], j, {"rot": lax.rem(rot + j, groups)})
        for p in range(2)
        for j in range(1, groups)
    ]

    def spread_field(lines, index):
        return jnp.where(
            low_half, lines[:, index : index + 1], lines[:, ZF + index : ZF + index + 1]
        )

    terms = []
    for j in range(groups):
        group = lax.rem(rot + groups - j, groups)
        lines = stats[group].reshape(-1, LANES)
        count = lines[:, FIELD_COUNT : FIELD_COUNT + 1]
        total = jnp.sum(count, axis=0, keepdims=True)
        average = jnp.sum(count * lines, axis=0, keepdims=True) / total
        off = lines - average
        square = jnp.sum(count * off * off, axis=0, keepdims=True) * plan.zs
        square += pltpu.roll(jnp.sum(lines, axis=0, keepdims=True), LANES - 1, 1)
        inverse = 1.0 / jnp.sqrt(square / (total * plan.zs) + EPSILON)
        for p in range(2):
            source = ready if j == 0 else parts
            quat = [spread_field(lines[:1], FIELD_QUAT + 4 * p + c) for c in range(4)]
            terms.append(
                (source.at[p, j], spread_field(average, 2 * p), spread_field(inverse, 2 * p), quat)
            )

    finish(incoming)

    def column(y):
        at = pl.ds(pl.multiple_of(y * xs, 8), xs)
        scores = [(ref[at, :] - average) * inverse for ref, average, inverse, _ in terms]
        high = functools.reduce(jnp.maximum, scores)
        high = jnp.maximum(high, pltpu.roll(high, ZF, 1))
        weights = [jnp.exp(score - high) for score in scores]
        sums = [functools.reduce(jnp.add, weights)]
        for c in range(4):
            sums.append(functools.reduce(jnp.add, [w * t[3][c] for w, t in zip(weights, terms)]))
        return [high] + [value + pltpu.roll(value, ZF, 1) for value in sums]

    def answer(j, carry):
        both = [jnp.where(low_half, a, b) for a, b in zip(column(2 * j), column(2 * j + 1))]
        base = pl.multiple_of(rot * (share * xs) + 2 * j * xs, 8)
        inside = jnp.where(
            low_half, marks[pl.ds(base, xs), :], marks[pl.ds(pl.multiple_of(base + xs, 8), xs), :]
        )
        high, total = both[0], both[1]
        lanes = pl.ds(pl.multiple_of(j * LANES, LANES), LANES)
        best[:, lanes] = inside * high
        evidence[:, lanes] = inside * (high + jnp.log(total))
        ratio = inside / total
        for c in range(4):
            moments[c, :, lanes] = both[2 + c] * ratio
        return carry

    lax.fori_loop(0, share // 2 // 5, unrolled(answer, 5), 0)


def matched(plan, tiles, groups, own, block, valid, quats, rot_index):
    ring_z = tiles // (CORES * RING_X)
    order = (
        np.arange(TEMPL // ring_z)[:, None] + (TEMPL // ring_z) * np.arange(ring_z)[None]
    ).reshape(-1)
    z_table = plan.tmpl_z()
    tables = [
        row_stack(plan.slab_z()),
        stacked_table(plan.folded(plan.kx, plan.kxp, np.arange(plan.lx), plan.lx)),
        stacked_table(plan.folded(plan.ky, plan.kyp, np.arange(plan.ys), plan.ly)),
        row_stack(z_table),
        stacked_table(plan.folded(plan.kx, plan.kxp, order, plan.lx)),
        stacked_table(plan.folded(plan.ky, plan.kyp, np.arange(TEMPL) - HALF, plan.ly)),
        paired_table(plan.inverse_rows(np.arange(plan.ys), plan.ky, plan.ly, plan.kyp, 2 * plan.kyp)),
        row_tables(plan.inverse_rows(np.arange(plan.xs), plan.kx, plan.lx, plan.kxc, plan.kxi)),
        col_tables(plan.inverse_z()),
    ]
    spots, first = [], 0
    for table in tables:
        spots.append((first, table.shape[0], table.shape[1]))
        first += table.shape[0]
    tables = [
        np.concatenate([padded_cols(table, 2 * LANES) for table in tables], axis=0),
        z_table.sum(axis=0, keepdims=True).astype(np.float32),
        np.kron(np.eye(2), np.ones((ZF, ZF))).astype(np.float32),
    ]
    share = plan.ys // groups * plan.xs
    copies = 2 * HALO_PARTS + ring_z + 2 * RING_X - 2 + ring_z * CORES + RING_X * groups - 2
    vmem = pl.BlockSpec(memory_space=pltpu.VMEM)
    flat_out = jax.ShapeDtypeStruct((plan.xs, plan.ys // groups * plan.zs), F32)
    return pl.pallas_call(
        functools.partial(match_kernel, plan, tiles, groups, spots),
        out_shape=[flat_out, flat_out, jax.ShapeDtypeStruct((4,) + flat_out.shape, F32)],
        in_specs=[vmem] * 4
        + [pl.BlockSpec(memory_space=pltpu.SMEM)]
        + [vmem] * len(tables),
        out_specs=[vmem] * 3,
        scratch_shapes=[
            pltpu.VMEM((2, groups, share, LANES), F32),
            pltpu.VMEM((groups, RING_X, ring_z * CORES, 1, LANES), F32),
            pltpu.VMEM(own.shape, BF16),
            pltpu.VMEM(own.shape, BF16),
            pltpu.VMEM((CORES, RING_X, ring_z) + block.shape, BF16),
            pltpu.VMEM((plan.kxc, 2, 2, plan.kyp, 2 * LANES), F32),
            pltpu.VMEM((plan.ys * 2 * plan.kxp, LANES), F32),
            pltpu.VMEM((2, tiles * BLOCK, LANES), F32),
            pltpu.VMEM((2, TEMPL * 2 * plan.kxp, LANES), F32),
            pltpu.VMEM((2, plan.kxi * plan.ys, LANES), F32),
            pltpu.VMEM((plan.ys * plan.xs, LANES), F32),
            pltpu.VMEM((2, groups, share, LANES), F32),
            pltpu.VMEM((1, LANES), F32),
            pltpu.SemaphoreType.DMA((copies,)),
            pltpu.SemaphoreType.DMA((copies,)),
            pltpu.SemaphoreType.DMA((2, groups)),
            pltpu.SemaphoreType.DMA((2, groups)),
        ],
        compiler_params=pltpu.CompilerParams(
            collective_id=0, has_side_effects=True, vmem_limit_bytes=48 << 20
        ),
        name="match",
    )(own, block, valid, quats, rot_index, *tables)


def row_stack(table):
    return np.concatenate(halves(table), axis=0)


def local(tomogram, templates, valid, quats, rot_index):
    xs, voxels = tomogram.shape
    ys = valid.shape[1]
    zs = voxels // ys
    plan = Plan(xs, ys, zs)
    tiles, groups = lax.axis_size("tile"), lax.axis_size("rot")
    per = templates.shape[1] // TEMPL
    block = templates.reshape(2, 2, per, TEMPL).transpose(0, 2, 1, 3)
    block = jnp.pad(block, ((0, 0), (0, 0), (0, 0), (0, ZF - TEMPL))).reshape(2 * per, LANES)
    block = jnp.pad(block, ((0, BLOCK - 2 * per), (0, 0)))
    return tuple(matched(plan, tiles, groups, tomogram, block, valid, quats, rot_index))


def solution(mesh):
    placed = (P("tile", None), P("rot", "tile"), P("tile", None), P(), P("rot"))
    return jax.shard_map(
        local,
        mesh=mesh,
        in_specs=placed,
        out_specs=(P("tile", "rot"), P("tile", "rot"), P(None, "tile", "rot")),
        check_vma=False,
    )
```

```python
import functools
import math

import jax
import jax.numpy as jnp
import ml_dtypes
import numpy as np
from jax import lax
from jax.experimental import pallas as pl
from jax.experimental.pallas import tpu as pltpu
from jax.sharding import PartitionSpec as P

TEMPL = 48
HALF = 24
EPSILON = 1e-06
LANES = 128
ZF = 64
CORES = 2
RING_X = 4
BLOCK = 80
HALO_PARTS = 4
MESH = pl.DeviceIdType.MESH
FIELDS = 4
FIELD_COUNT = 8
FIELD_QUAT = 16
F32 = jnp.float32
BF16 = jnp.bfloat16


def halves(table):
    high = table.astype(np.float32).astype(ml_dtypes.bfloat16)
    low = (table - high.astype(np.float64)).astype(np.float32).astype(ml_dtypes.bfloat16)
    return high, low


def row_tables(table):
    high, low = halves(table)
    return np.concatenate([high, low], axis=0)


def col_tables(table):
    high, low = halves(table)
    return np.concatenate([high, low], axis=1)


def phases(rows, cols, length):
    index = np.outer(np.asarray(rows), np.asarray(cols)) % length
    return index * (2.0 * np.pi / length)


def padded_rows(table, rows):
    return np.pad(table, ((0, rows - table.shape[0]), (0, 0)))


def padded_cols(table, cols):
    return np.pad(table, ((0, 0), (0, cols - table.shape[1])))


def up8(n):
    return -(-n // 8) * 8


class Plan:
    def __init__(self, xs, ys, zs):
        self.xs, self.ys, self.zs = xs, ys, zs
        self.lx, self.ly, self.lz = xs + TEMPL, ys + HALF, zs + HALF
        self.kx, self.ky, self.kz = self.lx // 2 + 1, self.ly // 2 + 1, self.lz // 2 + 1
        self.kxp, self.kyp = up8(self.kx), up8(self.ky)
        self.kxc = -(-self.kx // 4) * 4
        self.kxi = 2 * self.kxc

    def folded(self, count, pad, points, length):
        angle = phases(np.arange(count), points, length)
        return np.concatenate(
            [padded_rows(np.cos(angle), pad), padded_rows(np.sin(angle), pad)], axis=0
        )

    def slab_z(self):
        angle = phases(np.arange(self.zs), np.arange(self.kz), self.lz)
        cos = padded_cols(np.cos(angle), ZF)
        sin = padded_cols(-np.sin(angle), ZF)
        one = np.concatenate([cos, sin], axis=1)
        return np.kron(np.eye(2), one)

    def tmpl_z(self):
        angle = phases(np.arange(TEMPL) - HALF, np.arange(self.kz), self.lz)
        cos = np.zeros((ZF, ZF))
        sin = np.zeros((ZF, ZF))
        cos[:TEMPL, : self.kz] = np.cos(angle)
        sin[:TEMPL, : self.kz] = np.sin(angle)
        return np.kron(np.eye(2), np.concatenate([cos, sin], axis=1))

    def inverse_rows(self, points, count, length, k_pad, tail):
        angle = phases(points, np.arange(count), length)
        weight = np.full((1, count), 1.0 / length)
        weight[0, 0] *= 0.5
        weight[0, count - 1] *= 0.5
        cos = padded_cols(np.cos(angle) * weight, k_pad)
        sin = padded_cols(np.sin(angle) * weight, k_pad)
        return padded_cols(np.concatenate([cos, sin], axis=1), tail)

    def inverse_z(self):
        angle = phases(np.arange(self.kz), np.arange(self.zs), self.lz)
        weight = np.full((self.kz, 1), 2.0 / self.lz)
        weight[0] *= 0.5
        weight[self.kz - 1] *= 0.5
        cos = padded_rows(np.cos(angle) * weight, ZF)
        sin = padded_rows(-np.sin(angle) * weight, ZF)
        return np.kron(np.eye(2), np.concatenate([cos, sin], axis=0))


def unrolled(body, count):
    def many(i, carry):
        return lax.fori_loop(0, count, lambda part, c: body(i * count + part, c), carry, unroll=True)

    return many


def split(value):
    high = value.astype(BF16)
    return high, (value - high.astype(F32)).astype(BF16)


def mm(left, right):
    return jnp.dot(left, right, preferred_element_type=F32)


def rows_product(table, value):
    count = table.shape[0] // 2
    high, low = split(value)
    both = mm(table, high)
    return both[:count] + both[count:] + mm(table[:count], low)


def stacked_table(table):
    high, low = halves(table)
    return np.concatenate([high, high, low], axis=1)


def stacked_product(table, value):
    high, low = split(value)
    return mm(table, jnp.concatenate([high, low, high], axis=0))


def paired_table(table):
    high, low = halves(table)
    return np.block([[high, high], [low, np.zeros_like(low)]])


def paired_product(table, value):
    high, low = split(value)
    count = table.shape[0] // 2
    both = mm(table, jnp.concatenate([high, low], axis=0))
    return both[:count] + both[count:]


def exact(left, right):
    return jnp.dot(left, right, precision=lax.Precision.HIGHEST, preferred_element_type=F32)


def tall_sum(value):
    return jnp.sum(value.reshape(-1, 8, value.shape[-1]), axis=0)


def tile_of(z, x, core):
    return (z * RING_X + x) * CORES + core


def greet(peers):
    barrier = pltpu.get_barrier_semaphore()
    for peer in peers:
        pl.semaphore_signal(barrier, inc=1, device_id=peer, device_id_type=MESH)
    pl.semaphore_wait(barrier, len(peers))


def remote(source, target, sends, receives, index, peer):
    return pltpu.make_async_remote_copy(
        src_ref=source,
        dst_ref=target,
        send_sem=sends.at[index],
        recv_sem=receives.at[index],
        device_id=peer,
        device_id_type=MESH,
    )


def begin(source, target, sends, receives, first, peers):
    copies = [
        remote(source, target, sends, receives, first + index, peer)
        for index, peer in enumerate(peers)
    ]
    for copy in copies:
        copy.start()
    return copies


def finish(copies):
    for copy in copies:
        copy.wait()


def packed_sides(folded, count, low_half):
    cos, sin = folded[:count], folded[count:]
    swapped = pltpu.roll(sin, ZF, 1)
    turned = jnp.where(low_half, swapped, -swapped)
    return cos + turned, cos - turned


def match_kernel(
    plan, tiles, groups, spots, own, block, valid, quats, rot_index, packed, zsum, ones, best, evidence, moments, parts,
    stats, low, high, bank, spectrum, slab_mid, zed, mid, back, marks, ready, row, sends,
    receives, part_sends, part_receives,
):
    slab_z, slab_x, slab_y, table_z, table_x, table_y, table_yi, table_xi, table_zi = [
        packed.at[first : first + tall, :wide] for first, tall, wide in spots
    ]
    ring_z = tiles // (CORES * RING_X)
    plane_size = RING_X * CORES
    kxp, kyp, ys, xs = plan.kxp, plan.kyp, plan.ys, plan.xs
    rows = 2 * kxp
    tile, rot = lax.axis_index("tile"), lax.axis_index("rot")
    core = lax.rem(tile, CORES)
    x = lax.rem(tile // CORES, RING_X)
    z = tile // (CORES * RING_X)
    z_peers = [{"tile": tile_of(lax.rem(z + d, ring_z), x, core)} for d in range(1, ring_z)]
    x_peers = [{"tile": tile_of(z, lax.rem(x + d, RING_X), core)} for d in range(1, RING_X)]
    other = {"tile": tile_of(z, x, 1 - core)}
    line_size, sheet_size = ring_z * CORES, RING_X * groups
    line_peers, sheet_peers = [], []
    for d in range(1, line_size):
        there = lax.rem(z * CORES + core + d, line_size)
        line_peers.append({"tile": tile_of(there // CORES, x, lax.rem(there, CORES))})
    for d in range(1, sheet_size):
        there = lax.rem(x * groups + rot + d, sheet_size)
        sheet_peers.append(
            {"tile": tile_of(z, there // groups, core), "rot": lax.rem(there, groups)}
        )
    after = {"tile": lax.rem(tile + 1, tiles)}
    before = {"tile": lax.rem(tile + tiles - 1, tiles)}
    low_half = lax.broadcasted_iota(jnp.int32, (1, LANES), 1) < ZF
    width = ys * plan.zs // HALO_PARTS
    first_halo, first_z = 0, 2 * HALO_PARTS
    first_x = first_z + ring_z - 1
    first_pass = first_x + RING_X
    first_stats = first_pass + RING_X - 1

    greet([after, before] + line_peers + sheet_peers)

    def halo(q):
        lanes = pl.ds(pl.multiple_of(q * width, LANES), width)
        return [
            remote(own.at[:, lanes], low.at[:, lanes], sends, receives, first_halo + 2 * q, after),
            remote(own.at[:, lanes], high.at[:, lanes], sends, receives, first_halo + 2 * q + 1, before),
        ]

    for q in range(HALO_PARTS):
        for copy in halo(q):
            copy.start()
    bank[core, x, z] = block[...]
    mine = bank.at[core, x, z]
    copies = begin(mine, mine, sends, receives, first_z, z_peers)

    flags = valid[...].astype(F32)
    columns = jnp.sum(flags)
    for y in range(0, ys, 2):
        marks[y // 2 * xs : y // 2 * xs + xs, :] = jnp.where(
            low_half, flags[:, y : y + 1], flags[:, y + 1 : y + 2]
        )
    field = lax.broadcasted_iota(jnp.int32, (1, LANES), 1)
    line = jnp.where(field == FIELD_COUNT, columns, 0.0)
    entry = lax.broadcasted_iota(jnp.int32, quats.shape, 1)
    for r in range(FIELDS):
        found = jnp.sum(jnp.where(entry == rot_index[r], quats[...], 0.0), axis=1, keepdims=True)
        for c in range(4):
            line = jnp.where(field == FIELD_QUAT + 4 * r + c, found[c : c + 1], line)
    row[...] = line

    def slab_first(j, carry):
        lanes = pl.ds(pl.multiple_of(j * LANES, LANES), LANES)
        strips = [
            jnp.where(tile > 0, low[:, lanes].astype(F32)[xs - HALF :], 0.0),
            own[:, lanes].astype(F32),
            jnp.where(tile < tiles - 1, high[:, lanes].astype(F32)[:HALF], 0.0),
        ]
        strip = jnp.concatenate(strips, axis=0).astype(BF16)
        strip = mm(jnp.concatenate([strip, strip], axis=1), slab_z[...])
        folded = stacked_product(slab_x[...], strip)
        for part in range(2):
            sides = packed_sides(folded[:, part * LANES : part * LANES + LANES], kxp, low_half)
            for s in range(2):
                at = pl.ds(pl.multiple_of((2 * j + part) * rows + s * kxp, 8), kxp)
                slab_mid[at, :] = sides[s]
        return carry

    pieces = ys // 2 // HALO_PARTS

    def slab_part(q, carry):
        for copy in halo(q):
            copy.wait()

        def body(i, inner):
            return lax.fori_loop(
                0, 5, lambda t, c: slab_first(q * pieces + i * 5 + t, c), inner, unroll=True
            )

        return lax.fori_loop(0, pieces // 5, body, carry)

    lax.fori_loop(0, HALO_PARTS // 2, slab_part, 0)
    finish(copies)
    mine = bank.at[core, x]
    copies = begin(mine, mine, sends, receives, first_x, x_peers + [other])
    lax.fori_loop(HALO_PARTS // 2, HALO_PARTS, slab_part, 0)

    def slab_second(k, carry):
        lines = [slab_mid[pl.ds(k + s * kxp, ys, stride=rows), :] for s in range(2)]
        folded = stacked_product(slab_y[...], jnp.concatenate(lines, axis=1))
        for s in range(2):
            sides = packed_sides(folded[:, s * LANES : s * LANES + LANES], kyp, low_half)
            for u in range(2):
                swapped = pltpu.roll(sides[u], ZF, 1)
                spectrum[k, s, u, :, :LANES] = jnp.where(low_half, sides[u], swapped)
                spectrum[k, s, u, :, LANES:] = jnp.where(low_half, -swapped, sides[u])
        return carry

    trips = plan.kxc // 11
    lax.fori_loop(0, trips // 2, unrolled(slab_second, 11), 0)
    forwards = []
    for d in range(1, RING_X):
        copies[d - 1].wait()
        mine = bank.at[core, lax.rem(x + RING_X - d, RING_X)]
        forward = remote(mine, mine, sends, receives, first_pass + d - 1, other)
        forward.start()
        forwards.append(forward)
    lax.fori_loop(trips // 2, trips, unrolled(slab_second, 11), 0)
    copies[-1].wait()
    finish(forwards)

    per = TEMPL * TEMPL // tiles
    total = float(TEMPL**3)
    lane = lax.broadcasted_iota(jnp.int32, (BLOCK, LANES), 1)
    place = lax.broadcasted_iota(jnp.int32, (BLOCK, LANES), 0)
    used = jnp.logical_and(lax.rem(lane, ZF) < TEMPL, place < 2 * per)[None]
    tall = ring_z * BLOCK

    def lane_groups(value):
        wide = jnp.broadcast_to(jnp.sum(value, axis=0, keepdims=True), (8, LANES))
        return exact(wide, ones[...])[:1]

    def both_pairs(value):
        first = lane_groups(jnp.where(place < per, value, 0.0))
        second = lane_groups(jnp.where(place < per, 0.0, value))
        return first, second

    def bank_rows(i):
        return bank[i // RING_X, lax.rem(i, RING_X)]

    def add_up(i, carry):
        return carry + jnp.sum(bank_rows(i).astype(F32), axis=0)

    empty = jnp.zeros((BLOCK, LANES), F32)
    means = both_pairs(lax.fori_loop(0, plane_size, add_up, empty))
    means = [mean / total for mean in means]
    mean_rows = jnp.where(place < per, means[0], means[1])[None]

    def add_squares(i, carry):
        off = jnp.where(used, bank_rows(i).astype(F32) - mean_rows, 0.0)
        return carry + jnp.sum(off * off, axis=0)

    squares = both_pairs(lax.fori_loop(0, plane_size, add_squares, empty))
    factors = [
        1.0 / (jnp.sqrt(square / total + EPSILON) * float(TEMPL) ** 1.5) for square in squares
    ]
    scale_rows = jnp.where(place < per, factors[0], factors[1])

    def for_halves(value):
        swapped = pltpu.roll(value, ZF, 1)
        return (
            jnp.where(low_half, value, swapped)[None],
            jnp.where(low_half, swapped, value)[None],
        )

    mean_halves, scale_halves = for_halves(mean_rows[0]), for_halves(scale_rows)

    def z_stage(i, carry):
        lines = bank_rows(i).reshape(tall, LANES)
        value = mm(jnp.concatenate([lines, lines], axis=1), table_z[...])
        at = pl.ds(pl.multiple_of(i * tall, tall), tall)
        for part in range(2):
            lanes = slice(part * LANES, part * LANES + LANES)
            side = value[:, lanes].reshape(ring_z, BLOCK, LANES)
            side = (side - mean_halves[part] * zsum[:, lanes]) * scale_halves[part]
            zed[part, at, :] = side.reshape(tall, LANES)
        return carry

    lax.fori_loop(0, plane_size, z_stage, 0)
    share = ys // groups
    lines_out = share // 2 * xs
    piece = per // 3
    upper_sign = jnp.where(low_half, 1.0, -1.0)

    def one(q, outer):
        p, h = q // 2, lax.rem(q, 2)

        def x_stage(g, carry):
            starts = []
            for s in range(TEMPL // ring_z):
                m = s * (TEMPL // piece) + g
                owner = m // 3
                there = lax.rem(owner, CORES) * RING_X + owner // CORES
                starts.append(there * tall + p * per + lax.rem(m, 3) * piece)

            def column(t):
                lines = [zed[h, pl.ds(at + t, ring_z, stride=BLOCK), :] for at in starts]
                return jnp.concatenate(lines, axis=0)

            for t in range(0, piece, 2):
                value = jnp.concatenate([column(t), column(t + 1)], axis=1)
                folded = stacked_product(table_x[...], value)
                for part in range(2):
                    lanes = slice(part * LANES, part * LANES + LANES)
                    first, second = packed_sides(folded[:, lanes], kxp, low_half)
                    to = pl.multiple_of((g * piece + t + part) * rows, 8)
                    mid[pl.ds(to, kxp), :] = second
                    mid[pl.ds(pl.multiple_of(to + kxp, 8), kxp), :] = first
            return carry

        lax.fori_loop(0, TEMPL // piece, x_stage, 0)

        def y_stage(k, carry):
            lines = [mid[pl.ds(k + s * kxp, TEMPL, stride=rows), :] for s in range(2)]
            folded = stacked_product(table_y[...], jnp.concatenate(lines, axis=1))
            evens, odds = [], []
            for s in range(2):
                lanes = slice(s * LANES, s * LANES + LANES)
                cos, sin = folded[:kyp, lanes], folded[kyp:, lanes]
                cos_turned, sin_turned = pltpu.roll(cos, ZF, 1), pltpu.roll(sin, ZF, 1)
                side = -upper_sign * sin_turned
                side_turned = upper_sign * sin
                found = []
                for u in range(2):
                    value = cos + side if u == 0 else cos - side
                    turned = cos_turned + side_turned if u == 0 else cos_turned - side_turned
                    found.append(
                        value * spectrum[k, s, u, :, :LANES] + turned * spectrum[k, s, u, :, LANES:]
                    )
                evens.append(found[0] + found[1])
                odds.append(-upper_sign * pltpu.roll(found[0] - found[1], ZF, 1))
            stacked = jnp.concatenate(
                [jnp.concatenate(evens, axis=1), jnp.concatenate(odds, axis=1)], axis=0
            )
            result = paired_product(table_yi[...], stacked)
            first, second = result[:, :LANES], result[:, LANES:]
            back[pl.ds(pl.multiple_of(k * ys, 8), ys), :] = first + second
            odd = -upper_sign * pltpu.roll(first - second, ZF, 1)
            back[pl.ds(pl.multiple_of((k + plan.kxc) * ys, 8), ys), :] = odd
            return carry

        lax.fori_loop(0, plan.kxc // 22, unrolled(y_stage, 22), 0)

        def last(i, lane_sum):
            j = lax.rem(2 + 3 * i + 3 * (i * (i - 1) // 2), groups)
            base = lax.rem(rot + j, groups) * share
            lines = []
            for y in range(0, share, 2):
                value = jnp.concatenate(
                    [back[pl.ds(base + y + part, plan.kxi, stride=ys), :] for part in range(2)],
                    axis=1,
                )
                lines.append(rows_product(table_xi[...], value))
            upper, lower = split(jnp.concatenate(lines, axis=0))
            both = mm(upper, table_zi[...])
            value = both[:, :LANES] + both[:, LANES:] + mm(lower, table_zi[:, :LANES])
            ready[q, j] = value

            @pl.when(j > 0)
            def _():
                send_part(q, j).start()

            mark = marks[pl.ds(pl.multiple_of(base // 2 * xs, 8), lines_out), :]
            return lane_sum + tall_sum(value * mark)

        def send_part(q, j):
            return pltpu.make_async_remote_copy(
                src_ref=ready.at[q, j],
                dst_ref=parts.at[q, j],
                send_sem=part_sends.at[q, j],
                recv_sem=part_receives.at[q, j],
                device_id={"rot": lax.rem(rot + j, groups)},
                device_id_type=MESH,
            )

        def sum_all(value):
            return jnp.sum(jnp.sum(value, axis=0, keepdims=True), axis=1, keepdims=True)

        cells = columns * float(plan.zs)
        lane_sum = lax.fori_loop(0, groups, last, jnp.zeros((8, LANES), F32))
        part_mean = sum_all(lane_sum) / jnp.maximum(cells, 1.0)

        def add_off(j, carry):
            base = lax.rem(rot + j, groups) * lines_out
            mark = marks[pl.ds(pl.multiple_of(base, 8), lines_out), :]
            off = ready[q, j] - part_mean
            return carry + tall_sum(off * off * mark)

        part_square = sum_all(lax.fori_loop(0, groups, add_off, jnp.zeros((8, LANES), F32)))
        now = jnp.where(field == q, part_mean, row[...])
        row[...] = jnp.where(field == FIELDS + q, part_square, now)
        return outer

    lax.fori_loop(0, FIELDS, one, 0)
    place = z * CORES + core
    stats[rot, x, place] = row[...]
    mine = stats.at[rot, x, place]
    finish(begin(mine, mine, sends, receives, first_stats, line_peers))
    mine = stats.at[rot, x]
    finish(begin(mine, mine, sends, receives, first_stats + line_size - 1, sheet_peers))
    incoming = [
        remote(ready.at[p, j], parts.at[p, j], part_sends.at[p], part_receives.at[p], j, {"rot": lax.rem(rot + j, groups)})
        for p in range(FIELDS)
        for j in range(1, groups)
    ]

    terms = []
    for j in range(groups):
        group = lax.rem(rot + groups - j, groups)
        lines = stats[group].reshape(-1, LANES)
        count = lines[:, FIELD_COUNT : FIELD_COUNT + 1]
        total = jnp.sum(count, axis=0, keepdims=True)
        average = jnp.sum(count * lines, axis=0, keepdims=True) / total
        off = lines - average
        square = jnp.sum(count * off * off, axis=0, keepdims=True) * plan.zs
        square += pltpu.roll(jnp.sum(lines, axis=0, keepdims=True), LANES - FIELDS, 1)
        inverse = 1.0 / jnp.sqrt(square / (total * plan.zs) + EPSILON)
        for q in range(FIELDS):
            source = ready if j == 0 else parts
            at = FIELD_QUAT + 4 * q
            quat = [lines[:1, at + c : at + c + 1] for c in range(4)]
            terms.append((source.at[q, j], average[:, q : q + 1], inverse[:, q : q + 1], quat))

    finish(incoming)

    def answer(j, carry):
        at = pl.ds(pl.multiple_of(j * xs, 8), xs)
        scores = [(ref[at, :] - average) * inverse for ref, average, inverse, _ in terms]
        high = functools.reduce(jnp.maximum, scores)
        weights = [jnp.exp(score - high) for score in scores]
        total = functools.reduce(jnp.add, weights)
        inside = marks[pl.ds(pl.multiple_of(rot * lines_out + j * xs, 8), xs), :]
        lanes = pl.ds(pl.multiple_of(j * LANES, LANES), LANES)
        best[:, lanes] = inside * high
        evidence[:, lanes] = inside * (high + jnp.log(total))
        ratio = inside / total
        for c in range(4):
            moment = functools.reduce(jnp.add, [w * t[3][c] for w, t in zip(weights, terms)])
            moments[c, :, lanes] = moment * ratio
        return carry

    lax.fori_loop(0, share // 2 // 5, unrolled(answer, 5), 0)


def matched(plan, tiles, groups, own, block, valid, quats, rot_index):
    ring_z = tiles // (CORES * RING_X)
    order = (
        np.arange(TEMPL // ring_z)[:, None] + (TEMPL // ring_z) * np.arange(ring_z)[None]
    ).reshape(-1)
    z_table = plan.tmpl_z()
    tables = [
        row_stack(plan.slab_z()),
        stacked_table(plan.folded(plan.kx, plan.kxp, np.arange(plan.lx), plan.lx)),
        stacked_table(plan.folded(plan.ky, plan.kyp, np.arange(plan.ys), plan.ly)),
        row_stack(z_table),
        stacked_table(plan.folded(plan.kx, plan.kxp, order, plan.lx)),
        stacked_table(plan.folded(plan.ky, plan.kyp, np.arange(TEMPL) - HALF, plan.ly)),
        paired_table(plan.inverse_rows(np.arange(plan.ys), plan.ky, plan.ly, plan.kyp, 2 * plan.kyp)),
        row_tables(plan.inverse_rows(np.arange(plan.xs), plan.kx, plan.lx, plan.kxc, plan.kxi)),
        col_tables(plan.inverse_z()),
    ]
    spots, first = [], 0
    for table in tables:
        spots.append((first, table.shape[0], table.shape[1]))
        first += table.shape[0]
    tables = [
        np.concatenate([padded_cols(table, 2 * LANES) for table in tables], axis=0),
        z_table.sum(axis=0, keepdims=True).astype(np.float32),
        np.kron(np.eye(2), np.ones((ZF, ZF))).astype(np.float32),
    ]
    share = plan.ys // groups * plan.xs
    copies = 2 * HALO_PARTS + ring_z + 2 * RING_X - 2 + ring_z * CORES + RING_X * groups - 2
    vmem = pl.BlockSpec(memory_space=pltpu.VMEM)
    flat_out = jax.ShapeDtypeStruct((plan.xs, plan.ys // groups * plan.zs), F32)
    return pl.pallas_call(
        functools.partial(match_kernel, plan, tiles, groups, spots),
        out_shape=[flat_out, flat_out, jax.ShapeDtypeStruct((4,) + flat_out.shape, F32)],
        in_specs=[vmem] * 4
        + [pl.BlockSpec(memory_space=pltpu.SMEM)]
        + [vmem] * len(tables),
        out_specs=[vmem] * 3,
        scratch_shapes=[
            pltpu.VMEM((FIELDS, groups, share // 2, LANES), F32),
            pltpu.VMEM((groups, RING_X, ring_z * CORES, 1, LANES), F32),
            pltpu.VMEM(own.shape, BF16),
            pltpu.VMEM(own.shape, BF16),
            pltpu.VMEM((CORES, RING_X, ring_z) + block.shape, BF16),
            pltpu.VMEM((plan.kxc, 2, 2, plan.kyp, 2 * LANES), F32),
            pltpu.VMEM((plan.ys * 2 * plan.kxp, LANES), F32),
            pltpu.VMEM((2, tiles * BLOCK, LANES), F32),
            pltpu.VMEM((TEMPL * 2 * plan.kxp, LANES), F32),
            pltpu.VMEM((plan.kxi * plan.ys, LANES), F32),
            pltpu.VMEM((plan.ys // 2 * plan.xs, LANES), F32),
            pltpu.VMEM((FIELDS, groups, share // 2, LANES), F32),
            pltpu.VMEM((1, LANES), F32),
            pltpu.SemaphoreType.DMA((copies,)),
            pltpu.SemaphoreType.DMA((copies,)),
            pltpu.SemaphoreType.DMA((FIELDS, groups)),
            pltpu.SemaphoreType.DMA((FIELDS, groups)),
        ],
        compiler_params=pltpu.CompilerParams(
            collective_id=0, has_side_effects=True, vmem_limit_bytes=48 << 20
        ),
        name="match",
    )(own, block, valid, quats, rot_index, *tables)


def row_stack(table):
    return np.concatenate(halves(table), axis=0)


def local(tomogram, templates, valid, quats, rot_index):
    xs, voxels = tomogram.shape
    ys = valid.shape[1]
    zs = voxels // ys
    plan = Plan(xs, ys, zs)
    tiles, groups = lax.axis_size("tile"), lax.axis_size("rot")
    per = templates.shape[1] // TEMPL
    block = templates.reshape(2, 2, per, TEMPL).transpose(0, 2, 1, 3)
    block = jnp.pad(block, ((0, 0), (0, 0), (0, 0), (0, ZF - TEMPL))).reshape(2 * per, LANES)
    block = jnp.pad(block, ((0, BLOCK - 2 * per), (0, 0)))
    return tuple(matched(plan, tiles, groups, tomogram, block, valid, quats, rot_index))


def solution(mesh):
    placed = (P("tile", None), P("rot", "tile"), P("tile", None), P(), P("rot"))
    return jax.shard_map(
        local,
        mesh=mesh,
        in_specs=placed,
        out_specs=(P("tile", "rot"), P("tile", "rot"), P(None, "tile", "rot")),
        check_vma=False,
    )
```

```python
import functools
import math

import jax
import jax.numpy as jnp
import ml_dtypes
import numpy as np
from jax import lax
from jax.experimental import pallas as pl
from jax.experimental.pallas import tpu as pltpu
from jax.sharding import PartitionSpec as P

TEMPL = 48
HALF = 24
EPSILON = 1e-06
LANES = 128
ZF = 64
CORES = 2
RING_X = 4
BLOCK = 80
HALO_PARTS = 4
MESH = pl.DeviceIdType.MESH
FIELD_COUNT = 4
FIELD_QUAT = 5
F32 = jnp.float32
BF16 = jnp.bfloat16


def halves(table):
    high = table.astype(np.float32).astype(ml_dtypes.bfloat16)
    low = (table - high.astype(np.float64)).astype(np.float32).astype(ml_dtypes.bfloat16)
    return high, low


def row_tables(table):
    high, low = halves(table)
    return np.concatenate([high, low], axis=0)


def col_tables(table):
    high, low = halves(table)
    return np.concatenate([high, low], axis=1)


def phases(rows, cols, length):
    index = np.outer(np.asarray(rows), np.asarray(cols)) % length
    return index * (2.0 * np.pi / length)


def padded_rows(table, rows):
    return np.pad(table, ((0, rows - table.shape[0]), (0, 0)))


def padded_cols(table, cols):
    return np.pad(table, ((0, 0), (0, cols - table.shape[1])))


def up8(n):
    return -(-n // 8) * 8


class Plan:
    def __init__(self, xs, ys, zs):
        self.xs, self.ys, self.zs = xs, ys, zs
        self.lx, self.ly, self.lz = xs + TEMPL, ys + HALF, zs + HALF
        self.kx, self.ky, self.kz = self.lx // 2 + 1, self.ly // 2 + 1, self.lz // 2 + 1
        self.kxp, self.kyp = up8(self.kx), up8(self.ky)
        self.kxu = -(-self.kx // 2) * 2
        self.kxc = -(-self.kx // 4) * 4
        self.kxi = 2 * self.kxc

    def folded(self, count, pad, points, length):
        angle = phases(np.arange(count), points, length)
        return np.concatenate(
            [padded_rows(np.cos(angle), pad), padded_rows(np.sin(angle), pad)], axis=0
        )

    def slab_z(self):
        angle = phases(np.arange(self.zs), np.arange(self.kz), self.lz)
        cos = padded_cols(np.cos(angle), ZF)
        sin = padded_cols(-np.sin(angle), ZF)
        one = np.concatenate([cos, sin], axis=1)
        return np.kron(np.eye(2), one)

    def tmpl_z(self):
        angle = phases(np.arange(TEMPL) - HALF, np.arange(self.kz), self.lz)
        cos = np.zeros((ZF, ZF))
        sin = np.zeros((ZF, ZF))
        cos[:TEMPL, : self.kz] = np.cos(angle)
        sin[:TEMPL, : self.kz] = np.sin(angle)
        none = np.zeros_like(cos)
        return np.block([[cos, none, sin, none], [none, cos, none, sin]])

    def inverse_rows(self, points, count, length, k_pad, tail):
        angle = phases(points, np.arange(count), length)
        weight = np.full((1, count), 1.0 / length)
        weight[0, 0] *= 0.5
        weight[0, count - 1] *= 0.5
        cos = padded_cols(np.cos(angle) * weight, k_pad)
        sin = padded_cols(np.sin(angle) * weight, k_pad)
        return padded_cols(np.concatenate([cos, sin], axis=1), tail)

    def inverse_z(self):
        angle = phases(np.arange(self.kz), np.arange(self.zs), self.lz)
        weight = np.full((self.kz, 1), 2.0 / self.lz)
        weight[0] *= 0.5
        weight[self.kz - 1] *= 0.5
        cos = padded_rows(np.cos(angle) * weight, ZF)
        sin = padded_rows(-np.sin(angle) * weight, ZF)
        none = np.zeros_like(cos)
        return np.block([[cos, none], [none, cos], [sin, none], [none, sin]])


def unrolled(body, count):
    def many(i, carry):
        return lax.fori_loop(0, count, lambda part, c: body(i * count + part, c), carry, unroll=True)

    return many


def split(value):
    high = value.astype(BF16)
    return high, (value - high.astype(F32)).astype(BF16)


def mm(left, right):
    return jnp.dot(left, right, preferred_element_type=F32)


def rows_product(table, value):
    count = table.shape[0] // 2
    high, low = split(value)
    both = mm(table, high)
    return both[:count] + both[count:] + mm(table[:count], low)


def stacked_table(table):
    high, low = halves(table)
    return np.concatenate([high, high, low], axis=1)


def stacked_product(table, value):
    high, low = split(value)
    return mm(table, jnp.concatenate([high, low, high], axis=0))


def paired_table(table):
    high, low = halves(table)
    return np.block([[high, high], [low, np.zeros_like(low)]])


def paired_product(table, value):
    high, low = split(value)
    count = table.shape[0] // 2
    both = mm(table, jnp.concatenate([high, low], axis=0))
    return both[:count] + both[count:]


def plus_minus(folded, count, sign):
    cos_re, cos_im = folded[:count, :LANES], folded[:count, LANES:]
    sin_re, sin_im = folded[count:, :LANES], folded[count:, LANES:]
    first = (cos_re - sin_im, cos_im + sin_re)
    second = (cos_re + sin_im, cos_im - sin_re)
    return (first, second) if sign > 0 else (second, first)


def exact(left, right):
    return jnp.dot(left, right, precision=lax.Precision.HIGHEST, preferred_element_type=F32)


def tall_sum(value):
    return jnp.sum(value.reshape(-1, 8, value.shape[-1]), axis=0)


def tile_of(z, x, core):
    return (z * RING_X + x) * CORES + core


def greet(peers):
    barrier = pltpu.get_barrier_semaphore()
    for peer in peers:
        pl.semaphore_signal(barrier, inc=1, device_id=peer, device_id_type=MESH)
    pl.semaphore_wait(barrier, len(peers))


def remote(source, target, sends, receives, index, peer):
    return pltpu.make_async_remote_copy(
        src_ref=source,
        dst_ref=target,
        send_sem=sends.at[index],
        recv_sem=receives.at[index],
        device_id=peer,
        device_id_type=MESH,
    )


def begin(source, target, sends, receives, first, peers):
    copies = [
        remote(source, target, sends, receives, first + index, peer)
        for index, peer in enumerate(peers)
    ]
    for copy in copies:
        copy.start()
    return copies


def finish(copies):
    for copy in copies:
        copy.wait()


def packed_sides(folded, count, low_half):
    cos, sin = folded[:count], folded[count:]
    swapped = pltpu.roll(sin, ZF, 1)
    turned = jnp.where(low_half, swapped, -swapped)
    return cos + turned, cos - turned


def match_kernel(
    plan, tiles, groups, spots, own, block, valid, quats, rot_index, packed, zsum, ones, best, evidence, moments, parts,
    stats, low, high, bank, spectrum, slab_mid, zed, mid, back, marks, ready, row, sends,
    receives, part_sends, part_receives,
):
    slab_z, slab_x, slab_y, table_z, table_x, table_y, table_yi, table_xi, table_zi = [
        packed.at[first : first + tall, :wide] for first, tall, wide in spots
    ]
    ring_z = tiles // (CORES * RING_X)
    plane_size = RING_X * CORES
    kxp, kyp, ys, xs = plan.kxp, plan.kyp, plan.ys, plan.xs
    rows = 2 * kxp
    tile, rot = lax.axis_index("tile"), lax.axis_index("rot")
    core = lax.rem(tile, CORES)
    x = lax.rem(tile // CORES, RING_X)
    z = tile // (CORES * RING_X)
    z_peers = [{"tile": tile_of(lax.rem(z + d, ring_z), x, core)} for d in range(1, ring_z)]
    x_peers = [{"tile": tile_of(z, lax.rem(x + d, RING_X), core)} for d in range(1, RING_X)]
    other = {"tile": tile_of(z, x, 1 - core)}
    line_size, sheet_size = ring_z * CORES, RING_X * groups
    line_peers, sheet_peers = [], []
    for d in range(1, line_size):
        there = lax.rem(z * CORES + core + d, line_size)
        line_peers.append({"tile": tile_of(there // CORES, x, lax.rem(there, CORES))})
    for d in range(1, sheet_size):
        there = lax.rem(x * groups + rot + d, sheet_size)
        sheet_peers.append(
            {"tile": tile_of(z, there // groups, core), "rot": lax.rem(there, groups)}
        )
    after = {"tile": lax.rem(tile + 1, tiles)}
    before = {"tile": lax.rem(tile + tiles - 1, tiles)}
    low_half = lax.broadcasted_iota(jnp.int32, (1, LANES), 1) < ZF
    width = ys * plan.zs // HALO_PARTS
    first_halo, first_z = 0, 2 * HALO_PARTS
    first_x = first_z + ring_z - 1
    first_pass = first_x + RING_X
    first_stats = first_pass + RING_X - 1

    for k in range(plan.kxu, plan.kxc):
        for side in range(2):
            first = (k + side * plan.kxc) * ys
            back[:, first : first + ys, :] = jnp.zeros((2, ys, LANES), F32)
    greet([after, before] + line_peers + sheet_peers)

    def halo(q):
        lanes = pl.ds(pl.multiple_of(q * width, LANES), width)
        return [
            remote(own.at[:, lanes], low.at[:, lanes], sends, receives, first_halo + 2 * q, after),
            remote(own.at[:, lanes], high.at[:, lanes], sends, receives, first_halo + 2 * q + 1, before),
        ]

    for q in range(HALO_PARTS):
        for copy in halo(q):
            copy.start()
    bank[core, x, z] = block[...]
    mine = bank.at[core, x, z]
    copies = begin(mine, mine, sends, receives, first_z, z_peers)

    flags = valid[...].astype(F32)
    columns = jnp.sum(flags)
    for y in range(ys):
        marks[y * xs : y * xs + xs, :] = jnp.broadcast_to(flags[:, y : y + 1], (xs, LANES))
    field = lax.rem(lax.broadcasted_iota(jnp.int32, (1, LANES), 1), ZF)
    line = jnp.where(field == FIELD_COUNT, columns, 0.0)
    entry = lax.broadcasted_iota(jnp.int32, quats.shape, 1)
    for r in range(4):
        found = jnp.sum(jnp.where(entry == rot_index[r], quats[...], 0.0), axis=1, keepdims=True)
        half = low_half if r % 2 == 0 else jnp.logical_not(low_half)
        for c in range(4):
            here = jnp.logical_and(field == FIELD_QUAT + 4 * (r // 2) + c, half)
            line = jnp.where(here, found[c : c + 1], line)
    row[...] = line

    several = 5

    def slab_first(first):
        blocks = []
        for t in range(several):
            lanes = pl.ds(pl.multiple_of((first + t) * LANES, LANES), LANES)
            blocks += [
                jnp.where(tile > 0, low[:, lanes].astype(F32)[xs - HALF :], 0.0),
                own[:, lanes].astype(F32),
                jnp.where(tile < tiles - 1, high[:, lanes].astype(F32)[:HALF], 0.0),
            ]
        block = jnp.concatenate(blocks, axis=0).astype(BF16)
        strips = mm(jnp.concatenate([block, block], axis=1), slab_z[...])
        for t in range(several):
            folded = stacked_product(slab_x[...], strips[t * plan.lx : t * plan.lx + plan.lx])
            for part in range(2):
                sides = packed_sides(folded[:, part * LANES : part * LANES + LANES], kxp, low_half)
                to = pl.multiple_of((2 * (first + t) + part) * rows, 8)
                for s in range(2):
                    slab_mid[pl.ds(pl.multiple_of(to + s * kxp, 8), kxp), :] = sides[s]

    pieces = ys // 2 // HALO_PARTS

    def slab_part(q, carry):
        for copy in halo(q):
            copy.wait()

        def body(i, inner):
            slab_first(q * pieces + i * several)
            return inner

        return lax.fori_loop(0, pieces // several, body, carry)

    lax.fori_loop(0, HALO_PARTS // 2, slab_part, 0)
    finish(copies)
    mine = bank.at[core, x]
    copies = begin(mine, mine, sends, receives, first_x, x_peers + [other])
    lax.fori_loop(HALO_PARTS // 2, HALO_PARTS, slab_part, 0)

    def slab_second(k, carry):
        lines = [slab_mid[pl.ds(k + s * kxp, ys, stride=rows), :] for s in range(2)]
        folded = stacked_product(slab_y[...], jnp.concatenate(lines, axis=1))
        for s in range(2):
            lanes = slice(s * LANES, s * LANES + LANES)
            cos, sin = folded[:kyp, lanes], folded[kyp:, lanes]
            cos_turned, sin_turned = pltpu.roll(cos, ZF, 1), pltpu.roll(sin, ZF, 1)
            for u in range(2):
                re_low, im_high = cos + sin_turned, cos - sin_turned
                im_low, re_high = cos_turned - sin, cos_turned + sin
                if u == 1:
                    re_low, im_high = im_high, re_low
                    im_low, re_high = re_high, im_low
                spectrum[k, s, u, :, :LANES] = jnp.where(low_half, re_low, re_high)
                spectrum[k, s, u, :, LANES:] = jnp.where(low_half, im_low, im_high)
        return carry

    trips = plan.kxu // 21
    lax.fori_loop(0, trips // 2, unrolled(slab_second, 21), 0)
    forwards = []
    for d in range(1, RING_X):
        copies[d - 1].wait()
        mine = bank.at[core, lax.rem(x + RING_X - d, RING_X)]
        forward = remote(mine, mine, sends, receives, first_pass + d - 1, other)
        forward.start()
        forwards.append(forward)
    lax.fori_loop(trips // 2, trips, unrolled(slab_second, 21), 0)
    copies[-1].wait()
    finish(forwards)

    per = TEMPL * TEMPL // tiles
    total = float(TEMPL**3)
    lane = lax.broadcasted_iota(jnp.int32, (BLOCK, LANES), 1)
    place = lax.broadcasted_iota(jnp.int32, (BLOCK, LANES), 0)
    used = jnp.logical_and(lax.rem(lane, ZF) < TEMPL, place < 2 * per)[None]
    tall = ring_z * BLOCK

    def lane_groups(value):
        wide = jnp.broadcast_to(jnp.sum(value, axis=0, keepdims=True), (8, LANES))
        return exact(wide, ones[...])[:1]

    def both_pairs(value):
        first = lane_groups(jnp.where(place < per, value, 0.0))
        second = lane_groups(jnp.where(place < per, 0.0, value))
        return first, second

    def bank_rows(i):
        return bank[i // RING_X, lax.rem(i, RING_X)]

    def add_up(i, carry):
        return carry + jnp.sum(bank_rows(i).astype(F32), axis=0)

    empty = jnp.zeros((BLOCK, LANES), F32)
    means = both_pairs(lax.fori_loop(0, plane_size, add_up, empty))
    means = [mean / total for mean in means]
    mean_rows = jnp.where(place < per, means[0], means[1])[None]

    def add_squares(i, carry):
        off = jnp.where(used, bank_rows(i).astype(F32) - mean_rows, 0.0)
        return carry + jnp.sum(off * off, axis=0)

    squares = both_pairs(lax.fori_loop(0, plane_size, add_squares, empty))
    factors = [
        1.0 / (jnp.sqrt(square / total + EPSILON) * float(TEMPL) ** 1.5) for square in squares
    ]
    scale_rows = jnp.where(place < per, factors[0], factors[1])[None]

    def z_stage(i, carry):
        lines = bank_rows(i).reshape(tall, LANES)
        value = mm(jnp.concatenate([lines, lines], axis=1), table_z[...])
        at = pl.ds(pl.multiple_of(i * tall, tall), tall)
        for part in range(2):
            lanes = slice(part * LANES, part * LANES + LANES)
            side = value[:, lanes].reshape(ring_z, BLOCK, LANES)
            side = (side - mean_rows * zsum[:, lanes]) * scale_rows
            zed[part, at, :] = side.reshape(tall, LANES)
        return carry

    lax.fori_loop(0, plane_size, z_stage, 0)
    share = ys // groups
    step = share
    piece = per // 3

    def pair(p, outer):
        def x_stage(g, carry):
            starts = []
            for s in range(TEMPL // ring_z):
                m = s * (TEMPL // piece) + g
                owner = m // 3
                there = lax.rem(owner, CORES) * RING_X + owner // CORES
                starts.append(there * tall + p * per + lax.rem(m, 3) * piece)
            for t in range(piece):
                lines = []
                for start in starts:
                    at = pl.ds(start + t, ring_z, stride=BLOCK)
                    lines.append(jnp.concatenate([zed[0, at, :], zed[1, at, :]], axis=1))
                folded = stacked_product(table_x[...], jnp.concatenate(lines, axis=0))
                to = pl.multiple_of((g * piece + t) * rows, 8)
                for s, (re, im) in enumerate(plus_minus(folded, kxp, 1)):
                    at = pl.ds(pl.multiple_of(to + s * kxp, 8), kxp)
                    mid[0, at, :] = re
                    mid[1, at, :] = im
            return carry

        lax.fori_loop(0, TEMPL // piece, x_stage, 0)

        def y_stage(k, carry):
            found = []
            for s in range(2):
                at = pl.ds(k + s * kxp, TEMPL, stride=rows)
                value = jnp.concatenate([mid[0, at, :], mid[1, at, :]], axis=1)
                folded = stacked_product(table_y[...], value)
                sides = []
                for u, (re, im) in enumerate(plus_minus(folded, kyp, 1)):
                    slab_re = spectrum[k, s, u, :, :LANES]
                    slab_im = spectrum[k, s, u, :, LANES:]
                    sides.append((re * slab_re - im * slab_im, re * slab_im + im * slab_re))
                (re_p, im_p), (re_m, im_m) = sides
                even = jnp.concatenate([re_p + re_m, im_p + im_m], axis=1)
                odd = jnp.concatenate([im_m - im_p, re_p - re_m], axis=1)
                found.append(paired_product(table_yi[...], jnp.concatenate([even, odd], axis=0)))
            even = found[0] + found[1]
            odd = found[0] - found[1]
            to = pl.ds(pl.multiple_of(k * ys, 8), ys)
            back[0, to, :] = even[:, :LANES]
            back[1, to, :] = even[:, LANES:]
            to = pl.ds(pl.multiple_of((k + plan.kxc) * ys, 8), ys)
            back[0, to, :] = -odd[:, LANES:]
            back[1, to, :] = odd[:, :LANES]
            return carry

        lax.fori_loop(0, plan.kxu // 14, unrolled(y_stage, 14), 0)

        def last(i, lane_sum):
            j = lax.rem(2 + 3 * i + 3 * (i * (i - 1) // 2), groups)
            base = lax.rem(rot + j, groups) * share
            lines = []
            for y in range(step):
                at = pl.ds(base + y, plan.kxi, stride=ys)
                value = jnp.concatenate([back[0, at, :], back[1, at, :]], axis=1)
                lines.append(rows_product(table_xi[...], value))
            upper, lower = split(jnp.concatenate(lines, axis=0))
            both = mm(upper, table_zi[...])
            value = both[:, :LANES] + both[:, LANES:] + mm(lower, table_zi[:, :LANES])
            ready[p, j] = value

            @pl.when(j > 0)
            def _():
                send_part(p, j).start()

            mark = marks[pl.ds(pl.multiple_of(base * xs, 8), share * xs), :]
            return lane_sum + tall_sum(value * mark)

        def send_part(p, j):
            return pltpu.make_async_remote_copy(
                src_ref=ready.at[p, j],
                dst_ref=parts.at[p, j],
                send_sem=part_sends.at[p, j],
                recv_sem=part_receives.at[p, j],
                device_id={"rot": lax.rem(rot + j, groups)},
                device_id_type=MESH,
            )

        lane_sum = lax.fori_loop(0, groups, last, jnp.zeros((8, LANES), F32))
        lane_mean = jnp.sum(lane_sum, axis=0, keepdims=True) / jnp.maximum(columns, 1.0)

        def add_off(j, carry):
            base = lax.rem(rot + j, groups) * (share * xs)
            mark = marks[pl.ds(pl.multiple_of(base, 8), share * xs), :]
            off = ready[p, j] - lane_mean
            return carry + tall_sum(off * off * mark)

        lane_square = lax.fori_loop(0, groups, add_off, jnp.zeros((8, LANES), F32))
        wide = jnp.broadcast_to(lane_mean, (8, LANES))
        part_mean = exact(wide, ones[...])[:1] / float(plan.zs)
        off = lane_mean - part_mean
        lane_square = jnp.sum(lane_square, axis=0, keepdims=True) + columns * off * off
        part_square = exact(jnp.broadcast_to(lane_square, (8, LANES)), ones[...])[:1]
        now = jnp.where(field == 2 * p, part_mean, row[...])
        row[...] = jnp.where(field == 2 * p + 1, part_square, now)
        return outer

    lax.fori_loop(0, 2, pair, 0)
    place = z * CORES + core
    stats[rot, x, place] = row[...]
    mine = stats.at[rot, x, place]
    finish(begin(mine, mine, sends, receives, first_stats, line_peers))
    mine = stats.at[rot, x]
    finish(begin(mine, mine, sends, receives, first_stats + line_size - 1, sheet_peers))
    incoming = [
        remote(ready.at[p, j], parts.at[p, j], part_sends.at[p], part_receives.at[p], j, {"rot": lax.rem(rot + j, groups)})
        for p in range(2)
        for j in range(1, groups)
    ]

    def spread_field(lines, index):
        return jnp.where(
            low_half, lines[:, index : index + 1], lines[:, ZF + index : ZF + index + 1]
        )

    terms = []
    for j in range(groups):
        group = lax.rem(rot + groups - j, groups)
        lines = stats[group].reshape(-1, LANES)
        count = lines[:, FIELD_COUNT : FIELD_COUNT + 1]
        total = jnp.sum(count, axis=0, keepdims=True)
        average = jnp.sum(count * lines, axis=0, keepdims=True) / total
        off = lines - average
        square = jnp.sum(count * off * off, axis=0, keepdims=True) * plan.zs
        square += pltpu.roll(jnp.sum(lines, axis=0, keepdims=True), LANES - 1, 1)
        inverse = 1.0 / jnp.sqrt(square / (total * plan.zs) + EPSILON)
        for p in range(2):
            source = ready if j == 0 else parts
            quat = [spread_field(lines[:1], FIELD_QUAT + 4 * p + c) for c in range(4)]
            terms.append(
                (source.at[p, j], spread_field(average, 2 * p), spread_field(inverse, 2 * p), quat)
            )

    finish(incoming)

    def column(y):
        at = pl.ds(pl.multiple_of(y * xs, 8), xs)
        scores = [(ref[at, :] - average) * inverse for ref, average, inverse, _ in terms]
        high = functools.reduce(jnp.maximum, scores)
        high = jnp.maximum(high, pltpu.roll(high, ZF, 1))
        weights = [jnp.exp(score - high) for score in scores]
        sums = [functools.reduce(jnp.add, weights)]
        for c in range(4):
            sums.append(functools.reduce(jnp.add, [w * t[3][c] for w, t in zip(weights, terms)]))
        return [high] + [value + pltpu.roll(value, ZF, 1) for value in sums]

    def answer(j, carry):
        both = [jnp.where(low_half, a, b) for a, b in zip(column(2 * j), column(2 * j + 1))]
        base = pl.multiple_of(rot * (share * xs) + 2 * j * xs, 8)
        inside = jnp.where(
            low_half, marks[pl.ds(base, xs), :], marks[pl.ds(pl.multiple_of(base + xs, 8), xs), :]
        )
        high, total = both[0], both[1]
        lanes = pl.ds(pl.multiple_of(j * LANES, LANES), LANES)
        best[:, lanes] = inside * high
        evidence[:, lanes] = inside * (high + jnp.log(total))
        ratio = inside / total
        for c in range(4):
            moments[c, :, lanes] = both[2 + c] * ratio
        return carry

    lax.fori_loop(0, share // 2 // 5, unrolled(answer, 5), 0)


def matched(plan, tiles, groups, own, block, valid, quats, rot_index):
    ring_z = tiles // (CORES * RING_X)
    order = (
        np.arange(TEMPL // ring_z)[:, None] + (TEMPL // ring_z) * np.arange(ring_z)[None]
    ).reshape(-1)
    z_table = plan.tmpl_z()
    tables = [
        row_stack(plan.slab_z()),
        stacked_table(plan.folded(plan.kx, plan.kxp, np.arange(plan.lx), plan.lx)),
        stacked_table(plan.folded(plan.ky, plan.kyp, np.arange(plan.ys), plan.ly)),
        row_stack(z_table),
        stacked_table(plan.folded(plan.kx, plan.kxp, order, plan.lx)),
        stacked_table(plan.folded(plan.ky, plan.kyp, np.arange(TEMPL) - HALF, plan.ly)),
        paired_table(plan.inverse_rows(np.arange(plan.ys), plan.ky, plan.ly, plan.kyp, 2 * plan.kyp)),
        row_tables(plan.inverse_rows(np.arange(plan.xs), plan.kx, plan.lx, plan.kxc, plan.kxi)),
        col_tables(plan.inverse_z()),
    ]
    spots, first = [], 0
    for table in tables:
        spots.append((first, table.shape[0], table.shape[1]))
        first += table.shape[0]
    tables = [
        np.concatenate([padded_cols(table, 2 * LANES) for table in tables], axis=0),
        z_table.sum(axis=0, keepdims=True).astype(np.float32),
        np.kron(np.eye(2), np.ones((ZF, ZF))).astype(np.float32),
    ]
    share = plan.ys // groups * plan.xs
    copies = 2 * HALO_PARTS + ring_z + 2 * RING_X - 2 + ring_z * CORES + RING_X * groups - 2
    vmem = pl.BlockSpec(memory_space=pltpu.VMEM)
    flat_out = jax.ShapeDtypeStruct((plan.xs, plan.ys // groups * plan.zs), F32)
    return pl.pallas_call(
        functools.partial(match_kernel, plan, tiles, groups, spots),
        out_shape=[flat_out, flat_out, jax.ShapeDtypeStruct((4,) + flat_out.shape, F32)],
        in_specs=[vmem] * 4
        + [pl.BlockSpec(memory_space=pltpu.SMEM)]
        + [vmem] * len(tables),
        out_specs=[vmem] * 3,
        scratch_shapes=[
            pltpu.VMEM((2, groups, share, LANES), F32),
            pltpu.VMEM((groups, RING_X, ring_z * CORES, 1, LANES), F32),
            pltpu.VMEM(own.shape, BF16),
            pltpu.VMEM(own.shape, BF16),
            pltpu.VMEM((CORES, RING_X, ring_z) + block.shape, BF16),
            pltpu.VMEM((plan.kxc, 2, 2, plan.kyp, 2 * LANES), F32),
            pltpu.VMEM((plan.ys * 2 * plan.kxp, LANES), F32),
            pltpu.VMEM((2, tiles * BLOCK, LANES), F32),
            pltpu.VMEM((2, TEMPL * 2 * plan.kxp, LANES), F32),
            pltpu.VMEM((2, plan.kxi * plan.ys, LANES), F32),
            pltpu.VMEM((plan.ys * plan.xs, LANES), F32),
            pltpu.VMEM((2, groups, share, LANES), F32),
            pltpu.VMEM((1, LANES), F32),
            pltpu.SemaphoreType.DMA((copies,)),
            pltpu.SemaphoreType.DMA((copies,)),
            pltpu.SemaphoreType.DMA((2, groups)),
            pltpu.SemaphoreType.DMA((2, groups)),
        ],
        compiler_params=pltpu.CompilerParams(
            collective_id=0, has_side_effects=True, vmem_limit_bytes=48 << 20
        ),
        name="match",
    )(own, block, valid, quats, rot_index, *tables)


def row_stack(table):
    return np.concatenate(halves(table), axis=0)


def local(tomogram, templates, valid, quats, rot_index):
    xs, voxels = tomogram.shape
    ys = valid.shape[1]
    zs = voxels // ys
    plan = Plan(xs, ys, zs)
    tiles, groups = lax.axis_size("tile"), lax.axis_size("rot")
    per = templates.shape[1] // TEMPL
    block = templates.reshape(2, 2, per, TEMPL).transpose(0, 2, 1, 3)
    block = jnp.pad(block, ((0, 0), (0, 0), (0, 0), (0, ZF - TEMPL))).reshape(2 * per, LANES)
    block = jnp.pad(block, ((0, BLOCK - 2 * per), (0, 0)))
    return tuple(matched(plan, tiles, groups, tomogram, block, valid, quats, rot_index))


def solution(mesh):
    placed = (P("tile", None), P("rot", "tile"), P("tile", None), P(), P("rot"))
    return jax.shard_map(
        local,
        mesh=mesh,
        in_specs=placed,
        out_specs=(P("tile", "rot"), P("tile", "rot"), P(None, "tile", "rot")),
        check_vma=False,
    )
```

```python
import functools
import math

import jax
import jax.numpy as jnp
import ml_dtypes
import numpy as np
from jax import lax
from jax.experimental import pallas as pl
from jax.experimental.pallas import tpu as pltpu
from jax.sharding import PartitionSpec as P

TEMPL = 48
HALF = 24
EPSILON = 1e-06
LANES = 128
ZF = 64
CORES = 2
RING_X = 4
BLOCK = 80
HALO_PARTS = 4
MESH = pl.DeviceIdType.MESH
FIELD_COUNT = 4
FIELD_QUAT = 5
F32 = jnp.float32
BF16 = jnp.bfloat16


def halves(table):
    high = table.astype(np.float32).astype(ml_dtypes.bfloat16)
    low = (table - high.astype(np.float64)).astype(np.float32).astype(ml_dtypes.bfloat16)
    return high, low


def row_tables(table):
    high, low = halves(table)
    return np.concatenate([high, low], axis=0)


def col_tables(table):
    high, low = halves(table)
    return np.concatenate([high, low], axis=1)


def phases(rows, cols, length):
    index = np.outer(np.asarray(rows), np.asarray(cols)) % length
    return index * (2.0 * np.pi / length)


def padded_rows(table, rows):
    return np.pad(table, ((0, rows - table.shape[0]), (0, 0)))


def padded_cols(table, cols):
    return np.pad(table, ((0, 0), (0, cols - table.shape[1])))


def up8(n):
    return -(-n // 8) * 8


class Plan:
    def __init__(self, xs, ys, zs):
        self.xs, self.ys, self.zs = xs, ys, zs
        self.lx, self.ly, self.lz = xs + TEMPL, ys + HALF, zs + HALF
        self.kx, self.ky, self.kz = self.lx // 2 + 1, self.ly // 2 + 1, self.lz // 2 + 1
        self.kxp, self.kyp = up8(self.kx), up8(self.ky)
        self.kxu = -(-self.kx // 2) * 2
        self.kxc = -(-self.kx // 4) * 4
        self.kxi = 2 * self.kxc

    def folded(self, count, pad, points, length):
        angle = phases(np.arange(count), points, length)
        return np.concatenate(
            [padded_rows(np.cos(angle), pad), padded_rows(np.sin(angle), pad)], axis=0
        )

    def slab_z(self):
        angle = phases(np.arange(self.zs), np.arange(self.kz), self.lz)
        cos = padded_cols(np.cos(angle), ZF)
        sin = padded_cols(-np.sin(angle), ZF)
        one = np.concatenate([cos, sin], axis=1)
        return np.kron(np.eye(2), one)

    def tmpl_z(self):
        angle = phases(np.arange(TEMPL) - HALF, np.arange(self.kz), self.lz)
        cos = np.zeros((ZF, ZF))
        sin = np.zeros((ZF, ZF))
        cos[:TEMPL, : self.kz] = np.cos(angle)
        sin[:TEMPL, : self.kz] = np.sin(angle)
        none = np.zeros_like(cos)
        return np.block([[cos, none, sin, none], [none, cos, none, sin]])

    def inverse_rows(self, points, count, length, k_pad, tail):
        angle = phases(points, np.arange(count), length)
        weight = np.full((1, count), 1.0 / length)
        weight[0, 0] *= 0.5
        weight[0, count - 1] *= 0.5
        cos = padded_cols(np.cos(angle) * weight, k_pad)
        sin = padded_cols(np.sin(angle) * weight, k_pad)
        return padded_cols(np.concatenate([cos, sin], axis=1), tail)

    def inverse_z(self):
        angle = phases(np.arange(self.kz), np.arange(self.zs), self.lz)
        weight = np.full((self.kz, 1), 2.0 / self.lz)
        weight[0] *= 0.5
        weight[self.kz - 1] *= 0.5
        cos = padded_rows(np.cos(angle) * weight, ZF)
        sin = padded_rows(-np.sin(angle) * weight, ZF)
        none = np.zeros_like(cos)
        return np.block([[cos, none], [none, cos], [sin, none], [none, sin]])


def unrolled(body, count):
    def many(i, carry):
        return lax.fori_loop(0, count, lambda part, c: body(i * count + part, c), carry, unroll=True)

    return many


def split(value):
    high = value.astype(BF16)
    return high, (value - high.astype(F32)).astype(BF16)


def mm(left, right):
    return jnp.dot(left, right, preferred_element_type=F32)


def rows_product(table, value):
    count = table.shape[0] // 2
    high, low = split(value)
    both = mm(table, high)
    return both[:count] + both[count:] + mm(table[:count], low)


def stacked_table(table):
    high, low = halves(table)
    return np.concatenate([high, high, low], axis=1)


def stacked_product(table, value):
    high, low = split(value)
    return mm(table, jnp.concatenate([high, low, high], axis=0))


def paired_table(table):
    high, low = halves(table)
    return np.block([[high, high], [low, np.zeros_like(low)]])


def paired_product(table, value):
    high, low = split(value)
    count = table.shape[0] // 2
    both = mm(table, jnp.concatenate([high, low], axis=0))
    return both[:count] + both[count:]


def plus_minus(folded, count, sign):
    cos_re, cos_im = folded[:count, :LANES], folded[:count, LANES:]
    sin_re, sin_im = folded[count:, :LANES], folded[count:, LANES:]
    first = (cos_re - sin_im, cos_im + sin_re)
    second = (cos_re + sin_im, cos_im - sin_re)
    return (first, second) if sign > 0 else (second, first)


def exact(left, right):
    return jnp.dot(left, right, precision=lax.Precision.HIGHEST, preferred_element_type=F32)


def tall_sum(value):
    return jnp.sum(value.reshape(-1, 8, value.shape[-1]), axis=0)


def tile_of(z, x, core):
    return (z * RING_X + x) * CORES + core


def greet(peers):
    barrier = pltpu.get_barrier_semaphore()
    for peer in peers:
        pl.semaphore_signal(barrier, inc=1, device_id=peer, device_id_type=MESH)
    pl.semaphore_wait(barrier, len(peers))


def remote(source, target, sends, receives, index, peer):
    return pltpu.make_async_remote_copy(
        src_ref=source,
        dst_ref=target,
        send_sem=sends.at[index],
        recv_sem=receives.at[index],
        device_id=peer,
        device_id_type=MESH,
    )


def begin(source, target, sends, receives, first, peers):
    copies = [
        remote(source, target, sends, receives, first + index, peer)
        for index, peer in enumerate(peers)
    ]
    for copy in copies:
        copy.start()
    return copies


def finish(copies):
    for copy in copies:
        copy.wait()


def packed_sides(folded, count, low_half):
    cos, sin = folded[:count], folded[count:]
    swapped = pltpu.roll(sin, ZF, 1)
    turned = jnp.where(low_half, swapped, -swapped)
    return cos + turned, cos - turned


def match_kernel(
    plan, tiles, groups, spots, own, block, valid, quats, rot_index, packed, zsum, ones, best, evidence, moments, parts,
    stats, low, high, bank, spectrum, slab_mid, zed, mid, back, marks, ready, row, sends,
    receives, part_sends, part_receives, passing, relay_sends, relay_receives,
):
    slab_z, slab_x, slab_y, table_z, table_x, table_y, table_yi, table_xi, table_zi = [
        packed.at[first : first + tall, :wide] for first, tall, wide in spots
    ]
    ring_z = tiles // (CORES * RING_X)
    plane_size = RING_X * CORES
    kxp, kyp, ys, xs = plan.kxp, plan.kyp, plan.ys, plan.xs
    rows = 2 * kxp
    tile, rot = lax.axis_index("tile"), lax.axis_index("rot")
    core = lax.rem(tile, CORES)
    x = lax.rem(tile // CORES, RING_X)
    z = tile // (CORES * RING_X)
    z_peers = [{"tile": tile_of(lax.rem(z + d, ring_z), x, core)} for d in range(1, ring_z)]
    x_peers = [{"tile": tile_of(z, lax.rem(x + d, RING_X), core)} for d in range(1, RING_X)]
    other = {"tile": tile_of(z, x, 1 - core)}
    line_size, sheet_size = ring_z * CORES, RING_X * groups
    line_peers, sheet_peers = [], []
    for d in range(1, line_size):
        there = lax.rem(z * CORES + core + d, line_size)
        line_peers.append({"tile": tile_of(there // CORES, x, lax.rem(there, CORES))})
    for d in range(1, sheet_size):
        there = lax.rem(x * groups + rot + d, sheet_size)
        sheet_peers.append(
            {"tile": tile_of(z, there // groups, core), "rot": lax.rem(there, groups)}
        )
    after = {"tile": lax.rem(tile + 1, tiles)}
    before = {"tile": lax.rem(tile + tiles - 1, tiles)}
    low_half = lax.broadcasted_iota(jnp.int32, (1, LANES), 1) < ZF
    width = ys * plan.zs // HALO_PARTS
    first_halo, first_z = 0, 2 * HALO_PARTS
    first_x = first_z + ring_z - 1
    first_pass = first_x + RING_X
    first_stats = first_pass + RING_X - 1

    for k in range(plan.kxu, plan.kxc):
        for side in range(2):
            first = (k + side * plan.kxc) * ys
            back[:, first : first + ys, :] = jnp.zeros((2, ys, LANES), F32)
    greet([after, before] + line_peers + sheet_peers)

    def halo(q):
        lanes = pl.ds(pl.multiple_of(q * width, LANES), width)
        return [
            remote(own.at[:, lanes], low.at[:, lanes], sends, receives, first_halo + 2 * q, after),
            remote(own.at[:, lanes], high.at[:, lanes], sends, receives, first_halo + 2 * q + 1, before),
        ]

    for q in range(HALO_PARTS):
        for copy in halo(q):
            copy.start()
    bank[core, x, z] = block[...]
    mine = bank.at[core, x, z]
    copies = begin(mine, mine, sends, receives, first_z, z_peers)

    flags = valid[...].astype(F32)
    columns = jnp.sum(flags)
    for y in range(ys):
        marks[y * xs : y * xs + xs, :] = jnp.broadcast_to(flags[:, y : y + 1], (xs, LANES))
    field = lax.rem(lax.broadcasted_iota(jnp.int32, (1, LANES), 1), ZF)
    line = jnp.where(field == FIELD_COUNT, columns, 0.0)
    entry = lax.broadcasted_iota(jnp.int32, quats.shape, 1)
    for r in range(4):
        found = jnp.sum(jnp.where(entry == rot_index[r], quats[...], 0.0), axis=1, keepdims=True)
        half = low_half if r % 2 == 0 else jnp.logical_not(low_half)
        for c in range(4):
            here = jnp.logical_and(field == FIELD_QUAT + 4 * (r // 2) + c, half)
            line = jnp.where(here, found[c : c + 1], line)
    row[...] = line

    several = 5

    def slab_first(first):
        blocks = []
        for t in range(several):
            lanes = pl.ds(pl.multiple_of((first + t) * LANES, LANES), LANES)
            blocks += [
                jnp.where(tile > 0, low[:, lanes].astype(F32)[xs - HALF :], 0.0),
                own[:, lanes].astype(F32),
                jnp.where(tile < tiles - 1, high[:, lanes].astype(F32)[:HALF], 0.0),
            ]
        block = jnp.concatenate(blocks, axis=0).astype(BF16)
        strips = mm(jnp.concatenate([block, block], axis=1), slab_z[...])
        for t in range(several):
            folded = stacked_product(slab_x[...], strips[t * plan.lx : t * plan.lx + plan.lx])
            for part in range(2):
                sides = packed_sides(folded[:, part * LANES : part * LANES + LANES], kxp, low_half)
                to = pl.multiple_of((2 * (first + t) + part) * rows, 8)
                for s in range(2):
                    slab_mid[pl.ds(pl.multiple_of(to + s * kxp, 8), kxp), :] = sides[s]

    pieces = ys // 2 // HALO_PARTS

    def slab_part(q, carry):
        for copy in halo(q):
            copy.wait()

        def body(i, inner):
            slab_first(q * pieces + i * several)
            return inner

        return lax.fori_loop(0, pieces // several, body, carry)

    lax.fori_loop(0, HALO_PARTS // 2, slab_part, 0)
    finish(copies)
    mine = bank.at[core, x]
    copies = begin(mine, mine, sends, receives, first_x, x_peers + [other])
    lax.fori_loop(HALO_PARTS // 2, HALO_PARTS, slab_part, 0)

    def slab_second(k, carry):
        lines = [slab_mid[pl.ds(k + s * kxp, ys, stride=rows), :] for s in range(2)]
        folded = stacked_product(slab_y[...], jnp.concatenate(lines, axis=1))
        for s in range(2):
            lanes = slice(s * LANES, s * LANES + LANES)
            cos, sin = folded[:kyp, lanes], folded[kyp:, lanes]
            cos_turned, sin_turned = pltpu.roll(cos, ZF, 1), pltpu.roll(sin, ZF, 1)
            for u in range(2):
                re_low, im_high = cos + sin_turned, cos - sin_turned
                im_low, re_high = cos_turned - sin, cos_turned + sin
                if u == 1:
                    re_low, im_high = im_high, re_low
                    im_low, re_high = re_high, im_low
                spectrum[k, s, u, :, :LANES] = jnp.where(low_half, re_low, re_high)
                spectrum[k, s, u, :, LANES:] = jnp.where(low_half, im_low, im_high)
        return carry

    trips = plan.kxu // 21
    lax.fori_loop(0, trips // 2, unrolled(slab_second, 21), 0)
    forwards = []
    for d in range(1, RING_X):
        copies[d - 1].wait()
        mine = bank.at[core, lax.rem(x + RING_X - d, RING_X)]
        forward = remote(mine, mine, sends, receives, first_pass + d - 1, other)
        forward.start()
        forwards.append(forward)
    lax.fori_loop(trips // 2, trips, unrolled(slab_second, 21), 0)
    copies[-1].wait()
    finish(forwards)

    per = TEMPL * TEMPL // tiles
    total = float(TEMPL**3)
    lane = lax.broadcasted_iota(jnp.int32, (BLOCK, LANES), 1)
    place = lax.broadcasted_iota(jnp.int32, (BLOCK, LANES), 0)
    used = jnp.logical_and(lax.rem(lane, ZF) < TEMPL, place < 2 * per)[None]
    tall = ring_z * BLOCK

    def lane_groups(value):
        wide = jnp.broadcast_to(jnp.sum(value, axis=0, keepdims=True), (8, LANES))
        return exact(wide, ones[...])[:1]

    def both_pairs(value):
        first = lane_groups(jnp.where(place < per, value, 0.0))
        second = lane_groups(jnp.where(place < per, 0.0, value))
        return first, second

    def bank_rows(i):
        return bank[i // RING_X, lax.rem(i, RING_X)]

    def add_up(i, carry):
        return carry + jnp.sum(bank_rows(i).astype(F32), axis=0)

    empty = jnp.zeros((BLOCK, LANES), F32)
    means = both_pairs(lax.fori_loop(0, plane_size, add_up, empty))
    means = [mean / total for mean in means]
    mean_rows = jnp.where(place < per, means[0], means[1])[None]

    def add_squares(i, carry):
        off = jnp.where(used, bank_rows(i).astype(F32) - mean_rows, 0.0)
        return carry + jnp.sum(off * off, axis=0)

    squares = both_pairs(lax.fori_loop(0, plane_size, add_squares, empty))
    factors = [
        1.0 / (jnp.sqrt(square / total + EPSILON) * float(TEMPL) ** 1.5) for square in squares
    ]
    scale_rows = jnp.where(place < per, factors[0], factors[1])[None]

    def z_stage(i, carry):
        lines = bank_rows(i).reshape(tall, LANES)
        value = mm(jnp.concatenate([lines, lines], axis=1), table_z[...])
        at = pl.ds(pl.multiple_of(i * tall, tall), tall)
        for part in range(2):
            lanes = slice(part * LANES, part * LANES + LANES)
            side = value[:, lanes].reshape(ring_z, BLOCK, LANES)
            side = (side - mean_rows * zsum[:, lanes]) * scale_rows
            zed[part, at, :] = side.reshape(tall, LANES)
        return carry

    lax.fori_loop(0, plane_size, z_stage, 0)
    share = ys // groups
    step = share
    piece = per // 3

    middle = share * xs // 2
    across, back_one = {"rot": lax.rem(rot + 2, groups)}, {"rot": lax.rem(rot + 3, groups)}

    def direct(p):
        source, target = ready.at[p, 2, :middle], parts.at[p, 2, :middle]
        return remote(source, target, part_sends.at[p], part_receives.at[p], 2, across)

    def hop(p):
        source, target = ready.at[p, 2, middle:], passing.at[p]
        return remote(source, target, relay_sends.at[p], relay_receives.at[p], 0, back_one)

    def forward_half(p):
        source, target = passing.at[p], parts.at[p, 2, middle:]
        return remote(source, target, relay_sends.at[p], relay_receives.at[p], 1, back_one)

    def pair(p, outer):
        def x_stage(g, carry):
            starts = []
            for s in range(TEMPL // ring_z):
                m = s * (TEMPL // piece) + g
                owner = m // 3
                there = lax.rem(owner, CORES) * RING_X + owner // CORES
                starts.append(there * tall + p * per + lax.rem(m, 3) * piece)
            for t in range(piece):
                lines = []
                for start in starts:
                    at = pl.ds(start + t, ring_z, stride=BLOCK)
                    lines.append(jnp.concatenate([zed[0, at, :], zed[1, at, :]], axis=1))
                folded = stacked_product(table_x[...], jnp.concatenate(lines, axis=0))
                to = pl.multiple_of((g * piece + t) * rows, 8)
                for s, (re, im) in enumerate(plus_minus(folded, kxp, 1)):
                    at = pl.ds(pl.multiple_of(to + s * kxp, 8), kxp)
                    mid[0, at, :] = re
                    mid[1, at, :] = im
            return carry

        lax.fori_loop(0, TEMPL // piece, x_stage, 0)

        @pl.when(p == 1)
        def _():
            hop(0).wait_recv()
            forward_half(0).start()

        def y_stage(k, carry):
            found = []
            for s in range(2):
                at = pl.ds(k + s * kxp, TEMPL, stride=rows)
                value = jnp.concatenate([mid[0, at, :], mid[1, at, :]], axis=1)
                folded = stacked_product(table_y[...], value)
                sides = []
                for u, (re, im) in enumerate(plus_minus(folded, kyp, 1)):
                    slab_re = spectrum[k, s, u, :, :LANES]
                    slab_im = spectrum[k, s, u, :, LANES:]
                    sides.append((re * slab_re - im * slab_im, re * slab_im + im * slab_re))
                (re_p, im_p), (re_m, im_m) = sides
                even = jnp.concatenate([re_p + re_m, im_p + im_m], axis=1)
                odd = jnp.concatenate([im_m - im_p, re_p - re_m], axis=1)
                found.append(paired_product(table_yi[...], jnp.concatenate([even, odd], axis=0)))
            even = found[0] + found[1]
            odd = found[0] - found[1]
            to = pl.ds(pl.multiple_of(k * ys, 8), ys)
            back[0, to, :] = even[:, :LANES]
            back[1, to, :] = even[:, LANES:]
            to = pl.ds(pl.multiple_of((k + plan.kxc) * ys, 8), ys)
            back[0, to, :] = -odd[:, LANES:]
            back[1, to, :] = odd[:, :LANES]
            return carry

        lax.fori_loop(0, plan.kxu // 21, unrolled(y_stage, 21), 0)

        def last(i, lane_sum):
            j = lax.rem(2 + 3 * i + 3 * (i * (i - 1) // 2), groups)
            base = lax.rem(rot + j, groups) * share
            lines = []
            for y in range(step):
                at = pl.ds(base + y, plan.kxi, stride=ys)
                value = jnp.concatenate([back[0, at, :], back[1, at, :]], axis=1)
                lines.append(rows_product(table_xi[...], value))
            upper, lower = split(jnp.concatenate(lines, axis=0))
            both = mm(upper, table_zi[...])
            value = both[:, :LANES] + both[:, LANES:] + mm(lower, table_zi[:, :LANES])
            ready[p, j] = value

            @pl.when(lax.rem(j, 2) == 1)
            def _():
                send_part(p, j).start()

            @pl.when(j == 2)
            def _():
                hop(p).start()
                direct(p).start()

            mark = marks[pl.ds(pl.multiple_of(base * xs, 8), share * xs), :]
            return lane_sum + tall_sum(value * mark)

        def send_part(p, j):
            return pltpu.make_async_remote_copy(
                src_ref=ready.at[p, j],
                dst_ref=parts.at[p, j],
                send_sem=part_sends.at[p, j],
                recv_sem=part_receives.at[p, j],
                device_id={"rot": lax.rem(rot + j, groups)},
                device_id_type=MESH,
            )

        lane_sum = lax.fori_loop(0, groups, last, jnp.zeros((8, LANES), F32))
        lane_mean = jnp.sum(lane_sum, axis=0, keepdims=True) / jnp.maximum(columns, 1.0)

        def add_off(j, carry):
            base = lax.rem(rot + j, groups) * (share * xs)
            mark = marks[pl.ds(pl.multiple_of(base, 8), share * xs), :]
            off = ready[p, j] - lane_mean
            return carry + tall_sum(off * off * mark)

        lane_square = lax.fori_loop(0, groups, add_off, jnp.zeros((8, LANES), F32))
        wide = jnp.broadcast_to(lane_mean, (8, LANES))
        part_mean = exact(wide, ones[...])[:1] / float(plan.zs)
        off = lane_mean - part_mean
        lane_square = jnp.sum(lane_square, axis=0, keepdims=True) + columns * off * off
        part_square = exact(jnp.broadcast_to(lane_square, (8, LANES)), ones[...])[:1]
        now = jnp.where(field == 2 * p, part_mean, row[...])
        row[...] = jnp.where(field == 2 * p + 1, part_square, now)
        return outer

    lax.fori_loop(0, 2, pair, 0)
    place = z * CORES + core
    stats[rot, x, place] = row[...]
    mine = stats.at[rot, x, place]
    finish(begin(mine, mine, sends, receives, first_stats, line_peers))
    mine = stats.at[rot, x]
    copies = begin(mine, mine, sends, receives, first_stats + line_size - 1, sheet_peers)
    hop(1).wait_recv()
    forward_half(1).start()
    finish(copies)
    incoming = [
        remote(ready.at[p, j], parts.at[p, j], part_sends.at[p], part_receives.at[p], j, {"rot": lax.rem(rot + j, groups)})
        for p in range(2)
        for j in (1, 3)
    ]

    def spread_field(lines, index):
        return jnp.where(
            low_half, lines[:, index : index + 1], lines[:, ZF + index : ZF + index + 1]
        )

    terms = []
    for j in range(groups):
        group = lax.rem(rot + groups - j, groups)
        lines = stats[group].reshape(-1, LANES)
        count = lines[:, FIELD_COUNT : FIELD_COUNT + 1]
        total = jnp.sum(count, axis=0, keepdims=True)
        average = jnp.sum(count * lines, axis=0, keepdims=True) / total
        off = lines - average
        square = jnp.sum(count * off * off, axis=0, keepdims=True) * plan.zs
        square += pltpu.roll(jnp.sum(lines, axis=0, keepdims=True), LANES - 1, 1)
        inverse = 1.0 / jnp.sqrt(square / (total * plan.zs) + EPSILON)
        for p in range(2):
            source = ready if j == 0 else parts
            quat = [spread_field(lines[:1], FIELD_QUAT + 4 * p + c) for c in range(4)]
            terms.append(
                (source.at[p, j], spread_field(average, 2 * p), spread_field(inverse, 2 * p), quat)
            )

    finish(incoming)
    for p in range(2):
        direct(p).wait()
        hop(p).wait_send()
        forward_half(p).wait()

    def column(y):
        at = pl.ds(pl.multiple_of(y * xs, 8), xs)
        scores = [(ref[at, :] - average) * inverse for ref, average, inverse, _ in terms]
        high = functools.reduce(jnp.maximum, scores)
        high = jnp.maximum(high, pltpu.roll(high, ZF, 1))
        weights = [jnp.exp(score - high) for score in scores]
        sums = [functools.reduce(jnp.add, weights)]
        for c in range(4):
            sums.append(functools.reduce(jnp.add, [w * t[3][c] for w, t in zip(weights, terms)]))
        return [high] + [value + pltpu.roll(value, ZF, 1) for value in sums]

    def answer(j, carry):
        both = [jnp.where(low_half, a, b) for a, b in zip(column(2 * j), column(2 * j + 1))]
        base = pl.multiple_of(rot * (share * xs) + 2 * j * xs, 8)
        inside = jnp.where(
            low_half, marks[pl.ds(base, xs), :], marks[pl.ds(pl.multiple_of(base + xs, 8), xs), :]
        )
        high, total = both[0], both[1]
        lanes = pl.ds(pl.multiple_of(j * LANES, LANES), LANES)
        best[:, lanes] = inside * high
        evidence[:, lanes] = inside * (high + jnp.log(total))
        ratio = inside / total
        for c in range(4):
            moments[c, :, lanes] = both[2 + c] * ratio
        return carry

    lax.fori_loop(0, share // 2 // 5, unrolled(answer, 5), 0)


def matched(plan, tiles, groups, own, block, valid, quats, rot_index):
    ring_z = tiles // (CORES * RING_X)
    order = (
        np.arange(TEMPL // ring_z)[:, None] + (TEMPL // ring_z) * np.arange(ring_z)[None]
    ).reshape(-1)
    z_table = plan.tmpl_z()
    tables = [
        row_stack(plan.slab_z()),
        stacked_table(plan.folded(plan.kx, plan.kxp, np.arange(plan.lx), plan.lx)),
        stacked_table(plan.folded(plan.ky, plan.kyp, np.arange(plan.ys), plan.ly)),
        row_stack(z_table),
        stacked_table(plan.folded(plan.kx, plan.kxp, order, plan.lx)),
        stacked_table(plan.folded(plan.ky, plan.kyp, np.arange(TEMPL) - HALF, plan.ly)),
        paired_table(plan.inverse_rows(np.arange(plan.ys), plan.ky, plan.ly, plan.kyp, 2 * plan.kyp)),
        row_tables(plan.inverse_rows(np.arange(plan.xs), plan.kx, plan.lx, plan.kxc, plan.kxi)),
        col_tables(plan.inverse_z()),
    ]
    spots, first = [], 0
    for table in tables:
        spots.append((first, table.shape[0], table.shape[1]))
        first += table.shape[0]
    tables = [
        np.concatenate([padded_cols(table, 2 * LANES) for table in tables], axis=0),
        z_table.sum(axis=0, keepdims=True).astype(np.float32),
        np.kron(np.eye(2), np.ones((ZF, ZF))).astype(np.float32),
    ]
    share = plan.ys // groups * plan.xs
    copies = 2 * HALO_PARTS + ring_z + 2 * RING_X - 2 + ring_z * CORES + RING_X * groups - 2
    vmem = pl.BlockSpec(memory_space=pltpu.VMEM)
    flat_out = jax.ShapeDtypeStruct((plan.xs, plan.ys // groups * plan.zs), F32)
    return pl.pallas_call(
        functools.partial(match_kernel, plan, tiles, groups, spots),
        out_shape=[flat_out, flat_out, jax.ShapeDtypeStruct((4,) + flat_out.shape, F32)],
        in_specs=[vmem] * 4
        + [pl.BlockSpec(memory_space=pltpu.SMEM)]
        + [vmem] * len(tables),
        out_specs=[vmem] * 3,
        scratch_shapes=[
            pltpu.VMEM((2, groups, share, LANES), F32),
            pltpu.VMEM((groups, RING_X, ring_z * CORES, 1, LANES), F32),
            pltpu.VMEM(own.shape, BF16),
            pltpu.VMEM(own.shape, BF16),
            pltpu.VMEM((CORES, RING_X, ring_z) + block.shape, BF16),
            pltpu.VMEM((plan.kxc, 2, 2, plan.kyp, 2 * LANES), F32),
            pltpu.VMEM((plan.ys * 2 * plan.kxp, LANES), F32),
            pltpu.VMEM((2, tiles * BLOCK, LANES), F32),
            pltpu.VMEM((2, TEMPL * 2 * plan.kxp, LANES), F32),
            pltpu.VMEM((2, plan.kxi * plan.ys, LANES), F32),
            pltpu.VMEM((plan.ys * plan.xs, LANES), F32),
            pltpu.VMEM((2, groups, share, LANES), F32),
            pltpu.VMEM((1, LANES), F32),
            pltpu.SemaphoreType.DMA((copies,)),
            pltpu.SemaphoreType.DMA((copies,)),
            pltpu.SemaphoreType.DMA((2, groups)),
            pltpu.SemaphoreType.DMA((2, groups)),
            pltpu.VMEM((2, share // 2, LANES), F32),
            pltpu.SemaphoreType.DMA((2, 2)),
            pltpu.SemaphoreType.DMA((2, 2)),
        ],
        compiler_params=pltpu.CompilerParams(
            collective_id=0, has_side_effects=True, vmem_limit_bytes=48 << 20
        ),
        name="match",
    )(own, block, valid, quats, rot_index, *tables)


def row_stack(table):
    return np.concatenate(halves(table), axis=0)


def local(tomogram, templates, valid, quats, rot_index):
    xs, voxels = tomogram.shape
    ys = valid.shape[1]
    zs = voxels // ys
    plan = Plan(xs, ys, zs)
    tiles, groups = lax.axis_size("tile"), lax.axis_size("rot")
    per = templates.shape[1] // TEMPL
    block = templates.reshape(2, 2, per, TEMPL).transpose(0, 2, 1, 3)
    block = jnp.pad(block, ((0, 0), (0, 0), (0, 0), (0, ZF - TEMPL))).reshape(2 * per, LANES)
    block = jnp.pad(block, ((0, BLOCK - 2 * per), (0, 0)))
    return tuple(matched(plan, tiles, groups, tomogram, block, valid, quats, rot_index))


def solution(mesh):
    placed = (P("tile", None), P("rot", "tile"), P("tile", None), P(), P("rot"))
    return jax.shard_map(
        local,
        mesh=mesh,
        in_specs=placed,
        out_specs=(P("tile", "rot"), P("tile", "rot"), P(None, "tile", "rot")),
        check_vma=False,
    )
```

```python
import functools
import math

import jax
import jax.numpy as jnp
import ml_dtypes
import numpy as np
from jax import lax
from jax.experimental import pallas as pl
from jax.experimental.pallas import tpu as pltpu
from jax.sharding import PartitionSpec as P

TEMPL = 48
HALF = 24
EPSILON = 1e-06
LANES = 128
ZF = 64
CORES = 2
RING_X = 4
BLOCK = 80
HALO_PARTS = 4
MESH = pl.DeviceIdType.MESH
FIELD_COUNT = 4
FIELD_QUAT = 5
F32 = jnp.float32
BF16 = jnp.bfloat16


def halves(table):
    high = table.astype(np.float32).astype(ml_dtypes.bfloat16)
    low = (table - high.astype(np.float64)).astype(np.float32).astype(ml_dtypes.bfloat16)
    return high, low


def row_tables(table):
    high, low = halves(table)
    return np.concatenate([high, low], axis=0)


def col_tables(table):
    high, low = halves(table)
    return np.concatenate([high, low], axis=1)


def phases(rows, cols, length):
    index = np.outer(np.asarray(rows), np.asarray(cols)) % length
    return index * (2.0 * np.pi / length)


def padded_rows(table, rows):
    return np.pad(table, ((0, rows - table.shape[0]), (0, 0)))


def padded_cols(table, cols):
    return np.pad(table, ((0, 0), (0, cols - table.shape[1])))


def up8(n):
    return -(-n // 8) * 8


class Plan:
    def __init__(self, xs, ys, zs):
        self.xs, self.ys, self.zs = xs, ys, zs
        self.lx, self.ly, self.lz = xs + TEMPL, ys + HALF, zs + HALF
        self.kx, self.ky, self.kz = self.lx // 2 + 1, self.ly // 2 + 1, self.lz // 2 + 1
        self.kxp, self.kyp = up8(self.kx), up8(self.ky)
        self.kxu = -(-self.kx // 2) * 2
        self.kxc = -(-self.kx // 4) * 4
        self.kxi = 2 * self.kxc

    def folded(self, count, pad, points, length):
        angle = phases(np.arange(count), points, length)
        return np.concatenate(
            [padded_rows(np.cos(angle), pad), padded_rows(np.sin(angle), pad)], axis=0
        )

    def slab_z(self):
        angle = phases(np.arange(self.zs), np.arange(self.kz), self.lz)
        cos = padded_cols(np.cos(angle), ZF)
        sin = padded_cols(-np.sin(angle), ZF)
        one = np.concatenate([cos, sin], axis=1)
        return np.kron(np.eye(2), one)

    def tmpl_z(self):
        angle = phases(np.arange(TEMPL) - HALF, np.arange(self.kz), self.lz)
        cos = np.zeros((ZF, ZF))
        sin = np.zeros((ZF, ZF))
        cos[:TEMPL, : self.kz] = np.cos(angle)
        sin[:TEMPL, : self.kz] = np.sin(angle)
        none = np.zeros_like(cos)
        return np.block([[cos, none, sin, none], [none, cos, none, sin]])

    def inverse_rows(self, points, count, length, k_pad, tail):
        angle = phases(points, np.arange(count), length)
        weight = np.full((1, count), 1.0 / length)
        weight[0, 0] *= 0.5
        weight[0, count - 1] *= 0.5
        cos = padded_cols(np.cos(angle) * weight, k_pad)
        sin = padded_cols(np.sin(angle) * weight, k_pad)
        return padded_cols(np.concatenate([cos, sin], axis=1), tail)

    def inverse_z(self):
        angle = phases(np.arange(self.kz), np.arange(self.zs), self.lz)
        weight = np.full((self.kz, 1), 2.0 / self.lz)
        weight[0] *= 0.5
        weight[self.kz - 1] *= 0.5
        cos = padded_rows(np.cos(angle) * weight, ZF)
        sin = padded_rows(-np.sin(angle) * weight, ZF)
        none = np.zeros_like(cos)
        return np.block([[cos, none], [none, cos], [sin, none], [none, sin]])


def unrolled(body, count):
    def many(i, carry):
        return lax.fori_loop(0, count, lambda part, c: body(i * count + part, c), carry, unroll=True)

    return many


def split(value):
    high = value.astype(BF16)
    return high, (value - high.astype(F32)).astype(BF16)


def mm(left, right):
    return jnp.dot(left, right, preferred_element_type=F32)


def rows_product(table, value):
    count = table.shape[0] // 2
    high, low = split(value)
    both = mm(table, high)
    return both[:count] + both[count:] + mm(table[:count], low)


def stacked_table(table):
    high, low = halves(table)
    return np.concatenate([high, high, low], axis=1)


def stacked_product(table, value):
    high, low = split(value)
    return mm(table, jnp.concatenate([high, low, high], axis=0))


def paired_table(table):
    high, low = halves(table)
    return np.block([[high, high], [low, np.zeros_like(low)]])


def paired_product(table, value):
    high, low = split(value)
    count = table.shape[0] // 2
    both = mm(table, jnp.concatenate([high, low], axis=0))
    return both[:count] + both[count:]


def plus_minus(folded, count, sign):
    cos_re, cos_im = folded[:count, :LANES], folded[:count, LANES:]
    sin_re, sin_im = folded[count:, :LANES], folded[count:, LANES:]
    first = (cos_re - sin_im, cos_im + sin_re)
    second = (cos_re + sin_im, cos_im - sin_re)
    return (first, second) if sign > 0 else (second, first)


def exact(left, right):
    return jnp.dot(left, right, precision=lax.Precision.HIGHEST, preferred_element_type=F32)


def tall_sum(value):
    return jnp.sum(value.reshape(-1, 8, value.shape[-1]), axis=0)


def tile_of(z, x, core):
    return (z * RING_X + x) * CORES + core


def greet(peers):
    barrier = pltpu.get_barrier_semaphore()
    for peer in peers:
        pl.semaphore_signal(barrier, inc=1, device_id=peer, device_id_type=MESH)
    pl.semaphore_wait(barrier, len(peers))


def remote(source, target, sends, receives, index, peer):
    return pltpu.make_async_remote_copy(
        src_ref=source,
        dst_ref=target,
        send_sem=sends.at[index],
        recv_sem=receives.at[index],
        device_id=peer,
        device_id_type=MESH,
    )


def begin(source, target, sends, receives, first, peers):
    copies = [
        remote(source, target, sends, receives, first + index, peer)
        for index, peer in enumerate(peers)
    ]
    for copy in copies:
        copy.start()
    return copies


def finish(copies):
    for copy in copies:
        copy.wait()


def packed_sides(folded, count, low_half):
    cos, sin = folded[:count], folded[count:]
    swapped = pltpu.roll(sin, ZF, 1)
    turned = jnp.where(low_half, swapped, -swapped)
    return cos + turned, cos - turned


def match_kernel(
    plan, tiles, groups, spots, own, block, valid, quats, rot_index, packed, zsum, ones, best, evidence, moments, parts,
    stats, low, high, bank, spectrum, slab_mid, zed, mid, back, marks, ready, row, sends,
    receives, part_sends, part_receives,
):
    slab_z, slab_x, slab_y, table_z, table_x, table_y, table_yi, table_xi, table_zi = [
        packed.at[first : first + tall, :wide] for first, tall, wide in spots
    ]
    ring_z = tiles // (CORES * RING_X)
    plane_size = RING_X * CORES
    kxp, kyp, ys, xs = plan.kxp, plan.kyp, plan.ys, plan.xs
    rows = 2 * kxp
    tile, rot = lax.axis_index("tile"), lax.axis_index("rot")
    core = lax.rem(tile, CORES)
    x = lax.rem(tile // CORES, RING_X)
    z = tile // (CORES * RING_X)
    z_peers = [{"tile": tile_of(lax.rem(z + d, ring_z), x, core)} for d in range(1, ring_z)]
    x_peers = [{"tile": tile_of(z, lax.rem(x + d, RING_X), core)} for d in range(1, RING_X)]
    other = {"tile": tile_of(z, x, 1 - core)}
    line_size, sheet_size = ring_z * CORES, RING_X * groups
    line_peers, sheet_peers = [], []
    for d in range(1, line_size):
        there = lax.rem(z * CORES + core + d, line_size)
        line_peers.append({"tile": tile_of(there // CORES, x, lax.rem(there, CORES))})
    for d in range(1, sheet_size):
        there = lax.rem(x * groups + rot + d, sheet_size)
        sheet_peers.append(
            {"tile": tile_of(z, there // groups, core), "rot": lax.rem(there, groups)}
        )
    after = {"tile": lax.rem(tile + 1, tiles)}
    before = {"tile": lax.rem(tile + tiles - 1, tiles)}
    low_half = lax.broadcasted_iota(jnp.int32, (1, LANES), 1) < ZF
    width = ys * plan.zs // HALO_PARTS
    first_halo, first_z = 0, 2 * HALO_PARTS
    first_x = first_z + ring_z - 1
    first_pass = first_x + RING_X
    first_stats = first_pass + RING_X - 1

    bank[core, x, z] = block[...]
    for k in range(plan.kxu, plan.kxc):
        for side in range(2):
            first = (k + side * plan.kxc) * ys
            back[:, first : first + ys, :] = jnp.zeros((2, ys, LANES), F32)
    greet([after, before] + line_peers + sheet_peers)

    def halo(q):
        lanes = pl.ds(pl.multiple_of(q * width, LANES), width)
        return [
            remote(own.at[:, lanes], low.at[:, lanes], sends, receives, first_halo + 2 * q, after),
            remote(own.at[:, lanes], high.at[:, lanes], sends, receives, first_halo + 2 * q + 1, before),
        ]

    mine = bank.at[core, x, z]
    copies = begin(mine, mine, sends, receives, first_z, z_peers)
    for q in range(HALO_PARTS):
        for copy in halo(q):
            copy.start()

    flags = valid[...].astype(F32)
    columns = jnp.sum(flags)
    for y in range(ys):
        marks[y * xs : y * xs + xs, :] = jnp.broadcast_to(flags[:, y : y + 1], (xs, LANES))
    field = lax.rem(lax.broadcasted_iota(jnp.int32, (1, LANES), 1), ZF)
    line = jnp.where(field == FIELD_COUNT, columns, 0.0)
    entry = lax.broadcasted_iota(jnp.int32, quats.shape, 1)
    for r in range(4):
        found = jnp.sum(jnp.where(entry == rot_index[r], quats[...], 0.0), axis=1, keepdims=True)
        half = low_half if r % 2 == 0 else jnp.logical_not(low_half)
        for c in range(4):
            here = jnp.logical_and(field == FIELD_QUAT + 4 * (r // 2) + c, half)
            line = jnp.where(here, found[c : c + 1], line)
    row[...] = line

    several = 5

    def slab_first(first):
        blocks = []
        for t in range(several):
            lanes = pl.ds(pl.multiple_of((first + t) * LANES, LANES), LANES)
            blocks += [
                jnp.where(tile > 0, low[:, lanes].astype(F32)[xs - HALF :], 0.0),
                own[:, lanes].astype(F32),
                jnp.where(tile < tiles - 1, high[:, lanes].astype(F32)[:HALF], 0.0),
            ]
        block = jnp.concatenate(blocks, axis=0).astype(BF16)
        strips = mm(jnp.concatenate([block, block], axis=1), slab_z[...])
        for t in range(several):
            folded = stacked_product(slab_x[...], strips[t * plan.lx : t * plan.lx + plan.lx])
            for part in range(2):
                sides = packed_sides(folded[:, part * LANES : part * LANES + LANES], kxp, low_half)
                to = pl.multiple_of((2 * (first + t) + part) * rows, 8)
                for s in range(2):
                    slab_mid[pl.ds(pl.multiple_of(to + s * kxp, 8), kxp), :] = sides[s]

    pieces = ys // 2 // HALO_PARTS

    def slab_part(q, carry):
        for copy in halo(q):
            copy.wait()

        def body(i, inner):
            slab_first(q * pieces + i * several)
            return inner

        return lax.fori_loop(0, pieces // several, body, carry)

    finish(copies)
    mine = bank.at[core, x]
    copies = begin(mine, mine, sends, receives, first_x, x_peers + [other])
    lax.fori_loop(0, HALO_PARTS, slab_part, 0)

    def slab_second(k, carry):
        lines = [slab_mid[pl.ds(k + s * kxp, ys, stride=rows), :] for s in range(2)]
        folded = stacked_product(slab_y[...], jnp.concatenate(lines, axis=1))
        for s in range(2):
            lanes = slice(s * LANES, s * LANES + LANES)
            cos, sin = folded[:kyp, lanes], folded[kyp:, lanes]
            cos_turned, sin_turned = pltpu.roll(cos, ZF, 1), pltpu.roll(sin, ZF, 1)
            for u in range(2):
                re_low, im_high = cos + sin_turned, cos - sin_turned
                im_low, re_high = cos_turned - sin, cos_turned + sin
                if u == 1:
                    re_low, im_high = im_high, re_low
                    im_low, re_high = re_high, im_low
                spectrum[k, s, u, :, :LANES] = jnp.where(low_half, re_low, re_high)
                spectrum[k, s, u, :, LANES:] = jnp.where(low_half, im_low, im_high)
        return carry

    trips = plan.kxu // 21
    lax.fori_loop(0, trips // 2, unrolled(slab_second, 21), 0)
    forwards = []
    for d in range(1, RING_X):
        copies[d - 1].wait()
        mine = bank.at[core, lax.rem(x + RING_X - d, RING_X)]
        forward = remote(mine, mine, sends, receives, first_pass + d - 1, other)
        forward.start()
        forwards.append(forward)
    lax.fori_loop(trips // 2, trips, unrolled(slab_second, 21), 0)
    copies[-1].wait()
    finish(forwards)

    per = TEMPL * TEMPL // tiles
    total = float(TEMPL**3)
    lane = lax.broadcasted_iota(jnp.int32, (BLOCK, LANES), 1)
    place = lax.broadcasted_iota(jnp.int32, (BLOCK, LANES), 0)
    used = jnp.logical_and(lax.rem(lane, ZF) < TEMPL, place < 2 * per)[None]
    tall = ring_z * BLOCK

    def lane_groups(value):
        wide = jnp.broadcast_to(jnp.sum(value, axis=0, keepdims=True), (8, LANES))
        return exact(wide, ones[...])[:1]

    def both_pairs(value):
        first = lane_groups(jnp.where(place < per, value, 0.0))
        second = lane_groups(jnp.where(place < per, 0.0, value))
        return first, second

    def bank_rows(i):
        return bank[i // RING_X, lax.rem(i, RING_X)]

    def add_up(i, carry):
        return carry + jnp.sum(bank_rows(i).astype(F32), axis=0)

    empty = jnp.zeros((BLOCK, LANES), F32)
    means = both_pairs(lax.fori_loop(0, plane_size, add_up, empty))
    means = [mean / total for mean in means]
    mean_rows = jnp.where(place < per, means[0], means[1])[None]

    def add_squares(i, carry):
        off = jnp.where(used, bank_rows(i).astype(F32) - mean_rows, 0.0)
        return carry + jnp.sum(off * off, axis=0)

    squares = both_pairs(lax.fori_loop(0, plane_size, add_squares, empty))
    factors = [
        1.0 / (jnp.sqrt(square / total + EPSILON) * float(TEMPL) ** 1.5) for square in squares
    ]
    scale_rows = jnp.where(place < per, factors[0], factors[1])[None]

    def z_stage(i, carry):
        lines = bank_rows(i).reshape(tall, LANES)
        value = mm(jnp.concatenate([lines, lines], axis=1), table_z[...])
        at = pl.ds(pl.multiple_of(i * tall, tall), tall)
        for part in range(2):
            lanes = slice(part * LANES, part * LANES + LANES)
            side = value[:, lanes].reshape(ring_z, BLOCK, LANES)
            side = (side - mean_rows * zsum[:, lanes]) * scale_rows
            zed[part, at, :] = side.reshape(tall, LANES)
        return carry

    lax.fori_loop(0, plane_size, z_stage, 0)
    share = ys // groups
    step = share
    piece = per // 3

    def pair(p, outer):
        def x_stage(g, carry):
            starts = []
            for s in range(TEMPL // ring_z):
                m = s * (TEMPL // piece) + g
                owner = m // 3
                there = lax.rem(owner, CORES) * RING_X + owner // CORES
                starts.append(there * tall + p * per + lax.rem(m, 3) * piece)
            for t in range(piece):
                lines = []
                for start in starts:
                    at = pl.ds(start + t, ring_z, stride=BLOCK)
                    lines.append(jnp.concatenate([zed[0, at, :], zed[1, at, :]], axis=1))
                folded = stacked_product(table_x[...], jnp.concatenate(lines, axis=0))
                to = pl.multiple_of((g * piece + t) * rows, 8)
                for s, (re, im) in enumerate(plus_minus(folded, kxp, 1)):
                    at = pl.ds(pl.multiple_of(to + s * kxp, 8), kxp)
                    mid[0, at, :] = re
                    mid[1, at, :] = im
            return carry

        lax.fori_loop(0, TEMPL // piece, x_stage, 0)

        def y_stage(k, carry):
            found = []
            for s in range(2):
                at = pl.ds(k + s * kxp, TEMPL, stride=rows)
                value = jnp.concatenate([mid[0, at, :], mid[1, at, :]], axis=1)
                folded = stacked_product(table_y[...], value)
                sides = []
                for u, (re, im) in enumerate(plus_minus(folded, kyp, 1)):
                    slab_re = spectrum[k, s, u, :, :LANES]
                    slab_im = spectrum[k, s, u, :, LANES:]
                    sides.append((re * slab_re - im * slab_im, re * slab_im + im * slab_re))
                (re_p, im_p), (re_m, im_m) = sides
                even = jnp.concatenate([re_p + re_m, im_p + im_m], axis=1)
                odd = jnp.concatenate([im_m - im_p, re_p - re_m], axis=1)
                found.append(paired_product(table_yi[...], jnp.concatenate([even, odd], axis=0)))
            even = found[0] + found[1]
            odd = found[0] - found[1]
            to = pl.ds(pl.multiple_of(k * ys, 8), ys)
            back[0, to, :] = even[:, :LANES]
            back[1, to, :] = even[:, LANES:]
            to = pl.ds(pl.multiple_of((k + plan.kxc) * ys, 8), ys)
            back[0, to, :] = -odd[:, LANES:]
            back[1, to, :] = odd[:, :LANES]
            return carry

        lax.fori_loop(0, plan.kxu // 21, unrolled(y_stage, 21), 0)

        def last(i, lane_sum):
            j = lax.rem(2 + 3 * i + 3 * (i * (i - 1) // 2), groups)
            base = lax.rem(rot + j, groups) * share
            lines = []
            for y in range(step):
                at = pl.ds(base + y, plan.kxi, stride=ys)
                value = jnp.concatenate([back[0, at, :], back[1, at, :]], axis=1)
                lines.append(rows_product(table_xi[...], value))
            upper, lower = split(jnp.concatenate(lines, axis=0))
            both = mm(upper, table_zi[...])
            value = both[:, :LANES] + both[:, LANES:] + mm(lower, table_zi[:, :LANES])
            ready[p, j] = value

            @pl.when(j > 0)
            def _():
                send_part(p, j).start()

            mark = marks[pl.ds(pl.multiple_of(base * xs, 8), share * xs), :]
            return lane_sum + tall_sum(value * mark)

        def send_part(p, j):
            return pltpu.make_async_remote_copy(
                src_ref=ready.at[p, j],
                dst_ref=parts.at[p, j],
                send_sem=part_sends.at[p, j],
                recv_sem=part_receives.at[p, j],
                device_id={"rot": lax.rem(rot + j, groups)},
                device_id_type=MESH,
            )

        lane_sum = lax.fori_loop(0, groups, last, jnp.zeros((8, LANES), F32))
        lane_mean = jnp.sum(lane_sum, axis=0, keepdims=True) / jnp.maximum(columns, 1.0)

        def add_off(j, carry):
            base = lax.rem(rot + j, groups) * (share * xs)
            mark = marks[pl.ds(pl.multiple_of(base, 8), share * xs), :]
            off = ready[p, j] - lane_mean
            return carry + tall_sum(off * off * mark)

        lane_square = lax.fori_loop(0, groups, add_off, jnp.zeros((8, LANES), F32))
        wide = jnp.broadcast_to(lane_mean, (8, LANES))
        part_mean = exact(wide, ones[...])[:1] / float(plan.zs)
        off = lane_mean - part_mean
        lane_square = jnp.sum(lane_square, axis=0, keepdims=True) + columns * off * off
        part_square = exact(jnp.broadcast_to(lane_square, (8, LANES)), ones[...])[:1]
        now = jnp.where(field == 2 * p, part_mean, row[...])
        row[...] = jnp.where(field == 2 * p + 1, part_square, now)
        return outer

    lax.fori_loop(0, 2, pair, 0)
    place = z * CORES + core
    stats[rot, x, place] = row[...]
    mine = stats.at[rot, x, place]
    finish(begin(mine, mine, sends, receives, first_stats, line_peers))
    mine = stats.at[rot, x]
    finish(begin(mine, mine, sends, receives, first_stats + line_size - 1, sheet_peers))
    incoming = [
        remote(ready.at[p, j], parts.at[p, j], part_sends.at[p], part_receives.at[p], j, {"rot": lax.rem(rot + j, groups)})
        for p in range(2)
        for j in range(1, groups)
    ]

    def spread_field(lines, index):
        return jnp.where(
            low_half, lines[:, index : index + 1], lines[:, ZF + index : ZF + index + 1]
        )

    terms = []
    for j in range(groups):
        group = lax.rem(rot + groups - j, groups)
        lines = stats[group].reshape(-1, LANES)
        count = lines[:, FIELD_COUNT : FIELD_COUNT + 1]
        total = jnp.sum(count, axis=0, keepdims=True)
        average = jnp.sum(count * lines, axis=0, keepdims=True) / total
        off = lines - average
        square = jnp.sum(count * off * off, axis=0, keepdims=True) * plan.zs
        square += pltpu.roll(jnp.sum(lines, axis=0, keepdims=True), LANES - 1, 1)
        inverse = 1.0 / jnp.sqrt(square / (total * plan.zs) + EPSILON)
        for p in range(2):
            source = ready if j == 0 else parts
            quat = [spread_field(lines[:1], FIELD_QUAT + 4 * p + c) for c in range(4)]
            terms.append(
                (source.at[p, j], spread_field(average, 2 * p), spread_field(inverse, 2 * p), quat)
            )

    finish(incoming)

    def column(y):
        at = pl.ds(pl.multiple_of(y * xs, 8), xs)
        scores = [(ref[at, :] - average) * inverse for ref, average, inverse, _ in terms]
        high = functools.reduce(jnp.maximum, scores)
        high = jnp.maximum(high, pltpu.roll(high, ZF, 1))
        weights = [jnp.exp(score - high) for score in scores]
        sums = [functools.reduce(jnp.add, weights)]
        for c in range(4):
            sums.append(functools.reduce(jnp.add, [w * t[3][c] for w, t in zip(weights, terms)]))
        return [high] + [value + pltpu.roll(value, ZF, 1) for value in sums]

    def answer(j, carry):
        both = [jnp.where(low_half, a, b) for a, b in zip(column(2 * j), column(2 * j + 1))]
        base = pl.multiple_of(rot * (share * xs) + 2 * j * xs, 8)
        inside = jnp.where(
            low_half, marks[pl.ds(base, xs), :], marks[pl.ds(pl.multiple_of(base + xs, 8), xs), :]
        )
        high, total = both[0], both[1]
        lanes = pl.ds(pl.multiple_of(j * LANES, LANES), LANES)
        best[:, lanes] = inside * high
        evidence[:, lanes] = inside * (high + jnp.log(total))
        ratio = inside / total
        for c in range(4):
            moments[c, :, lanes] = both[2 + c] * ratio
        return carry

    lax.fori_loop(0, share // 2 // 5, unrolled(answer, 5), 0)


def matched(plan, tiles, groups, own, block, valid, quats, rot_index):
    ring_z = tiles // (CORES * RING_X)
    order = (
        np.arange(TEMPL // ring_z)[:, None] + (TEMPL // ring_z) * np.arange(ring_z)[None]
    ).reshape(-1)
    z_table = plan.tmpl_z()
    tables = [
        row_stack(plan.slab_z()),
        stacked_table(plan.folded(plan.kx, plan.kxp, np.arange(plan.lx), plan.lx)),
        stacked_table(plan.folded(plan.ky, plan.kyp, np.arange(plan.ys), plan.ly)),
        row_stack(z_table),
        stacked_table(plan.folded(plan.kx, plan.kxp, order, plan.lx)),
        stacked_table(plan.folded(plan.ky, plan.kyp, np.arange(TEMPL) - HALF, plan.ly)),
        paired_table(plan.inverse_rows(np.arange(plan.ys), plan.ky, plan.ly, plan.kyp, 2 * plan.kyp)),
        row_tables(plan.inverse_rows(np.arange(plan.xs), plan.kx, plan.lx, plan.kxc, plan.kxi)),
        col_tables(plan.inverse_z()),
    ]
    spots, first = [], 0
    for table in tables:
        spots.append((first, table.shape[0], table.shape[1]))
        first += table.shape[0]
    tables = [
        np.concatenate([padded_cols(table, 2 * LANES) for table in tables], axis=0),
        z_table.sum(axis=0, keepdims=True).astype(np.float32),
        np.kron(np.eye(2), np.ones((ZF, ZF))).astype(np.float32),
    ]
    share = plan.ys // groups * plan.xs
    copies = 2 * HALO_PARTS + ring_z + 2 * RING_X - 2 + ring_z * CORES + RING_X * groups - 2
    vmem = pl.BlockSpec(memory_space=pltpu.VMEM)
    flat_out = jax.ShapeDtypeStruct((plan.xs, plan.ys // groups * plan.zs), F32)
    return pl.pallas_call(
        functools.partial(match_kernel, plan, tiles, groups, spots),
        out_shape=[flat_out, flat_out, jax.ShapeDtypeStruct((4,) + flat_out.shape, F32)],
        in_specs=[vmem] * 4
        + [pl.BlockSpec(memory_space=pltpu.SMEM)]
        + [vmem] * len(tables),
        out_specs=[vmem] * 3,
        scratch_shapes=[
            pltpu.VMEM((2, groups, share, LANES), F32),
            pltpu.VMEM((groups, RING_X, ring_z * CORES, 1, LANES), F32),
            pltpu.VMEM(own.shape, BF16),
            pltpu.VMEM(own.shape, BF16),
            pltpu.VMEM((CORES, RING_X, ring_z) + block.shape, BF16),
            pltpu.VMEM((plan.kxc, 2, 2, plan.kyp, 2 * LANES), F32),
            pltpu.VMEM((plan.ys * 2 * plan.kxp, LANES), F32),
            pltpu.VMEM((2, tiles * BLOCK, LANES), F32),
            pltpu.VMEM((2, TEMPL * 2 * plan.kxp, LANES), F32),
            pltpu.VMEM((2, plan.kxi * plan.ys, LANES), F32),
            pltpu.VMEM((plan.ys * plan.xs, LANES), F32),
            pltpu.VMEM((2, groups, share, LANES), F32),
            pltpu.VMEM((1, LANES), F32),
            pltpu.SemaphoreType.DMA((copies,)),
            pltpu.SemaphoreType.DMA((copies,)),
            pltpu.SemaphoreType.DMA((2, groups)),
            pltpu.SemaphoreType.DMA((2, groups)),
        ],
        compiler_params=pltpu.CompilerParams(
            collective_id=0, has_side_effects=True, vmem_limit_bytes=48 << 20
        ),
        name="match",
    )(own, block, valid, quats, rot_index, *tables)


def row_stack(table):
    return np.concatenate(halves(table), axis=0)


def local(tomogram, templates, valid, quats, rot_index):
    xs, voxels = tomogram.shape
    ys = valid.shape[1]
    zs = voxels // ys
    plan = Plan(xs, ys, zs)
    tiles, groups = lax.axis_size("tile"), lax.axis_size("rot")
    per = templates.shape[1] // TEMPL
    block = templates.reshape(2, 2, per, TEMPL).transpose(0, 2, 1, 3)
    block = jnp.pad(block, ((0, 0), (0, 0), (0, 0), (0, ZF - TEMPL))).reshape(2 * per, LANES)
    block = jnp.pad(block, ((0, BLOCK - 2 * per), (0, 0)))
    return tuple(matched(plan, tiles, groups, tomogram, block, valid, quats, rot_index))


def solution(mesh):
    placed = (P("tile", None), P("rot", "tile"), P("tile", None), P(), P("rot"))
    return jax.shard_map(
        local,
        mesh=mesh,
        in_specs=placed,
        out_specs=(P("tile", "rot"), P("tile", "rot"), P(None, "tile", "rot")),
        check_vma=False,
    )
```

```python
import functools
import math

import jax
import jax.numpy as jnp
import ml_dtypes
import numpy as np
from jax import lax
from jax.experimental import pallas as pl
from jax.experimental.pallas import tpu as pltpu
from jax.sharding import PartitionSpec as P

TEMPL = 48
HALF = 24
EPSILON = 1e-06
LANES = 128
ZF = 64
CORES = 2
RING_X = 4
BLOCK = 80
HALO_PARTS = 4
MESH = pl.DeviceIdType.MESH
FIELD_COUNT = 4
FIELD_QUAT = 5
F32 = jnp.float32
BF16 = jnp.bfloat16


def halves(table):
    high = table.astype(np.float32).astype(ml_dtypes.bfloat16)
    low = (table - high.astype(np.float64)).astype(np.float32).astype(ml_dtypes.bfloat16)
    return high, low


def row_tables(table):
    high, low = halves(table)
    return np.concatenate([high, low], axis=0)


def col_tables(table):
    high, low = halves(table)
    return np.concatenate([high, low], axis=1)


def phases(rows, cols, length):
    index = np.outer(np.asarray(rows), np.asarray(cols)) % length
    return index * (2.0 * np.pi / length)


def padded_rows(table, rows):
    return np.pad(table, ((0, rows - table.shape[0]), (0, 0)))


def padded_cols(table, cols):
    return np.pad(table, ((0, 0), (0, cols - table.shape[1])))


def up8(n):
    return -(-n // 8) * 8


class Plan:
    def __init__(self, xs, ys, zs):
        self.xs, self.ys, self.zs = xs, ys, zs
        self.lx, self.ly, self.lz = xs + TEMPL, ys + HALF, zs + HALF
        self.kx, self.ky, self.kz = self.lx // 2 + 1, self.ly // 2 + 1, self.lz // 2 + 1
        self.kxp, self.kyp = up8(self.kx), up8(self.ky)
        self.kxu = -(-self.kx // 2) * 2
        self.kxc = -(-self.kx // 4) * 4
        self.kxi = 2 * self.kxc

    def folded(self, count, pad, points, length):
        angle = phases(np.arange(count), points, length)
        return np.concatenate(
            [padded_rows(np.cos(angle), pad), padded_rows(np.sin(angle), pad)], axis=0
        )

    def slab_z(self):
        angle = phases(np.arange(self.zs), np.arange(self.kz), self.lz)
        cos = padded_cols(np.cos(angle), ZF)
        sin = padded_cols(-np.sin(angle), ZF)
        one = np.concatenate([cos, sin], axis=1)
        return np.kron(np.eye(2), one)

    def tmpl_z(self):
        angle = phases(np.arange(TEMPL) - HALF, np.arange(self.kz), self.lz)
        cos = np.zeros((ZF, ZF))
        sin = np.zeros((ZF, ZF))
        cos[:TEMPL, : self.kz] = np.cos(angle)
        sin[:TEMPL, : self.kz] = np.sin(angle)
        none = np.zeros_like(cos)
        return np.block([[cos, none, sin, none], [none, cos, none, sin]])

    def inverse_rows(self, points, count, length, k_pad, tail):
        angle = phases(points, np.arange(count), length)
        weight = np.full((1, count), 1.0 / length)
        weight[0, 0] *= 0.5
        weight[0, count - 1] *= 0.5
        cos = padded_cols(np.cos(angle) * weight, k_pad)
        sin = padded_cols(np.sin(angle) * weight, k_pad)
        return padded_cols(np.concatenate([cos, sin], axis=1), tail)

    def inverse_z(self):
        angle = phases(np.arange(self.kz), np.arange(self.zs), self.lz)
        weight = np.full((self.kz, 1), 2.0 / self.lz)
        weight[0] *= 0.5
        weight[self.kz - 1] *= 0.5
        cos = padded_rows(np.cos(angle) * weight, ZF)
        sin = padded_rows(-np.sin(angle) * weight, ZF)
        none = np.zeros_like(cos)
        return np.block([[cos, none], [none, cos], [sin, none], [none, sin]])


def unrolled(body, count):
    def many(i, carry):
        return lax.fori_loop(0, count, lambda part, c: body(i * count + part, c), carry, unroll=True)

    return many


def split(value):
    high = value.astype(BF16)
    return high, (value - high.astype(F32)).astype(BF16)


def mm(left, right):
    return jnp.dot(left, right, preferred_element_type=F32)


def rows_product(table, value):
    count = table.shape[0] // 2
    high, low = split(value)
    both = mm(table, high)
    return both[:count] + both[count:] + mm(table[:count], low)


def stacked_table(table):
    high, low = halves(table)
    return np.concatenate([high, high, low], axis=1)


def stacked_product(table, value):
    high, low = split(value)
    return mm(table, jnp.concatenate([high, low, high], axis=0))


def paired_table(table):
    high, low = halves(table)
    return np.block([[high, high], [low, np.zeros_like(low)]])


def paired_product(table, value):
    high, low = split(value)
    count = table.shape[0] // 2
    both = mm(table, jnp.concatenate([high, low], axis=0))
    return both[:count] + both[count:]


def plus_minus(folded, count, sign):
    cos_re, cos_im = folded[:count, :LANES], folded[:count, LANES:]
    sin_re, sin_im = folded[count:, :LANES], folded[count:, LANES:]
    first = (cos_re - sin_im, cos_im + sin_re)
    second = (cos_re + sin_im, cos_im - sin_re)
    return (first, second) if sign > 0 else (second, first)


def exact(left, right):
    return jnp.dot(left, right, precision=lax.Precision.HIGHEST, preferred_element_type=F32)


def tall_sum(value):
    return jnp.sum(value.reshape(-1, 8, value.shape[-1]), axis=0)


def tile_of(z, x, core):
    return (z * RING_X + x) * CORES + core


def greet(peers):
    barrier = pltpu.get_barrier_semaphore()
    for peer in peers:
        pl.semaphore_signal(barrier, inc=1, device_id=peer, device_id_type=MESH)
    pl.semaphore_wait(barrier, len(peers))


def remote(source, target, sends, receives, index, peer):
    return pltpu.make_async_remote_copy(
        src_ref=source,
        dst_ref=target,
        send_sem=sends.at[index],
        recv_sem=receives.at[index],
        device_id=peer,
        device_id_type=MESH,
    )


def begin(source, target, sends, receives, first, peers):
    copies = [
        remote(source, target, sends, receives, first + index, peer)
        for index, peer in enumerate(peers)
    ]
    for copy in copies:
        copy.start()
    return copies


def finish(copies):
    for copy in copies:
        copy.wait()


def packed_sides(folded, count, low_half):
    cos, sin = folded[:count], folded[count:]
    swapped = pltpu.roll(sin, ZF, 1)
    turned = jnp.where(low_half, swapped, -swapped)
    return cos + turned, cos - turned


def match_kernel(
    plan, tiles, groups, spots, own_far, block, valid, quats, rot_index, packed_far, zsum, ones, best, evidence, moments, parts,
    stats, low, high, bank, spectrum, slab_mid, zed, mid, back, marks, ready, row, sends,
    receives, part_sends, part_receives, own, packed, load_sems,
):
    loads = [
        pltpu.make_async_copy(packed_far, packed, load_sems.at[0]),
        pltpu.make_async_copy(own_far, own, load_sems.at[1]),
    ]
    for load in loads:
        load.start()
    slab_z, slab_x, slab_y, table_z, table_x, table_y, table_yi, table_xi, table_zi = [
        packed.at[first : first + tall, :wide] for first, tall, wide in spots
    ]
    ring_z = tiles // (CORES * RING_X)
    plane_size = RING_X * CORES
    kxp, kyp, ys, xs = plan.kxp, plan.kyp, plan.ys, plan.xs
    rows = 2 * kxp
    tile, rot = lax.axis_index("tile"), lax.axis_index("rot")
    core = lax.rem(tile, CORES)
    x = lax.rem(tile // CORES, RING_X)
    z = tile // (CORES * RING_X)
    z_peers = [{"tile": tile_of(lax.rem(z + d, ring_z), x, core)} for d in range(1, ring_z)]
    x_peers = [{"tile": tile_of(z, lax.rem(x + d, RING_X), core)} for d in range(1, RING_X)]
    other = {"tile": tile_of(z, x, 1 - core)}
    line_size, sheet_size = ring_z * CORES, RING_X * groups
    line_peers, sheet_peers = [], []
    for d in range(1, line_size):
        there = lax.rem(z * CORES + core + d, line_size)
        line_peers.append({"tile": tile_of(there // CORES, x, lax.rem(there, CORES))})
    for d in range(1, sheet_size):
        there = lax.rem(x * groups + rot + d, sheet_size)
        sheet_peers.append(
            {"tile": tile_of(z, there // groups, core), "rot": lax.rem(there, groups)}
        )
    after = {"tile": lax.rem(tile + 1, tiles)}
    before = {"tile": lax.rem(tile + tiles - 1, tiles)}
    low_half = lax.broadcasted_iota(jnp.int32, (1, LANES), 1) < ZF
    width = ys * plan.zs // HALO_PARTS
    first_halo, first_z = 0, 2 * HALO_PARTS
    first_x = first_z + ring_z - 1
    first_pass = first_x + RING_X
    first_stats = first_pass + RING_X - 1

    bank[core, x, z] = block[...]
    for k in range(plan.kxu, plan.kxc):
        for side in range(2):
            first = (k + side * plan.kxc) * ys
            back[:, first : first + ys, :] = jnp.zeros((2, ys, LANES), F32)
    greet([after, before] + line_peers + sheet_peers)

    def halo(q):
        lanes = pl.ds(pl.multiple_of(q * width, LANES), width)
        return [
            remote(own_far.at[:, lanes], low.at[:, lanes], sends, receives, first_halo + 2 * q, after),
            remote(own_far.at[:, lanes], high.at[:, lanes], sends, receives, first_halo + 2 * q + 1, before),
        ]

    mine = bank.at[core, x, z]
    copies = begin(mine, mine, sends, receives, first_z, z_peers)
    for q in range(HALO_PARTS):
        for copy in halo(q):
            copy.start()

    flags = valid[...].astype(F32)
    columns = jnp.sum(flags)
    for y in range(ys):
        marks[y * xs : y * xs + xs, :] = jnp.broadcast_to(flags[:, y : y + 1], (xs, LANES))
    field = lax.rem(lax.broadcasted_iota(jnp.int32, (1, LANES), 1), ZF)
    line = jnp.where(field == FIELD_COUNT, columns, 0.0)
    entry = lax.broadcasted_iota(jnp.int32, quats.shape, 1)
    for r in range(4):
        found = jnp.sum(jnp.where(entry == rot_index[r], quats[...], 0.0), axis=1, keepdims=True)
        half = low_half if r % 2 == 0 else jnp.logical_not(low_half)
        for c in range(4):
            here = jnp.logical_and(field == FIELD_QUAT + 4 * (r // 2) + c, half)
            line = jnp.where(here, found[c : c + 1], line)
    row[...] = line
    for load in loads:
        load.wait()

    several = 5

    def slab_first(first):
        blocks = []
        for t in range(several):
            lanes = pl.ds(pl.multiple_of((first + t) * LANES, LANES), LANES)
            blocks += [
                jnp.where(tile > 0, low[:, lanes].astype(F32)[xs - HALF :], 0.0),
                own[:, lanes].astype(F32),
                jnp.where(tile < tiles - 1, high[:, lanes].astype(F32)[:HALF], 0.0),
            ]
        block = jnp.concatenate(blocks, axis=0).astype(BF16)
        strips = mm(jnp.concatenate([block, block], axis=1), slab_z[...])
        for t in range(several):
            folded = stacked_product(slab_x[...], strips[t * plan.lx : t * plan.lx + plan.lx])
            for part in range(2):
                sides = packed_sides(folded[:, part * LANES : part * LANES + LANES], kxp, low_half)
                to = pl.multiple_of((2 * (first + t) + part) * rows, 8)
                for s in range(2):
                    slab_mid[pl.ds(pl.multiple_of(to + s * kxp, 8), kxp), :] = sides[s]

    pieces = ys // 2 // HALO_PARTS

    def slab_part(q, carry):
        for copy in halo(q):
            copy.wait()

        def body(i, inner):
            slab_first(q * pieces + i * several)
            return inner

        return lax.fori_loop(0, pieces // several, body, carry)

    finish(copies)
    mine = bank.at[core, x]
    copies = begin(mine, mine, sends, receives, first_x, x_peers + [other])
    lax.fori_loop(0, HALO_PARTS, slab_part, 0)

    def slab_second(k, carry):
        lines = [slab_mid[pl.ds(k + s * kxp, ys, stride=rows), :] for s in range(2)]
        folded = stacked_product(slab_y[...], jnp.concatenate(lines, axis=1))
        for s in range(2):
            lanes = slice(s * LANES, s * LANES + LANES)
            cos, sin = folded[:kyp, lanes], folded[kyp:, lanes]
            cos_turned, sin_turned = pltpu.roll(cos, ZF, 1), pltpu.roll(sin, ZF, 1)
            for u in range(2):
                re_low, im_high = cos + sin_turned, cos - sin_turned
                im_low, re_high = cos_turned - sin, cos_turned + sin
                if u == 1:
                    re_low, im_high = im_high, re_low
                    im_low, re_high = re_high, im_low
                spectrum[k, s, u, :, :LANES] = jnp.where(low_half, re_low, re_high)
                spectrum[k, s, u, :, LANES:] = jnp.where(low_half, im_low, im_high)
        return carry

    trips = plan.kxu // 21
    lax.fori_loop(0, trips // 2, unrolled(slab_second, 21), 0)
    forwards = []
    for d in range(1, RING_X):
        copies[d - 1].wait()
        mine = bank.at[core, lax.rem(x + RING_X - d, RING_X)]
        forward = remote(mine, mine, sends, receives, first_pass + d - 1, other)
        forward.start()
        forwards.append(forward)
    lax.fori_loop(trips // 2, trips, unrolled(slab_second, 21), 0)
    copies[-1].wait()
    finish(forwards)

    per = TEMPL * TEMPL // tiles
    total = float(TEMPL**3)
    lane = lax.broadcasted_iota(jnp.int32, (BLOCK, LANES), 1)
    place = lax.broadcasted_iota(jnp.int32, (BLOCK, LANES), 0)
    used = jnp.logical_and(lax.rem(lane, ZF) < TEMPL, place < 2 * per)[None]
    tall = ring_z * BLOCK

    def lane_groups(value):
        wide = jnp.broadcast_to(jnp.sum(value, axis=0, keepdims=True), (8, LANES))
        return exact(wide, ones[...])[:1]

    def both_pairs(value):
        first = lane_groups(jnp.where(place < per, value, 0.0))
        second = lane_groups(jnp.where(place < per, 0.0, value))
        return first, second

    def bank_rows(i):
        return bank[i // RING_X, lax.rem(i, RING_X)]

    def add_up(i, carry):
        return carry + jnp.sum(bank_rows(i).astype(F32), axis=0)

    empty = jnp.zeros((BLOCK, LANES), F32)
    means = both_pairs(lax.fori_loop(0, plane_size, add_up, empty))
    means = [mean / total for mean in means]
    mean_rows = jnp.where(place < per, means[0], means[1])[None]

    def add_squares(i, carry):
        off = jnp.where(used, bank_rows(i).astype(F32) - mean_rows, 0.0)
        return carry + jnp.sum(off * off, axis=0)

    squares = both_pairs(lax.fori_loop(0, plane_size, add_squares, empty))
    factors = [
        1.0 / (jnp.sqrt(square / total + EPSILON) * float(TEMPL) ** 1.5) for square in squares
    ]
    scale_rows = jnp.where(place < per, factors[0], factors[1])[None]

    def z_stage(i, carry):
        lines = bank_rows(i).reshape(tall, LANES)
        value = mm(jnp.concatenate([lines, lines], axis=1), table_z[...])
        at = pl.ds(pl.multiple_of(i * tall, tall), tall)
        for part in range(2):
            lanes = slice(part * LANES, part * LANES + LANES)
            side = value[:, lanes].reshape(ring_z, BLOCK, LANES)
            side = (side - mean_rows * zsum[:, lanes]) * scale_rows
            zed[part, at, :] = side.reshape(tall, LANES)
        return carry

    lax.fori_loop(0, plane_size, z_stage, 0)
    share = ys // groups
    step = share
    piece = per // 3

    def pair(p, outer):
        def x_stage(g, carry):
            starts = []
            for s in range(TEMPL // ring_z):
                m = s * (TEMPL // piece) + g
                owner = m // 3
                there = lax.rem(owner, CORES) * RING_X + owner // CORES
                starts.append(there * tall + p * per + lax.rem(m, 3) * piece)
            for t in range(piece):
                lines = []
                for start in starts:
                    at = pl.ds(start + t, ring_z, stride=BLOCK)
                    lines.append(jnp.concatenate([zed[0, at, :], zed[1, at, :]], axis=1))
                folded = stacked_product(table_x[...], jnp.concatenate(lines, axis=0))
                to = pl.multiple_of((g * piece + t) * rows, 8)
                for s, (re, im) in enumerate(plus_minus(folded, kxp, 1)):
                    at = pl.ds(pl.multiple_of(to + s * kxp, 8), kxp)
                    mid[0, at, :] = re
                    mid[1, at, :] = im
            return carry

        lax.fori_loop(0, TEMPL // piece, x_stage, 0)

        def y_stage(k, carry):
            found = []
            for s in range(2):
                at = pl.ds(k + s * kxp, TEMPL, stride=rows)
                value = jnp.concatenate([mid[0, at, :], mid[1, at, :]], axis=1)
                folded = stacked_product(table_y[...], value)
                sides = []
                for u, (re, im) in enumerate(plus_minus(folded, kyp, 1)):
                    slab_re = spectrum[k, s, u, :, :LANES]
                    slab_im = spectrum[k, s, u, :, LANES:]
                    sides.append((re * slab_re - im * slab_im, re * slab_im + im * slab_re))
                (re_p, im_p), (re_m, im_m) = sides
                even = jnp.concatenate([re_p + re_m, im_p + im_m], axis=1)
                odd = jnp.concatenate([im_m - im_p, re_p - re_m], axis=1)
                found.append(paired_product(table_yi[...], jnp.concatenate([even, odd], axis=0)))
            even = found[0] + found[1]
            odd = found[0] - found[1]
            to = pl.ds(pl.multiple_of(k * ys, 8), ys)
            back[0, to, :] = even[:, :LANES]
            back[1, to, :] = even[:, LANES:]
            to = pl.ds(pl.multiple_of((k + plan.kxc) * ys, 8), ys)
            back[0, to, :] = -odd[:, LANES:]
            back[1, to, :] = odd[:, :LANES]
            return carry

        lax.fori_loop(0, plan.kxu // 21, unrolled(y_stage, 21), 0)

        def last(i, lane_sum):
            j = lax.rem(2 + 3 * i + 3 * (i * (i - 1) // 2), groups)
            base = lax.rem(rot + j, groups) * share
            lines = []
            for y in range(step):
                at = pl.ds(base + y, plan.kxi, stride=ys)
                value = jnp.concatenate([back[0, at, :], back[1, at, :]], axis=1)
                lines.append(rows_product(table_xi[...], value))
            upper, lower = split(jnp.concatenate(lines, axis=0))
            both = mm(upper, table_zi[...])
            value = both[:, :LANES] + both[:, LANES:] + mm(lower, table_zi[:, :LANES])
            ready[p, j] = value

            @pl.when(j > 0)
            def _():
                send_part(p, j).start()

            mark = marks[pl.ds(pl.multiple_of(base * xs, 8), share * xs), :]
            return lane_sum + tall_sum(value * mark)

        def send_part(p, j):
            return pltpu.make_async_remote_copy(
                src_ref=ready.at[p, j],
                dst_ref=parts.at[p, j],
                send_sem=part_sends.at[p, j],
                recv_sem=part_receives.at[p, j],
                device_id={"rot": lax.rem(rot + j, groups)},
                device_id_type=MESH,
            )

        lane_sum = lax.fori_loop(0, groups, last, jnp.zeros((8, LANES), F32))
        lane_mean = jnp.sum(lane_sum, axis=0, keepdims=True) / jnp.maximum(columns, 1.0)

        def add_off(j, carry):
            base = lax.rem(rot + j, groups) * (share * xs)
            mark = marks[pl.ds(pl.multiple_of(base, 8), share * xs), :]
            off = ready[p, j] - lane_mean
            return carry + tall_sum(off * off * mark)

        lane_square = lax.fori_loop(0, groups, add_off, jnp.zeros((8, LANES), F32))
        wide = jnp.broadcast_to(lane_mean, (8, LANES))
        part_mean = exact(wide, ones[...])[:1] / float(plan.zs)
        off = lane_mean - part_mean
        lane_square = jnp.sum(lane_square, axis=0, keepdims=True) + columns * off * off
        part_square = exact(jnp.broadcast_to(lane_square, (8, LANES)), ones[...])[:1]
        now = jnp.where(field == 2 * p, part_mean, row[...])
        row[...] = jnp.where(field == 2 * p + 1, part_square, now)
        return outer

    lax.fori_loop(0, 2, pair, 0)
    place = z * CORES + core
    stats[rot, x, place] = row[...]
    mine = stats.at[rot, x, place]
    finish(begin(mine, mine, sends, receives, first_stats, line_peers))
    mine = stats.at[rot, x]
    finish(begin(mine, mine, sends, receives, first_stats + line_size - 1, sheet_peers))
    incoming = [
        remote(ready.at[p, j], parts.at[p, j], part_sends.at[p], part_receives.at[p], j, {"rot": lax.rem(rot + j, groups)})
        for p in range(2)
        for j in range(1, groups)
    ]

    def spread_field(lines, index):
        return jnp.where(
            low_half, lines[:, index : index + 1], lines[:, ZF + index : ZF + index + 1]
        )

    terms = []
    for j in range(groups):
        group = lax.rem(rot + groups - j, groups)
        lines = stats[group].reshape(-1, LANES)
        count = lines[:, FIELD_COUNT : FIELD_COUNT + 1]
        total = jnp.sum(count, axis=0, keepdims=True)
        average = jnp.sum(count * lines, axis=0, keepdims=True) / total
        off = lines - average
        square = jnp.sum(count * off * off, axis=0, keepdims=True) * plan.zs
        square += pltpu.roll(jnp.sum(lines, axis=0, keepdims=True), LANES - 1, 1)
        inverse = 1.0 / jnp.sqrt(square / (total * plan.zs) + EPSILON)
        for p in range(2):
            source = ready if j == 0 else parts
            quat = [spread_field(lines[:1], FIELD_QUAT + 4 * p + c) for c in range(4)]
            terms.append(
                (source.at[p, j], spread_field(average, 2 * p), spread_field(inverse, 2 * p), quat)
            )

    finish(incoming)

    def column(y):
        at = pl.ds(pl.multiple_of(y * xs, 8), xs)
        scores = [(ref[at, :] - average) * inverse for ref, average, inverse, _ in terms]
        high = functools.reduce(jnp.maximum, scores)
        high = jnp.maximum(high, pltpu.roll(high, ZF, 1))
        weights = [jnp.exp(score - high) for score in scores]
        sums = [functools.reduce(jnp.add, weights)]
        for c in range(4):
            sums.append(functools.reduce(jnp.add, [w * t[3][c] for w, t in zip(weights, terms)]))
        return [high] + [value + pltpu.roll(value, ZF, 1) for value in sums]

    def answer(j, carry):
        both = [jnp.where(low_half, a, b) for a, b in zip(column(2 * j), column(2 * j + 1))]
        base = pl.multiple_of(rot * (share * xs) + 2 * j * xs, 8)
        inside = jnp.where(
            low_half, marks[pl.ds(base, xs), :], marks[pl.ds(pl.multiple_of(base + xs, 8), xs), :]
        )
        high, total = both[0], both[1]
        lanes = pl.ds(pl.multiple_of(j * LANES, LANES), LANES)
        best[:, lanes] = inside * high
        evidence[:, lanes] = inside * (high + jnp.log(total))
        ratio = inside / total
        for c in range(4):
            moments[c, :, lanes] = both[2 + c] * ratio
        return carry

    lax.fori_loop(0, share // 2 // 5, unrolled(answer, 5), 0)


def matched(plan, tiles, groups, own, block, valid, quats, rot_index):
    ring_z = tiles // (CORES * RING_X)
    order = (
        np.arange(TEMPL // ring_z)[:, None] + (TEMPL // ring_z) * np.arange(ring_z)[None]
    ).reshape(-1)
    z_table = plan.tmpl_z()
    tables = [
        row_stack(plan.slab_z()),
        stacked_table(plan.folded(plan.kx, plan.kxp, np.arange(plan.lx), plan.lx)),
        stacked_table(plan.folded(plan.ky, plan.kyp, np.arange(plan.ys), plan.ly)),
        row_stack(z_table),
        stacked_table(plan.folded(plan.kx, plan.kxp, order, plan.lx)),
        stacked_table(plan.folded(plan.ky, plan.kyp, np.arange(TEMPL) - HALF, plan.ly)),
        paired_table(plan.inverse_rows(np.arange(plan.ys), plan.ky, plan.ly, plan.kyp, 2 * plan.kyp)),
        row_tables(plan.inverse_rows(np.arange(plan.xs), plan.kx, plan.lx, plan.kxc, plan.kxi)),
        col_tables(plan.inverse_z()),
    ]
    spots, first = [], 0
    for table in tables:
        spots.append((first, table.shape[0], table.shape[1]))
        first += table.shape[0]
    tables = [
        np.concatenate([padded_cols(table, 2 * LANES) for table in tables], axis=0),
        z_table.sum(axis=0, keepdims=True).astype(np.float32),
        np.kron(np.eye(2), np.ones((ZF, ZF))).astype(np.float32),
    ]
    share = plan.ys // groups * plan.xs
    copies = 2 * HALO_PARTS + ring_z + 2 * RING_X - 2 + ring_z * CORES + RING_X * groups - 2
    vmem = pl.BlockSpec(memory_space=pltpu.VMEM)
    far = pl.BlockSpec(memory_space=pltpu.HBM)
    flat_out = jax.ShapeDtypeStruct((plan.xs, plan.ys // groups * plan.zs), F32)
    return pl.pallas_call(
        functools.partial(match_kernel, plan, tiles, groups, spots),
        out_shape=[flat_out, flat_out, jax.ShapeDtypeStruct((4,) + flat_out.shape, F32)],
        in_specs=[far, vmem, vmem, vmem, pl.BlockSpec(memory_space=pltpu.SMEM), far, vmem, vmem],
        out_specs=[vmem] * 3,
        scratch_shapes=[
            pltpu.VMEM((2, groups, share, LANES), F32),
            pltpu.VMEM((groups, RING_X, ring_z * CORES, 1, LANES), F32),
            pltpu.VMEM(own.shape, BF16),
            pltpu.VMEM(own.shape, BF16),
            pltpu.VMEM((CORES, RING_X, ring_z) + block.shape, BF16),
            pltpu.VMEM((plan.kxc, 2, 2, plan.kyp, 2 * LANES), F32),
            pltpu.VMEM((plan.ys * 2 * plan.kxp, LANES), F32),
            pltpu.VMEM((2, tiles * BLOCK, LANES), F32),
            pltpu.VMEM((2, TEMPL * 2 * plan.kxp, LANES), F32),
            pltpu.VMEM((2, plan.kxi * plan.ys, LANES), F32),
            pltpu.VMEM((plan.ys * plan.xs, LANES), F32),
            pltpu.VMEM((2, groups, share, LANES), F32),
            pltpu.VMEM((1, LANES), F32),
            pltpu.SemaphoreType.DMA((copies,)),
            pltpu.SemaphoreType.DMA((copies,)),
            pltpu.SemaphoreType.DMA((2, groups)),
            pltpu.SemaphoreType.DMA((2, groups)),
            pltpu.VMEM(own.shape, BF16),
            pltpu.VMEM(tables[0].shape, BF16),
            pltpu.SemaphoreType.DMA((2,)),
        ],
        compiler_params=pltpu.CompilerParams(
            collective_id=0, has_side_effects=True, vmem_limit_bytes=52 << 20
        ),
        name="match",
    )(own, block, valid, quats, rot_index, *tables)


def row_stack(table):
    return np.concatenate(halves(table), axis=0)


def local(tomogram, templates, valid, quats, rot_index):
    xs, voxels = tomogram.shape
    ys = valid.shape[1]
    zs = voxels // ys
    plan = Plan(xs, ys, zs)
    tiles, groups = lax.axis_size("tile"), lax.axis_size("rot")
    per = templates.shape[1] // TEMPL
    block = templates.reshape(2, 2, per, TEMPL).transpose(0, 2, 1, 3)
    block = jnp.pad(block, ((0, 0), (0, 0), (0, 0), (0, ZF - TEMPL))).reshape(2 * per, LANES)
    block = jnp.pad(block, ((0, BLOCK - 2 * per), (0, 0)))
    return tuple(matched(plan, tiles, groups, tomogram, block, valid, quats, rot_index))


def solution(mesh):
    placed = (P("tile", None), P("rot", "tile"), P("tile", None), P(), P("rot"))
    return jax.shard_map(
        local,
        mesh=mesh,
        in_specs=placed,
        out_specs=(P("tile", "rot"), P("tile", "rot"), P(None, "tile", "rot")),
        check_vma=False,
    )
```

```python
import functools
import math

import jax
import jax.numpy as jnp
import ml_dtypes
import numpy as np
from jax import lax
from jax.experimental import pallas as pl
from jax.experimental.pallas import tpu as pltpu
from jax.sharding import PartitionSpec as P

TEMPL = 48
HALF = 24
EPSILON = 1e-06
LANES = 128
ZF = 64
CORES = 2
RING_X = 4
BLOCK = 80
HALO_PARTS = 4
MESH = pl.DeviceIdType.MESH
FIELD_COUNT = 4
FIELD_QUAT = 5
F32 = jnp.float32
BF16 = jnp.bfloat16


def halves(table):
    high = table.astype(np.float32).astype(ml_dtypes.bfloat16)
    low = (table - high.astype(np.float64)).astype(np.float32).astype(ml_dtypes.bfloat16)
    return high, low


def row_tables(table):
    high, low = halves(table)
    return np.concatenate([high, low], axis=0)


def col_tables(table):
    high, low = halves(table)
    return np.concatenate([high, low], axis=1)


def phases(rows, cols, length):
    index = np.outer(np.asarray(rows), np.asarray(cols)) % length
    return index * (2.0 * np.pi / length)


def padded_rows(table, rows):
    return np.pad(table, ((0, rows - table.shape[0]), (0, 0)))


def padded_cols(table, cols):
    return np.pad(table, ((0, 0), (0, cols - table.shape[1])))


def up8(n):
    return -(-n // 8) * 8


class Plan:
    def __init__(self, xs, ys, zs):
        self.xs, self.ys, self.zs = xs, ys, zs
        self.lx, self.ly, self.lz = xs + TEMPL, ys + HALF, zs + HALF
        self.kx, self.ky, self.kz = self.lx // 2 + 1, self.ly // 2 + 1, self.lz // 2 + 1
        self.kxp, self.kyp = up8(self.kx), up8(self.ky)
        self.kxu = -(-self.kx // 2) * 2
        self.kxc = -(-self.kx // 4) * 4
        self.kxi = 2 * self.kxc

    def folded(self, count, pad, points, length):
        angle = phases(np.arange(count), points, length)
        return np.concatenate(
            [padded_rows(np.cos(angle), pad), padded_rows(np.sin(angle), pad)], axis=0
        )

    def slab_z(self):
        angle = phases(np.arange(self.zs), np.arange(self.kz), self.lz)
        cos = padded_cols(np.cos(angle), ZF)
        sin = padded_cols(-np.sin(angle), ZF)
        one = np.concatenate([cos, sin], axis=1)
        return np.kron(np.eye(2), one)

    def tmpl_z(self):
        angle = phases(np.arange(TEMPL) - HALF, np.arange(self.kz), self.lz)
        cos = np.zeros((ZF, ZF))
        sin = np.zeros((ZF, ZF))
        cos[:TEMPL, : self.kz] = np.cos(angle)
        sin[:TEMPL, : self.kz] = np.sin(angle)
        none = np.zeros_like(cos)
        return np.block([[cos, none, sin, none], [none, cos, none, sin]])

    def inverse_rows(self, points, count, length, k_pad, tail):
        angle = phases(points, np.arange(count), length)
        weight = np.full((1, count), 1.0 / length)
        weight[0, 0] *= 0.5
        weight[0, count - 1] *= 0.5
        cos = padded_cols(np.cos(angle) * weight, k_pad)
        sin = padded_cols(np.sin(angle) * weight, k_pad)
        return padded_cols(np.concatenate([cos, sin], axis=1), tail)

    def inverse_z(self):
        angle = phases(np.arange(self.kz), np.arange(self.zs), self.lz)
        weight = np.full((self.kz, 1), 2.0 / self.lz)
        weight[0] *= 0.5
        weight[self.kz - 1] *= 0.5
        cos = padded_rows(np.cos(angle) * weight, ZF)
        sin = padded_rows(-np.sin(angle) * weight, ZF)
        none = np.zeros_like(cos)
        return np.block([[cos, none], [none, cos], [sin, none], [none, sin]])


def unrolled(body, count):
    def many(i, carry):
        return lax.fori_loop(0, count, lambda part, c: body(i * count + part, c), carry, unroll=True)

    return many


def split(value):
    high = value.astype(BF16)
    return high, (value - high.astype(F32)).astype(BF16)


def mm(left, right):
    return jnp.dot(left, right, preferred_element_type=F32)


def rows_product(table, value):
    count = table.shape[0] // 2
    high, low = split(value)
    both = mm(table, high)
    return both[:count] + both[count:] + mm(table[:count], low)


def stacked_table(table):
    high, low = halves(table)
    return np.concatenate([high, high, low], axis=1)


def stacked_product(table, value):
    high, low = split(value)
    return mm(table, jnp.concatenate([high, low, high], axis=0))


def paired_table(table):
    high, low = halves(table)
    return np.block([[high, high], [low, np.zeros_like(low)]])


def paired_product(table, value):
    high, low = split(value)
    count = table.shape[0] // 2
    both = mm(table, jnp.concatenate([high, low], axis=0))
    return both[:count] + both[count:]


def plus_minus(folded, count, sign):
    cos_re, cos_im = folded[:count, :LANES], folded[:count, LANES:]
    sin_re, sin_im = folded[count:, :LANES], folded[count:, LANES:]
    first = (cos_re - sin_im, cos_im + sin_re)
    second = (cos_re + sin_im, cos_im - sin_re)
    return (first, second) if sign > 0 else (second, first)


def exact(left, right):
    return jnp.dot(left, right, precision=lax.Precision.HIGHEST, preferred_element_type=F32)


def tall_sum(value):
    return jnp.sum(value.reshape(-1, 8, value.shape[-1]), axis=0)


def tile_of(z, x, core):
    return (z * RING_X + x) * CORES + core


def greet(peers):
    barrier = pltpu.get_barrier_semaphore()
    for peer in peers:
        pl.semaphore_signal(barrier, inc=1, device_id=peer, device_id_type=MESH)
    pl.semaphore_wait(barrier, len(peers))


def remote(source, target, sends, receives, index, peer):
    return pltpu.make_async_remote_copy(
        src_ref=source,
        dst_ref=target,
        send_sem=sends.at[index],
        recv_sem=receives.at[index],
        device_id=peer,
        device_id_type=MESH,
    )


def begin(source, target, sends, receives, first, peers):
    copies = [
        remote(source, target, sends, receives, first + index, peer)
        for index, peer in enumerate(peers)
    ]
    for copy in copies:
        copy.start()
    return copies


def finish(copies):
    for copy in copies:
        copy.wait()


def packed_sides(folded, count, low_half):
    cos, sin = folded[:count], folded[count:]
    swapped = pltpu.roll(sin, ZF, 1)
    turned = jnp.where(low_half, swapped, -swapped)
    return cos + turned, cos - turned


def match_kernel(
    plan, tiles, groups, spots, own_far, block, valid, quats, rot_index, packed_far, zsum, ones, best, evidence, moments, parts,
    stats, low, high, bank, spectrum, slab_mid, zed, mid, back, marks, ready, row, sends,
    receives, part_sends, part_receives, own, packed, load_sems,
):
    loads = [
        pltpu.make_async_copy(packed_far, packed, load_sems.at[0]),
        pltpu.make_async_copy(own_far, own, load_sems.at[1]),
    ]
    for load in loads:
        load.start()
    slab_z, slab_x, slab_y, table_z, table_x, table_y, table_yi, table_xi, table_zi = [
        packed.at[first : first + tall, :wide] for first, tall, wide in spots
    ]
    ring_z = tiles // (CORES * RING_X)
    plane_size = RING_X * CORES
    kxp, kyp, ys, xs = plan.kxp, plan.kyp, plan.ys, plan.xs
    rows = 2 * kxp
    tile, rot = lax.axis_index("tile"), lax.axis_index("rot")
    core = lax.rem(tile, CORES)
    x = lax.rem(tile // CORES, RING_X)
    z = tile // (CORES * RING_X)
    z_peers = [{"tile": tile_of(lax.rem(z + d, ring_z), x, core)} for d in range(1, ring_z)]
    x_peers = [{"tile": tile_of(z, lax.rem(x + d, RING_X), core)} for d in range(1, RING_X)]
    other = {"tile": tile_of(z, x, 1 - core)}
    line_size, sheet_size = ring_z * CORES, RING_X * groups
    line_peers, sheet_peers = [], []
    for d in range(1, line_size):
        there = lax.rem(z * CORES + core + d, line_size)
        line_peers.append({"tile": tile_of(there // CORES, x, lax.rem(there, CORES))})
    for d in range(1, sheet_size):
        there = lax.rem(x * groups + rot + d, sheet_size)
        sheet_peers.append(
            {"tile": tile_of(z, there // groups, core), "rot": lax.rem(there, groups)}
        )
    after = {"tile": lax.rem(tile + 1, tiles)}
    before = {"tile": lax.rem(tile + tiles - 1, tiles)}
    low_half = lax.broadcasted_iota(jnp.int32, (1, LANES), 1) < ZF
    width = ys * plan.zs // HALO_PARTS
    first_halo, first_z = 0, 2 * HALO_PARTS
    first_x = first_z + ring_z - 1
    first_pass = first_x + RING_X
    first_stats = first_pass + RING_X - 1

    bank[core, x, z] = block[...]
    for k in range(plan.kxu, plan.kxc):
        for side in range(2):
            first = (k + side * plan.kxc) * ys
            back[:, first : first + ys, :] = jnp.zeros((2, ys, LANES), F32)
    greet([after, before] + line_peers + sheet_peers)

    def halo(q):
        lanes = pl.ds(pl.multiple_of(q * width, LANES), width)
        return [
            remote(own_far.at[:, lanes], low.at[:, lanes], sends, receives, first_halo + 2 * q, after),
            remote(own_far.at[:, lanes], high.at[:, lanes], sends, receives, first_halo + 2 * q + 1, before),
        ]

    mine = bank.at[core, x, z]
    copies = begin(mine, mine, sends, receives, first_z, z_peers)
    for q in range(HALO_PARTS):
        for copy in halo(q):
            copy.start()

    flags = valid[...].astype(F32)
    columns = jnp.sum(flags)
    for y in range(ys):
        marks[y * xs : y * xs + xs, :] = jnp.broadcast_to(flags[:, y : y + 1], (xs, LANES))
    field = lax.rem(lax.broadcasted_iota(jnp.int32, (1, LANES), 1), ZF)
    line = jnp.where(field == FIELD_COUNT, columns, 0.0)
    entry = lax.broadcasted_iota(jnp.int32, quats.shape, 1)
    for r in range(4):
        found = jnp.sum(jnp.where(entry == rot_index[r], quats[...], 0.0), axis=1, keepdims=True)
        half = low_half if r % 2 == 0 else jnp.logical_not(low_half)
        for c in range(4):
            here = jnp.logical_and(field == FIELD_QUAT + 4 * (r // 2) + c, half)
            line = jnp.where(here, found[c : c + 1], line)
    row[...] = line
    for load in loads:
        load.wait()

    several = 5

    def slab_first(first):
        blocks = []
        for t in range(several):
            lanes = pl.ds(pl.multiple_of((first + t) * LANES, LANES), LANES)
            blocks += [
                jnp.where(tile > 0, low[:, lanes].astype(F32)[xs - HALF :], 0.0),
                own[:, lanes].astype(F32),
                jnp.where(tile < tiles - 1, high[:, lanes].astype(F32)[:HALF], 0.0),
            ]
        block = jnp.concatenate(blocks, axis=0).astype(BF16)
        strips = mm(jnp.concatenate([block, block], axis=1), slab_z[...])
        for t in range(several):
            folded = stacked_product(slab_x[...], strips[t * plan.lx : t * plan.lx + plan.lx])
            for part in range(2):
                sides = packed_sides(folded[:, part * LANES : part * LANES + LANES], kxp, low_half)
                to = pl.multiple_of((2 * (first + t) + part) * rows, 8)
                for s in range(2):
                    slab_mid[pl.ds(pl.multiple_of(to + s * kxp, 8), kxp), :] = sides[s]

    pieces = ys // 2 // HALO_PARTS

    def slab_part(q, carry):
        for copy in halo(q):
            copy.wait()

        def body(i, inner):
            slab_first(q * pieces + i * several)
            return inner

        return lax.fori_loop(0, pieces // several, body, carry)

    finish(copies)
    mine = bank.at[core, x]
    copies = begin(mine, mine, sends, receives, first_x, x_peers + [other])
    lax.fori_loop(0, HALO_PARTS, slab_part, 0)

    def slab_second(k, carry):
        lines = [slab_mid[pl.ds(k + s * kxp, ys, stride=rows), :] for s in range(2)]
        folded = stacked_product(slab_y[...], jnp.concatenate(lines, axis=1))
        for s in range(2):
            lanes = slice(s * LANES, s * LANES + LANES)
            cos, sin = folded[:kyp, lanes], folded[kyp:, lanes]
            cos_turned, sin_turned = pltpu.roll(cos, ZF, 1), pltpu.roll(sin, ZF, 1)
            for u in range(2):
                re_low, im_high = cos + sin_turned, cos - sin_turned
                im_low, re_high = cos_turned - sin, cos_turned + sin
                if u == 1:
                    re_low, im_high = im_high, re_low
                    im_low, re_high = re_high, im_low
                spectrum[k, s, u, :, :LANES] = jnp.where(low_half, re_low, re_high)
                spectrum[k, s, u, :, LANES:] = jnp.where(low_half, im_low, im_high)
        return carry

    trips = plan.kxu // 21
    lax.fori_loop(0, trips // 2, unrolled(slab_second, 21), 0)
    forwards = []
    for d in range(1, RING_X):
        copies[d - 1].wait()
        mine = bank.at[core, lax.rem(x + RING_X - d, RING_X)]
        forward = remote(mine, mine, sends, receives, first_pass + d - 1, other)
        forward.start()
        forwards.append(forward)
    lax.fori_loop(trips // 2, trips, unrolled(slab_second, 21), 0)
    copies[-1].wait()
    finish(forwards)

    per = TEMPL * TEMPL // tiles
    total = float(TEMPL**3)
    lane = lax.broadcasted_iota(jnp.int32, (BLOCK, LANES), 1)
    place = lax.broadcasted_iota(jnp.int32, (BLOCK, LANES), 0)
    used = jnp.logical_and(lax.rem(lane, ZF) < TEMPL, place < 2 * per)[None]
    tall = ring_z * BLOCK

    def lane_groups(value):
        wide = jnp.broadcast_to(jnp.sum(value, axis=0, keepdims=True), (8, LANES))
        return exact(wide, ones[...])[:1]

    def both_pairs(value):
        first = lane_groups(jnp.where(place < per, value, 0.0))
        second = lane_groups(jnp.where(place < per, 0.0, value))
        return first, second

    def bank_rows(i):
        return bank[i // RING_X, lax.rem(i, RING_X)]

    def add_up(i, carry):
        return carry + jnp.sum(bank_rows(i).astype(F32), axis=0)

    empty = jnp.zeros((BLOCK, LANES), F32)
    means = both_pairs(lax.fori_loop(0, plane_size, add_up, empty))
    means = [mean / total for mean in means]
    mean_rows = jnp.where(place < per, means[0], means[1])[None]

    def add_squares(i, carry):
        off = jnp.where(used, bank_rows(i).astype(F32) - mean_rows, 0.0)
        return carry + jnp.sum(off * off, axis=0)

    squares = both_pairs(lax.fori_loop(0, plane_size, add_squares, empty))
    factors = [
        1.0 / (jnp.sqrt(square / total + EPSILON) * float(TEMPL) ** 1.5) for square in squares
    ]
    scale_rows = jnp.where(place < per, factors[0], factors[1])[None]

    def z_stage(i, carry):
        lines = bank_rows(i).reshape(tall, LANES)
        value = mm(jnp.concatenate([lines, lines], axis=1), table_z[...])
        at = pl.ds(pl.multiple_of(i * tall, tall), tall)
        for part in range(2):
            lanes = slice(part * LANES, part * LANES + LANES)
            side = value[:, lanes].reshape(ring_z, BLOCK, LANES)
            side = (side - mean_rows * zsum[:, lanes]) * scale_rows
            zed[part, at, :] = side.reshape(tall, LANES)
        return carry

    lax.fori_loop(0, plane_size, z_stage, 0)
    share = ys // groups
    step = share
    piece = per // 3

    def pair(p, outer):
        def x_stage(g, carry):
            starts = []
            for s in range(TEMPL // ring_z):
                m = s * (TEMPL // piece) + g
                owner = m // 3
                there = lax.rem(owner, CORES) * RING_X + owner // CORES
                starts.append(there * tall + p * per + lax.rem(m, 3) * piece)
            for t in range(piece):
                lines = []
                for start in starts:
                    at = pl.ds(start + t, ring_z, stride=BLOCK)
                    lines.append(jnp.concatenate([zed[0, at, :], zed[1, at, :]], axis=1))
                folded = stacked_product(table_x[...], jnp.concatenate(lines, axis=0))
                to = pl.multiple_of((g * piece + t) * rows, 8)
                for s, (re, im) in enumerate(plus_minus(folded, kxp, 1)):
                    at = pl.ds(pl.multiple_of(to + s * kxp, 8), kxp)
                    mid[0, at, :] = re
                    mid[1, at, :] = im
            return carry

        lax.fori_loop(0, TEMPL // piece, x_stage, 0)

        def y_stage(k, carry):
            found = []
            for s in range(2):
                at = pl.ds(k + s * kxp, TEMPL, stride=rows)
                value = jnp.concatenate([mid[0, at, :], mid[1, at, :]], axis=1)
                folded = stacked_product(table_y[...], value)
                sides = []
                for u, (re, im) in enumerate(plus_minus(folded, kyp, 1)):
                    slab_re = spectrum[k, s, u, :, :LANES]
                    slab_im = spectrum[k, s, u, :, LANES:]
                    sides.append((re * slab_re - im * slab_im, re * slab_im + im * slab_re))
                (re_p, im_p), (re_m, im_m) = sides
                even = jnp.concatenate([re_p + re_m, im_p + im_m], axis=1)
                odd = jnp.concatenate([im_m - im_p, re_p - re_m], axis=1)
                found.append(paired_product(table_yi[...], jnp.concatenate([even, odd], axis=0)))
            even = found[0] + found[1]
            odd = found[0] - found[1]
            to = pl.ds(pl.multiple_of(k * ys, 8), ys)
            back[0, to, :] = even[:, :LANES]
            back[1, to, :] = even[:, LANES:]
            to = pl.ds(pl.multiple_of((k + plan.kxc) * ys, 8), ys)
            back[0, to, :] = -odd[:, LANES:]
            back[1, to, :] = odd[:, :LANES]
            return carry

        lax.fori_loop(0, plan.kxu // 21, unrolled(y_stage, 21), 0)

        def last(i, lane_sum):
            j = lax.rem(2 + 3 * i + 3 * (i * (i - 1) // 2), groups)
            base = lax.rem(rot + j, groups) * share
            lines = []
            for y in range(step):
                at = pl.ds(base + y, plan.kxi, stride=ys)
                value = jnp.concatenate([back[0, at, :], back[1, at, :]], axis=1)
                lines.append(rows_product(table_xi[...], value))
            upper, lower = split(jnp.concatenate(lines, axis=0))
            both = mm(upper, table_zi[...])
            value = both[:, :LANES] + both[:, LANES:] + mm(lower, table_zi[:, :LANES])
            ready[p, j] = value

            @pl.when(j > 0)
            def _():
                send_part(p, j).start()

            mark = marks[pl.ds(pl.multiple_of(base * xs, 8), share * xs), :]
            return lane_sum + tall_sum(value * mark)

        def send_part(p, j):
            return pltpu.make_async_remote_copy(
                src_ref=ready.at[p, j],
                dst_ref=parts.at[p, j],
                send_sem=part_sends.at[p, j],
                recv_sem=part_receives.at[p, j],
                device_id={"rot": lax.rem(rot + j, groups)},
                device_id_type=MESH,
            )

        lane_sum = lax.fori_loop(0, groups, last, jnp.zeros((8, LANES), F32))
        lane_mean = jnp.sum(lane_sum, axis=0, keepdims=True) / jnp.maximum(columns, 1.0)

        def add_off(j, carry):
            base = lax.rem(rot + j, groups) * (share * xs)
            mark = marks[pl.ds(pl.multiple_of(base, 8), share * xs), :]
            off = ready[p, j] - lane_mean
            return carry + tall_sum(off * off * mark)

        lane_square = lax.fori_loop(0, groups, add_off, jnp.zeros((8, LANES), F32), unroll=True)
        wide = jnp.broadcast_to(lane_mean, (8, LANES))
        part_mean = exact(wide, ones[...])[:1] / float(plan.zs)
        off = lane_mean - part_mean
        lane_square = jnp.sum(lane_square, axis=0, keepdims=True) + columns * off * off
        part_square = exact(jnp.broadcast_to(lane_square, (8, LANES)), ones[...])[:1]
        now = jnp.where(field == 2 * p, part_mean, row[...])
        row[...] = jnp.where(field == 2 * p + 1, part_square, now)
        return outer

    lax.fori_loop(0, 2, pair, 0)
    place = z * CORES + core
    stats[rot, x, place] = row[...]
    mine = stats.at[rot, x, place]
    finish(begin(mine, mine, sends, receives, first_stats, line_peers))
    mine = stats.at[rot, x]
    finish(begin(mine, mine, sends, receives, first_stats + line_size - 1, sheet_peers))
    incoming = [
        remote(ready.at[p, j], parts.at[p, j], part_sends.at[p], part_receives.at[p], j, {"rot": lax.rem(rot + j, groups)})
        for p in range(2)
        for j in range(1, groups)
    ]

    def spread_field(lines, index):
        return jnp.where(
            low_half, lines[:, index : index + 1], lines[:, ZF + index : ZF + index + 1]
        )

    terms = []
    for j in range(groups):
        group = lax.rem(rot + groups - j, groups)
        lines = stats[group].reshape(-1, LANES)
        count = lines[:, FIELD_COUNT : FIELD_COUNT + 1]
        total = jnp.sum(count, axis=0, keepdims=True)
        average = jnp.sum(count * lines, axis=0, keepdims=True) / total
        off = lines - average
        square = jnp.sum(count * off * off, axis=0, keepdims=True) * plan.zs
        square += pltpu.roll(jnp.sum(lines, axis=0, keepdims=True), LANES - 1, 1)
        inverse = 1.0 / jnp.sqrt(square / (total * plan.zs) + EPSILON)
        for p in range(2):
            source = ready if j == 0 else parts
            quat = [spread_field(lines[:1], FIELD_QUAT + 4 * p + c) for c in range(4)]
            terms.append(
                (source.at[p, j], spread_field(average, 2 * p), spread_field(inverse, 2 * p), quat)
            )

    finish(incoming)

    def column(y):
        at = pl.ds(pl.multiple_of(y * xs, 8), xs)
        scores = [(ref[at, :] - average) * inverse for ref, average, inverse, _ in terms]
        high = functools.reduce(jnp.maximum, scores)
        high = jnp.maximum(high, pltpu.roll(high, ZF, 1))
        weights = [jnp.exp(score - high) for score in scores]
        sums = [functools.reduce(jnp.add, weights)]
        for c in range(4):
            sums.append(functools.reduce(jnp.add, [w * t[3][c] for w, t in zip(weights, terms)]))
        return [high] + [value + pltpu.roll(value, ZF, 1) for value in sums]

    def answer(j, carry):
        both = [jnp.where(low_half, a, b) for a, b in zip(column(2 * j), column(2 * j + 1))]
        base = pl.multiple_of(rot * (share * xs) + 2 * j * xs, 8)
        inside = jnp.where(
            low_half, marks[pl.ds(base, xs), :], marks[pl.ds(pl.multiple_of(base + xs, 8), xs), :]
        )
        high, total = both[0], both[1]
        lanes = pl.ds(pl.multiple_of(j * LANES, LANES), LANES)
        best[:, lanes] = inside * high
        evidence[:, lanes] = inside * (high + jnp.log(total))
        ratio = inside / total
        for c in range(4):
            moments[c, :, lanes] = both[2 + c] * ratio
        return carry

    lax.fori_loop(0, share // 2 // 10, unrolled(answer, 10), 0)


def matched(plan, tiles, groups, own, block, valid, quats, rot_index):
    ring_z = tiles // (CORES * RING_X)
    order = (
        np.arange(TEMPL // ring_z)[:, None] + (TEMPL // ring_z) * np.arange(ring_z)[None]
    ).reshape(-1)
    z_table = plan.tmpl_z()
    tables = [
        row_stack(plan.slab_z()),
        stacked_table(plan.folded(plan.kx, plan.kxp, np.arange(plan.lx), plan.lx)),
        stacked_table(plan.folded(plan.ky, plan.kyp, np.arange(plan.ys), plan.ly)),
        row_stack(z_table),
        stacked_table(plan.folded(plan.kx, plan.kxp, order, plan.lx)),
        stacked_table(plan.folded(plan.ky, plan.kyp, np.arange(TEMPL) - HALF, plan.ly)),
        paired_table(plan.inverse_rows(np.arange(plan.ys), plan.ky, plan.ly, plan.kyp, 2 * plan.kyp)),
        row_tables(plan.inverse_rows(np.arange(plan.xs), plan.kx, plan.lx, plan.kxc, plan.kxi)),
        col_tables(plan.inverse_z()),
    ]
    spots, first = [], 0
    for table in tables:
        spots.append((first, table.shape[0], table.shape[1]))
        first += table.shape[0]
    tables = [
        np.concatenate([padded_cols(table, 2 * LANES) for table in tables], axis=0),
        z_table.sum(axis=0, keepdims=True).astype(np.float32),
        np.kron(np.eye(2), np.ones((ZF, ZF))).astype(np.float32),
    ]
    share = plan.ys // groups * plan.xs
    copies = 2 * HALO_PARTS + ring_z + 2 * RING_X - 2 + ring_z * CORES + RING_X * groups - 2
    vmem = pl.BlockSpec(memory_space=pltpu.VMEM)
    far = pl.BlockSpec(memory_space=pltpu.HBM)
    flat_out = jax.ShapeDtypeStruct((plan.xs, plan.ys // groups * plan.zs), F32)
    return pl.pallas_call(
        functools.partial(match_kernel, plan, tiles, groups, spots),
        out_shape=[flat_out, flat_out, jax.ShapeDtypeStruct((4,) + flat_out.shape, F32)],
        in_specs=[far, vmem, vmem, vmem, pl.BlockSpec(memory_space=pltpu.SMEM), far, vmem, vmem],
        out_specs=[vmem] * 3,
        scratch_shapes=[
            pltpu.VMEM((2, groups, share, LANES), F32),
            pltpu.VMEM((groups, RING_X, ring_z * CORES, 1, LANES), F32),
            pltpu.VMEM(own.shape, BF16),
            pltpu.VMEM(own.shape, BF16),
            pltpu.VMEM((CORES, RING_X, ring_z) + block.shape, BF16),
            pltpu.VMEM((plan.kxc, 2, 2, plan.kyp, 2 * LANES), F32),
            pltpu.VMEM((plan.ys * 2 * plan.kxp, LANES), F32),
            pltpu.VMEM((2, tiles * BLOCK, LANES), F32),
            pltpu.VMEM((2, TEMPL * 2 * plan.kxp, LANES), F32),
            pltpu.VMEM((2, plan.kxi * plan.ys, LANES), F32),
            pltpu.VMEM((plan.ys * plan.xs, LANES), F32),
            pltpu.VMEM((2, groups, share, LANES), F32),
            pltpu.VMEM((1, LANES), F32),
            pltpu.SemaphoreType.DMA((copies,)),
            pltpu.SemaphoreType.DMA((copies,)),
            pltpu.SemaphoreType.DMA((2, groups)),
            pltpu.SemaphoreType.DMA((2, groups)),
            pltpu.VMEM(own.shape, BF16),
            pltpu.VMEM(tables[0].shape, BF16),
            pltpu.SemaphoreType.DMA((2,)),
        ],
        compiler_params=pltpu.CompilerParams(
            collective_id=0, has_side_effects=True, vmem_limit_bytes=52 << 20
        ),
        name="match",
    )(own, block, valid, quats, rot_index, *tables)


def row_stack(table):
    return np.concatenate(halves(table), axis=0)


def local(tomogram, templates, valid, quats, rot_index):
    xs, voxels = tomogram.shape
    ys = valid.shape[1]
    zs = voxels // ys
    plan = Plan(xs, ys, zs)
    tiles, groups = lax.axis_size("tile"), lax.axis_size("rot")
    per = templates.shape[1] // TEMPL
    block = templates.reshape(2, 2, per, TEMPL).transpose(0, 2, 1, 3)
    block = jnp.pad(block, ((0, 0), (0, 0), (0, 0), (0, ZF - TEMPL))).reshape(2 * per, LANES)
    block = jnp.pad(block, ((0, BLOCK - 2 * per), (0, 0)))
    return tuple(matched(plan, tiles, groups, tomogram, block, valid, quats, rot_index))


def solution(mesh):
    placed = (P("tile", None), P("rot", "tile"), P("tile", None), P(), P("rot"))
    return jax.shard_map(
        local,
        mesh=mesh,
        in_specs=placed,
        out_specs=(P("tile", "rot"), P("tile", "rot"), P(None, "tile", "rot")),
        check_vma=False,
    )
```
